256 devices in a mesh: lat: 4 (over y), lon: 64 (over x, z, core).
Axes of the slice: x: 4, y: 4, z: 8, core: 2. Of those that a mesh axis runs over, the one named last changes fastest.
Arguments:
- grid_feat: bfloat16 [64, 2048, 1024], P('lat', 'lon'), may hold values from -40 to 40
- mesh_feat: bfloat16 [32, 1024, 1024], P('lat', 'lon'), may hold values from -40 to 40
- edges: int32 [12, 64, 2048], P(None, 'lat', 'lon'), may hold values from 0 to 32767, as said below
- edge_mask: int32 [12, 64, 2048], P(None, 'lat', 'lon'), may hold values from 0 to 1, as said below
- w_query: bfloat16 [1024, 1024], replicated, may hold values from -0.1875 to 0.1875
- w_key: bfloat16 [1024, 1024], replicated, may hold values from -0.1875 to 0.1875
- w_value: bfloat16 [1024, 1024], replicated, may hold values from -0.1875 to 0.1875
- w_out: bfloat16 [1024, 1024], replicated, may hold values from -0.1875 to 0.1875
- cotangent: bfloat16 [64, 2048, 1024], P('lat', 'lon'), may hold values from -6 to 6
Outputs:
- layer_out: bfloat16 [64, 2048, 1024], P('lat', 'lon')
- grid_grad: bfloat16 [64, 2048, 1024], P('lat', 'lon')
- mesh_grad: bfloat16 [32, 1024, 1024], P('lat', 'lon')
The draws below stay inside these ranges and needn't reach their ends.
Inputs may be any that keep to these rules, and one draw needn't show every extreme that they name: edges[e,i,j] = r * 1024 + c names a mesh node with 0 <= r < 32, |r - i // 2| <= 4, and c within 4 of j // 2 around the circle of 1024 columns; the 12 slots of a grid point name distinct nodes, masked slots included. `edge_mask`: each grid point has 3 to 12 live slots, and they come first.
All inputs are finite; a program needn't handle non-finite values.
Results may differ from the reference program's by a relative error of at most 0.01.
The reference program's roundings to bfloat16 on the way (of `queries`, `probs_half`, `attended`, `d_attended`, `d_scores` and `d_query`) count: a program that leaves them out, or rounds other values in their place, can miss the bound.
Values may be sent and summed in bfloat16 or wider, within the bound.
No kernel may reach another device: no remote copies, remote signals or barrier semaphores. Data moves between devices by JAX's collectives and lax.ppermute only.
A program may use at most 128 MiB of HBM per device.

```python
import math
import jax
import jax.numpy as jnp
from jax import lax

MODEL_WIDTH = 1024
HEAD_COUNT = 16
EDGE_SLOTS = 12
HALO_REACH = 4
MESH_LAT = 32
MESH_LON = 1024
GRID_LAT = 64
GRID_LON = 2048


def scaled_features(key, shape_rows, shape_cols):
    base = jnp.clip(jax.random.normal(jax.random.fold_in(key, 11), (shape_rows, shape_cols, MODEL_WIDTH), jnp.float32), -5.0, 5.0)
    return base.astype(jnp.bfloat16)


def draw_grid_feat(key, part):
    return scaled_features(jax.random.fold_in(key, 101), GRID_LAT, GRID_LON)


def draw_mesh_feat(key, part):
    return scaled_features(jax.random.fold_in(key, 202), MESH_LAT, MESH_LON)


def draw_edges(key, part):
    span = 2 * HALO_REACH + 1
    offset_count = span * span
    offset_id = jnp.arange(offset_count, dtype=jnp.int32)
    d_lat = offset_id // span - HALO_REACH
    d_lon = offset_id % span - HALO_REACH
    home_lat = jnp.arange(GRID_LAT, dtype=jnp.int32) // 2
    home_lon = jnp.arange(GRID_LON, dtype=jnp.int32) // 2
    node_lat = home_lat[:, None, None] + d_lat[None, None, :]
    inside = (node_lat >= 0) & (node_lat < MESH_LAT)
    noise = jax.random.randint(jax.random.fold_in(key, 31), (GRID_LAT, GRID_LON, offset_count), 0, 1 << 20)
    ranking = jnp.where(inside, noise * 128 + offset_id[None, None, :], -1)
    picked = lax.top_k(ranking, EDGE_SLOTS)[1]
    chosen_lat = home_lat[:, None, None] + jnp.take(d_lat, picked)
    chosen_lon = jnp.mod(home_lon[None, :, None] + jnp.take(d_lon, picked), MESH_LON)
    node_index = chosen_lat * MESH_LON + chosen_lon
    return jnp.transpose(node_index, (2, 0, 1)).astype(jnp.int32)


def draw_edge_mask(key, part):
    live_count = jax.random.randint(jax.random.fold_in(key, 41), (1, GRID_LAT, GRID_LON), 3, EDGE_SLOTS + 1)
    slot_id = jnp.arange(EDGE_SLOTS, dtype=jnp.int32)[:, None, None]
    return jnp.where(slot_id < live_count, 1, 0).astype(jnp.int32)


def block_levels(rng, dims, split, smallest, high):
    def one(dim, blocks):
        steps = jax.random.uniform(jax.random.fold_in(jax.random.fold_in(rng, 6), dim), (blocks,), jnp.float32, smallest / len(split), high / len(split))
        return jnp.repeat(jnp.exp(steps), dims[dim] // blocks).reshape((-1,) + (1,) * (len(dims) - dim - 1))

    gain = one(*split[0])
    for cut in split[1:]:
        gain = gain * one(*cut)
    return gain


def normal_values(stream_key, dims, scale, bound, shards=(), held_as=jnp.bfloat16):
    values = scale * jax.random.normal(stream_key, dims, jnp.float32)
    if shards:
        values = values * block_levels(stream_key, dims, shards, -0.22, 0.18)
    return jnp.clip(values, -bound, bound).astype(held_as)


def setup_inputs(seed: int = 0) -> dict:
    seeds = jax.random.split(jax.random.key(seed), 10)
    grid_feat = draw_grid_feat(jax.random.fold_in(seeds[9], 71), 0)
    mesh_feat = draw_mesh_feat(jax.random.fold_in(seeds[9], 71), 0)
    edges = draw_edges(jax.random.fold_in(seeds[9], 71), 0)
    edge_mask = draw_edge_mask(jax.random.fold_in(seeds[9], 71), 0)
    w_query = normal_values(seeds[4], (MODEL_WIDTH, MODEL_WIDTH), MODEL_WIDTH ** -0.5, 0.1875)
    w_key = normal_values(seeds[5], (MODEL_WIDTH, MODEL_WIDTH), MODEL_WIDTH ** -0.5, 0.1875)
    w_value = normal_values(seeds[6], (MODEL_WIDTH, MODEL_WIDTH), MODEL_WIDTH ** -0.5, 0.1875)
    w_out = normal_values(seeds[7], (MODEL_WIDTH, MODEL_WIDTH), MODEL_WIDTH ** -0.5, 0.1875)
    cotangent = normal_values(seeds[8], (GRID_LAT, GRID_LON, MODEL_WIDTH), 1.0, 6.0, ((0, 4), (1, 64)))
    return dict(grid_feat=grid_feat, mesh_feat=mesh_feat, edges=edges, edge_mask=edge_mask, w_query=w_query, w_key=w_key, w_value=w_value, w_out=w_out, cotangent=cotangent)


NEG_FILL = -1e+30

def reference(grid_feat, mesh_feat, edges, edge_mask, w_query, w_key, w_value, w_out, cotangent):
    width = grid_feat.shape[2]
    head_size = width // HEAD_COUNT
    score_scale = 1.0 / math.sqrt(head_size)
    node_count = MESH_LAT * MESH_LON
    mesh_flat = mesh_feat.reshape(node_count, width)
    key_all = lax.optimization_barrier(jnp.dot(mesh_flat, w_key, preferred_element_type=jnp.float32).astype(jnp.bfloat16))
    value_all = lax.optimization_barrier(jnp.dot(mesh_flat, w_value, preferred_element_type=jnp.float32).astype(jnp.bfloat16))
    edge_rows = jnp.transpose(edges, (1, 2, 0))
    live_rows = jnp.transpose(edge_mask, (1, 2, 0))

    def one_row(carry, inputs):
        key_grad, value_grad = carry
        feats, targets, live, cot_rows = inputs
        count = feats.shape[0]
        queries = lax.optimization_barrier(jnp.dot(feats, w_query, preferred_element_type=jnp.float32).astype(jnp.bfloat16))
        query_heads = queries.reshape(count, HEAD_COUNT, head_size).astype(jnp.float32)
        key_sel = key_all[targets].reshape(count, EDGE_SLOTS, HEAD_COUNT, head_size).astype(jnp.float32)
        value_sel = value_all[targets].reshape(count, EDGE_SLOTS, HEAD_COUNT, head_size).astype(jnp.float32)
        scores = jnp.einsum('nhd,nehd->nhe', query_heads, key_sel) * score_scale
        scores = jnp.where(live[:, None, :] > 0, scores, NEG_FILL)
        row_max = lax.optimization_barrier(jnp.max(scores, axis=2, keepdims=True))
        exp_scores = jnp.exp(scores - row_max)
        prob_full = exp_scores / lax.optimization_barrier(jnp.sum(exp_scores, axis=2, keepdims=True))
        probs_half = lax.optimization_barrier(prob_full.astype(jnp.bfloat16)).astype(jnp.float32)
        attended = jnp.einsum('nhe,nehd->nhd', probs_half, value_sel).astype(jnp.bfloat16).reshape(count, width)
        layer_out = (feats.astype(jnp.float32) + jnp.dot(attended, w_out, preferred_element_type=jnp.float32)).astype(jnp.bfloat16)
        d_attended = lax.optimization_barrier(jnp.dot(cot_rows, w_out.T, preferred_element_type=jnp.float32).astype(jnp.bfloat16))
        d_heads = d_attended.reshape(count, HEAD_COUNT, head_size).astype(jnp.float32)
        d_probs = jnp.einsum('nhd,nehd->nhe', d_heads, value_sel)
        centred = lax.optimization_barrier(jnp.sum(prob_full * d_probs, axis=2, keepdims=True))
        d_scores = lax.optimization_barrier((prob_full * (d_probs - centred) * score_scale).astype(jnp.bfloat16)).astype(jnp.float32)
        d_query = jnp.einsum('nhe,nehd->nhd', d_scores, key_sel).astype(jnp.bfloat16).reshape(count, width)
        grid_grad = (cot_rows.astype(jnp.float32) + jnp.dot(d_query, w_query.T, preferred_element_type=jnp.float32)).astype(jnp.bfloat16)
        key_terms = jnp.einsum('nhe,nhd->nehd', d_scores, query_heads).reshape(count * EDGE_SLOTS, width)
        value_terms = jnp.einsum('nhe,nhd->nehd', probs_half, d_heads).reshape(count * EDGE_SLOTS, width)
        flat_targets = targets.reshape(count * EDGE_SLOTS).astype(jnp.int32)
        key_grad = key_grad.at[flat_targets].add(key_terms)
        value_grad = value_grad.at[flat_targets].add(value_terms)
        return ((key_grad, value_grad), (layer_out, grid_grad))
    start = (jnp.zeros((node_count, width), jnp.float32), jnp.zeros((node_count, width), jnp.float32))
    (key_grad, value_grad), (layer_out, grid_grad) = lax.scan(one_row, start, (grid_feat, edge_rows, live_rows, cotangent))
    key_half = key_grad.astype(jnp.bfloat16)
    value_half = value_grad.astype(jnp.bfloat16)
    mesh_grad = jnp.dot(key_half, w_key.T, preferred_element_type=jnp.float32)
    mesh_grad = mesh_grad + jnp.dot(value_half, w_value.T, preferred_element_type=jnp.float32)
    mesh_grad = mesh_grad.astype(jnp.bfloat16).reshape(MESH_LAT, MESH_LON, width)
    return (layer_out, grid_grad, mesh_grad)
```

```python
import functools

import jax
import jax.numpy as jnp
from jax import lax
from jax.experimental import pallas as pl
from jax.experimental.pallas import tpu as pltpu
from jax.sharding import PartitionSpec as P

HEADS = 16
HEAD = 64
SLOTS = 12
REACH = 4
NEG_FILL = -1e30
SCALE = 0.125
GROUP = 4
WIDE = GROUP * HEAD

BF = jnp.bfloat16
F32 = jnp.float32
NT = (((1,), (1,)), ((), ()))
NN = (((1,), (0,)), ((), ()))
TN = (((0,), (0,)), ((), ()))


def mm(a, b, dims):
    return lax.dot_general(a, b, dims, preferred_element_type=F32)


TILES = 4
POINTS = 128
RUNS = 4
RUN = 48
NODES = RUNS * RUN
ALL_NODES = 384


def project_kernel(x_ref, c_ref, wq_ref, wo_ref, q_ref, da_ref):
    for t in range(TILES):
        tr, tc = t // 2, t % 2
        rows = pl.ds(t * POINTS, POINTS)
        x = x_ref[tr, :, tc].reshape(POINTS, x_ref.shape[-1])
        q = mm(x, wq_ref[...], NN).astype(BF)
        q_ref[rows, :] = q * SCALE
        c = c_ref[tr, :, tc].reshape(POINTS, c_ref.shape[-1])
        d = mm(c, wo_ref[...], NT).astype(BF)
        da_ref[rows, :] = d * SCALE


def project(x5, c5, w_query, w_out):
    width = x5.shape[-1]
    points = TILES * POINTS
    cols = 256
    whole5 = pl.BlockSpec(x5.shape, lambda j: (0, 0, 0, 0, 0))
    out = pl.BlockSpec((points, cols), lambda j: (0, j))
    return pl.pallas_call(
        project_kernel,
        grid=(width // cols,),
        in_specs=[
            whole5,
            whole5,
            pl.BlockSpec((width, cols), lambda j: (0, j)),
            pl.BlockSpec((cols, width), lambda j: (j, 0)),
        ],
        out_specs=[out, out],
        out_shape=[jax.ShapeDtypeStruct((points, width), BF)] * 2,
        cost_estimate=pl.CostEstimate(
            flops=4 * points * width * width, bytes_accessed=8 << 20, transcendentals=0
        ),
        name="project",
    )(x5, c5, w_query, w_out)


def attend_kernel(
    mesh_ref, wk_ref, wv_ref, q_ref, da_ref, slot_ref, att_ref, dq_ref, part_ref,
    k_scr, v_scr, dk_scr, dv_scr, bias_scr, pw_scr, sw_scr, pt_scr, st_scr,
):
    k_scr[...] = mm(mesh_ref[...], wk_ref[...], NN).astype(BF)
    v_scr[...] = mm(mesh_ref[...], wv_ref[...], NN).astype(BF)
    dk_scr[...] = jnp.zeros_like(dk_scr)
    dv_scr[...] = jnp.zeros_like(dv_scr)
    head_of_lane = lax.broadcasted_iota(jnp.int32, (1, WIDE), 1) // HEAD
    node = lax.broadcasted_iota(jnp.int32, (NODES, POINTS), 0)

    def tile(t, carry):
        tr, tc = t // 2, t % 2
        base = pl.multiple_of(tc * 128 + tr * 16, 16)
        runs = [pl.ds(pl.multiple_of(base + k * 64, 16), RUN) for k in range(RUNS)]
        rows = pl.ds(pl.multiple_of(t * POINTS, POINTS), POINTS)
        slots = slot_ref[t]
        hit = node == slots[0:1]
        for e in range(1, SLOTS):
            hit = hit | (node == slots[e : e + 1])
        bias_scr[...] = jnp.where(hit, 0.0, NEG_FILL)

        def take(ref, lanes):
            return jnp.concatenate([ref[r, lanes] for r in runs], axis=0)

        def spread(block):
            return jnp.concatenate(
                [jnp.where(head_of_lane == h, block, jnp.zeros_like(block)) for h in range(GROUP)],
                axis=0,
            )

        for g in range(HEADS // GROUP):
            lanes = pl.ds(g * WIDE, WIDE)
            keys = take(k_scr, lanes)
            values = take(v_scr, lanes)
            queries = spread(q_ref[rows, lanes])
            grads = spread(da_ref[rows, lanes])
            scores = mm(keys, queries, NT)
            d_probs = mm(values, grads, NT)
            for h in range(GROUP):
                at = slice(h * POINTS, (h + 1) * POINTS)
                s = scores[:, at] + bias_scr[...]
                e = jnp.exp(s - jnp.max(s, axis=0, keepdims=True))
                p = e * (1.0 / jnp.sum(e, axis=0, keepdims=True))
                half = p.astype(BF)
                dp = d_probs[:, at]
                centred = jnp.sum(p * dp, axis=0, keepdims=True)
                ds = (p * (dp - centred)).astype(BF)
                pw_scr[:, at] = half
                sw_scr[:, at] = ds
                tall = slice(h * NODES, (h + 1) * NODES)
                pt_scr[tall, :] = half
                st_scr[tall, :] = ds
            att_ref[rows, lanes] = mm(pt_scr[...], spread(values), TN).astype(BF)
            dq_ref[rows, lanes] = mm(st_scr[...], spread(keys), TN).astype(BF)
            dk = mm(sw_scr[...], queries, NN)
            dv = mm(pw_scr[...], grads, NN)
            for k in range(RUNS):
                part = slice(k * RUN, (k + 1) * RUN)
                dk_scr[runs[k], lanes] += dk[part]
                dv_scr[runs[k], lanes] += dv[part]
        return carry

    lax.fori_loop(0, TILES, tile, 0)
    part_ref[...] = (
        mm((dk_scr[...] * (1.0 / SCALE)).astype(BF), wk_ref[...], NT)
        + mm((dv_scr[...] * (1.0 / SCALE)).astype(BF), wv_ref[...], NT)
    ).astype(part_ref.dtype)


def attend(nodes, w_key, w_value, q, da, slots):
    width = q.shape[1]
    points = q.shape[0]
    return pl.pallas_call(
        attend_kernel,
        in_specs=[pl.BlockSpec(memory_space=pltpu.VMEM)] * 6,
        out_specs=[pl.BlockSpec(memory_space=pltpu.VMEM)] * 3,
        out_shape=[
            jax.ShapeDtypeStruct((points, width), BF),
            jax.ShapeDtypeStruct((points, width), BF),
            jax.ShapeDtypeStruct((ALL_NODES, width), F32),
        ],
        scratch_shapes=[
            pltpu.VMEM((ALL_NODES, width), BF),
            pltpu.VMEM((ALL_NODES, width), BF),
            pltpu.VMEM((ALL_NODES, width), F32),
            pltpu.VMEM((ALL_NODES, width), F32),
            pltpu.VMEM((NODES, POINTS), F32),
            pltpu.VMEM((NODES, GROUP * POINTS), BF),
            pltpu.VMEM((NODES, GROUP * POINTS), BF),
            pltpu.VMEM((GROUP * NODES, POINTS), BF),
            pltpu.VMEM((GROUP * NODES, POINTS), BF),
        ],
        cost_estimate=pl.CostEstimate(
            flops=12 * 10**9, bytes_accessed=10 << 20, transcendentals=2 * 10**6
        ),
        name="attend",
    )(nodes, w_key, w_value, q, da, slots)


def outputs_kernel(x_ref, c_ref, att_ref, dq_ref, wo_ref, wq_ref, out_ref, grad_ref):
    for t in range(TILES):
        tr, tc = t // 2, t % 2
        rows = pl.ds(t * POINTS, POINTS)
        shape = (8, 16, out_ref.shape[-1])
        a = mm(att_ref[rows, :], wo_ref[...], NN).reshape(shape)
        out_ref[tr, :, tc] = (x_ref[tr, :, tc].astype(F32) + a).astype(BF)
        b = mm(dq_ref[rows, :], wq_ref[...], NT).reshape(shape)
        grad_ref[tr, :, tc] = (c_ref[tr, :, tc].astype(F32) + b).astype(BF)


def outputs(x5, c5, att, dq, w_out, w_query):
    width = x5.shape[-1]
    points = TILES * POINTS
    cols = 256
    whole = pl.BlockSpec((points, width), lambda j: (0, 0))
    block5 = pl.BlockSpec(x5.shape[:-1] + (cols,), lambda j: (0, 0, 0, 0, j))
    return pl.pallas_call(
        outputs_kernel,
        grid=(width // cols,),
        in_specs=[
            block5,
            block5,
            whole,
            whole,
            pl.BlockSpec((width, cols), lambda j: (0, j)),
            pl.BlockSpec((cols, width), lambda j: (j, 0)),
        ],
        out_specs=[block5, block5],
        out_shape=[jax.ShapeDtypeStruct(x5.shape, BF)] * 2,
        cost_estimate=pl.CostEstimate(
            flops=4 * points * width * width, bytes_accessed=10 << 20, transcendentals=0
        ),
        name="outputs",
    )(x5, c5, att, dq, w_out, w_query)


def shift(piece, d_lat, d_lon):
    lats, lons = lax.axis_size("lat"), lax.axis_size("lon")
    pairs = [
        (a * lons + o, (a + d_lat) * lons + (o + d_lon) % lons)
        for a in range(lats)
        for o in range(lons)
        if 0 <= a + d_lat < lats
    ]
    return lax.ppermute(piece, ("lat", "lon"), pairs)


def local(grid_feat, mesh_feat, edges, edge_mask, w_query, w_key, w_value, w_out, cotangent):
    width = grid_feat.shape[-1]
    mesh_rows, mesh_cols = mesh_feat.shape[:2]
    lon_total = mesh_cols * lax.axis_size("lon")
    x5 = grid_feat.reshape(2, 8, 2, 16, width)
    c5 = cotangent.reshape(2, 8, 2, 16, width)

    own = mesh_feat.reshape(2, 4, 4, 4, width).transpose(2, 0, 1, 3, 4).reshape(4, 2, 16, width)
    from_low = shift(own[:, 1], 1, 0)
    from_high = shift(own[:, 0], -1, 0)
    from_left = shift(own[3], 0, 1)
    from_right = shift(own[0], 0, -1)
    low_left = shift(own[3, 1], 1, 1)
    low_right = shift(own[0, 1], 1, -1)
    high_left = shift(own[3, 0], -1, 1)
    high_right = shift(own[0, 0], -1, -1)

    q, da = project(x5, c5, w_query, w_out)

    lat_start = lax.axis_index("lat") * mesh_rows
    lon_start = lax.axis_index("lon") * mesh_cols
    row = edges // lon_total - lat_start + REACH
    col = jnp.mod(edges % lon_total - lon_start + REACH, lon_total)
    tile_row = lax.broadcasted_iota(jnp.int32, edges.shape, 1) // 8
    tile_col = lax.broadcasted_iota(jnp.int32, edges.shape, 2) // 16
    slot = (
        (col // 4 - 2 * tile_col) * RUN
        + (row // 4 - tile_row) * 16
        + (row % 4) * 4
        + col % 4
    )
    slot = jnp.where(edge_mask > 0, slot, -1)
    slot = slot.reshape(SLOTS, 2, 8, 2, 16).transpose(1, 3, 0, 2, 4).reshape(TILES, SLOTS, POINTS)

    middle = jnp.concatenate([from_low[:, None], own, from_high[:, None]], axis=1)
    left = jnp.concatenate([low_left[None], from_left, high_left[None]], axis=0)
    right = jnp.concatenate([low_right[None], from_right, high_right[None]], axis=0)
    nodes = jnp.concatenate([left[None], middle, right[None]], axis=0).reshape(ALL_NODES, width)

    att, dq, part = attend(nodes, w_key, w_value, q, da, slot)

    part = part.reshape(6, 4, 16, width)
    sent = part.astype(BF)
    to_low = shift(sent[1:5, 0], -1, 0)
    to_high = shift(sent[1:5, 3], 1, 0)
    to_left = shift(sent[0, 1:3], 0, -1)
    to_right = shift(sent[5, 1:3], 0, 1)
    to_low_left = shift(sent[0, 0], -1, -1)
    to_low_right = shift(sent[5, 0], -1, 1)
    to_high_left = shift(sent[0, 3], 1, -1)
    to_high_right = shift(sent[5, 3], 1, 1)

    layer_out, grid_grad = outputs(x5, c5, att, dq, w_out, w_query)

    total = part[1:5, 1:3]
    total = total.at[:, 1].add(to_low.astype(F32))
    total = total.at[:, 0].add(to_high.astype(F32))
    total = total.at[3].add(to_left.astype(F32))
    total = total.at[0].add(to_right.astype(F32))
    total = total.at[3, 1].add(to_low_left.astype(F32))
    total = total.at[0, 1].add(to_low_right.astype(F32))
    total = total.at[3, 0].add(to_high_left.astype(F32))
    total = total.at[0, 0].add(to_high_right.astype(F32))
    mesh_grad = (
        total.astype(BF)
        .reshape(4, 2, 4, 4, width)
        .transpose(1, 2, 0, 3, 4)
        .reshape(mesh_rows, mesh_cols, width)
    )
    return layer_out.reshape(grid_feat.shape), grid_grad.reshape(grid_feat.shape), mesh_grad


def solution(mesh):
    tiled = P("lat", "lon", None)
    placed = (tiled, tiled, P(None, "lat", "lon"), P(None, "lat", "lon")) + (P(),) * 4 + (tiled,)
    return jax.shard_map(
        local, mesh=mesh, in_specs=placed, out_specs=(tiled, tiled, tiled), check_vma=False
    )
```

```python
import jax
import jax.numpy as jnp
from jax import lax
from jax.experimental import pallas as pl
from jax.experimental.pallas import tpu as pltpu
from jax.sharding import PartitionSpec as P

HEADS = 16
HEAD = 64
SLOTS = 12
REACH = 4
NEG_FILL = -1e30
SCALE = 0.125
GROUP = 4
WIDE = GROUP * HEAD

TILES = 4
POINTS = 128
BLOCK = 64
NODES = 3 * BLOCK
MIDDLE = 4 * BLOCK

BF = jnp.bfloat16
F32 = jnp.float32
NT = (((1,), (1,)), ((), ()))
NN = (((1,), (0,)), ((), ()))
TN = (((0,), (0,)), ((), ()))
IN_VMEM = pl.BlockSpec(memory_space=pltpu.VMEM)


def mm(a, b, dims):
    return lax.dot_general(a, b, dims, preferred_element_type=F32)


def call(kernel, name, inputs, outs, flops, scratch=(), limit=16 << 20):
    moved = sum(a.size * a.dtype.itemsize for a in inputs)
    return pl.pallas_call(
        kernel,
        in_specs=[IN_VMEM] * len(inputs),
        out_specs=[IN_VMEM] * len(outs),
        out_shape=[jax.ShapeDtypeStruct(s, d) for s, d in outs],
        scratch_shapes=list(scratch),
        compiler_params=pltpu.CompilerParams(vmem_limit_bytes=limit),
        cost_estimate=pl.CostEstimate(flops=flops, bytes_accessed=moved, transcendentals=0),
        name=name,
    )(*inputs)


def to_tiles(rows):
    cut = rows.reshape(16, TILES, 8, rows.shape[-1])
    return [cut[:, t].reshape(POINTS, rows.shape[-1]) for t in range(TILES)]


def from_tiles(tiles):
    n = tiles[0].shape[-1]
    cut = [t.reshape(16, 1, 8, n) for t in tiles]
    return jnp.concatenate(cut, axis=1).reshape(TILES * POINTS, n)


def node_of(index):
    row, col = index // 16, index % 16
    return (col // 4) * BLOCK + row * 4 + col % 4


def project_kernel(x_ref, c_ref, wq_ref, wo_ref, edges_ref, mask_ref, q_ref, da_ref, bias_ref):
    lat_start = lax.axis_index("lat") * 8
    lon_start = lax.axis_index("lon") * 16
    edges = edges_ref[...]
    row = (edges >> 10) - lat_start + REACH
    col = (edges - lon_start + REACH) & 1023
    tile_of = lax.broadcasted_iota(jnp.int32, edges.shape, 2) >> 3
    slot = ((col >> 2) - tile_of) * BLOCK + row * 4 + (col & 3)
    slot = jnp.where(mask_ref[...] > 0, slot, -1).astype(F32).astype(BF)
    slot = slot.reshape(SLOTS * 16, 32)
    src = lax.broadcasted_iota(jnp.int32, (32, TILES * POINTS), 0)
    dst = lax.broadcasted_iota(jnp.int32, (32, TILES * POINTS), 1)
    pick = jnp.where(src == (dst >> 7) * 8 + (dst & 7), 1.0, 0.0).astype(BF)
    wide = mm(slot, pick, NN).reshape(SLOTS, 16, TILES * POINTS)
    r_of_lane = (lax.broadcasted_iota(jnp.int32, wide.shape, 2) >> 3) & 15
    own_row = lax.broadcasted_iota(jnp.int32, wide.shape, 1) == r_of_lane
    slots = jnp.sum(jnp.where(own_row, wide, 0.0), axis=1)
    node = lax.broadcasted_iota(jnp.int32, (NODES, POINTS), 0).astype(F32)
    for t in range(TILES):
        at = slice(t * POINTS, (t + 1) * POINTS)
        hit = node == slots[0:1, at]
        for e in range(1, SLOTS):
            hit = hit | (node == slots[e : e + 1, at])
        bias_ref[t] = jnp.where(hit, 0.0, NEG_FILL)
    width = q_ref.shape[-1]
    for j in range(0, width, 256):
        lanes = slice(j, j + 256)
        q = to_tiles(mm(x_ref[...], wq_ref[:, lanes], NN))
        d = to_tiles(mm(c_ref[...], wo_ref[lanes, :], NT))
        for t in range(TILES):
            q_ref[t, :, lanes] = q[t].astype(BF) * SCALE
            da_ref[t, :, lanes] = d[t].astype(BF) * SCALE


def assemble_kernel(low_ref, own_ref, high_ref, mid_ref):
    rows = jnp.concatenate([low_ref[...], own_ref[...], high_ref[...]], axis=0)
    dst = lax.broadcasted_iota(jnp.int32, (MIDDLE, MIDDLE), 0)
    src = lax.broadcasted_iota(jnp.int32, (MIDDLE, MIDDLE), 1)
    pick = jnp.where(dst == node_of(src), 1.0, 0.0).astype(BF)
    for j in range(0, mid_ref.shape[-1], 256):
        lanes = slice(j, j + 256)
        mid_ref[:, lanes] = mm(pick, rows[:, lanes], NN).astype(BF)


def pair_kernel(mid_ref, wk_ref, wv_ref, k_ref, v_ref):
    for j in range(0, mid_ref.shape[-1], 256):
        lanes = slice(j, j + 256)
        k_ref[:, lanes] = mm(mid_ref[...], wk_ref[:, lanes], NN).astype(BF)
        v_ref[:, lanes] = mm(mid_ref[...], wv_ref[:, lanes], NN).astype(BF)


def spread(block):
    head = lax.broadcasted_iota(jnp.int32, (1, WIDE), 1) // HEAD
    zero = jnp.zeros_like(block)
    return jnp.concatenate([jnp.where(head == h, block, zero) for h in range(GROUP)], axis=0)


def attend_group(keys, values, q4, d4, bias_ref, t, scratch):
    pw, sw, pt, st = scratch
    queries, grads = spread(q4), spread(d4)
    scores = mm(keys, queries, NT)
    d_probs = mm(values, grads, NT)
    for h in range(GROUP):
        at = slice(h * POINTS, (h + 1) * POINTS)
        s = scores[:, at] + bias_ref[t]
        e = jnp.exp(s - jnp.max(s, axis=0, keepdims=True))
        p = e * (1.0 / jnp.sum(e, axis=0, keepdims=True))
        half = p.astype(BF)
        dp = d_probs[:, at]
        centred = jnp.sum(p * dp, axis=0, keepdims=True)
        ds = (p * (dp - centred)).astype(BF)
        pw[:, at] = half
        sw[:, at] = ds
        tall = slice(h * NODES, (h + 1) * NODES)
        pt[tall, :] = half
        st[tall, :] = ds
    att = mm(pt[...], spread(values), TN).astype(BF)
    dq = mm(st[...], spread(keys), TN).astype(BF)
    dk = mm(sw[...], queries, NN)
    dv = mm(pw[...], grads, NN)
    return att, dq, dk, dv


ATTEND_SCRATCH = (
    pltpu.VMEM((NODES, GROUP * POINTS), BF),
    pltpu.VMEM((NODES, GROUP * POINTS), BF),
    pltpu.VMEM((GROUP * NODES, POINTS), BF),
    pltpu.VMEM((GROUP * NODES, POINTS), BF),
)


def edges_kernel(
    left_ref, right_ref, k_ref, v_ref, wk_ref, wv_ref, q_ref, da_ref, bias_ref,
    att_ref, dq_ref, dk_ref, dv_ref, low_ref, high_ref,
    kl, vl, dkl, dvl, *scratch,
):
    rim = jnp.concatenate([left_ref[...], right_ref[...]], axis=0)
    for j in range(0, rim.shape[-1], 256):
        lanes = slice(j, j + 256)
        kl[:, lanes] = mm(rim, wk_ref[:, lanes], NN).astype(BF)
        vl[:, lanes] = mm(rim, wv_ref[:, lanes], NN).astype(BF)

    def group(g, carry):
        lanes = pl.ds(pl.multiple_of(g * WIDE, WIDE), WIDE)
        left = (slice(0, BLOCK), slice(0, 2 * BLOCK))
        right = (slice(BLOCK, 2 * BLOCK), slice(2 * BLOCK, 4 * BLOCK))
        for i, t, (rim_at, mid_at) in ((0, 0, left), (1, 3, right)):
            order = (lambda r, m: [r, m]) if i == 0 else (lambda r, m: [m, r])
            keys = jnp.concatenate(order(kl[rim_at, lanes], k_ref[mid_at, lanes]), axis=0)
            values = jnp.concatenate(order(vl[rim_at, lanes], v_ref[mid_at, lanes]), axis=0)
            att, dq, dk, dv = attend_group(
                keys, values, q_ref[t, :, lanes], da_ref[t, :, lanes], bias_ref, t, scratch
            )
            att_ref[i, :, lanes] = att
            dq_ref[i, :, lanes] = dq
            r, m = (
                (slice(0, BLOCK), slice(BLOCK, NODES))
                if i == 0
                else (slice(2 * BLOCK, NODES), slice(0, 2 * BLOCK))
            )
            dkl[rim_at, lanes] = (dk[r] * (1.0 / SCALE)).astype(BF)
            dvl[rim_at, lanes] = (dv[r] * (1.0 / SCALE)).astype(BF)
            dk_ref[mid_at, lanes] = dk[m]
            dv_ref[mid_at, lanes] = dv[m]
        return carry

    lax.fori_loop(0, HEADS // GROUP, group, 0)
    for j in range(0, rim.shape[-1], 256):
        lanes = slice(j, j + 256)
        part = mm(dkl[...], wk_ref[lanes, :], NT) + mm(dvl[...], wv_ref[lanes, :], NT)
        low_ref[:, lanes] = part[:BLOCK].astype(BF)
        high_ref[:, lanes] = part[BLOCK:].astype(BF)


def middle_kernel(
    k_ref, v_ref, wk_ref, wv_ref, q_ref, da_ref, bias_ref, dk_ref, dv_ref,
    att_ref, dq_ref, part_ref,
    dks, dvs, *scratch,
):
    def group(g, carry):
        lanes = pl.ds(pl.multiple_of(g * WIDE, WIDE), WIDE)
        dks[:, lanes] = dk_ref[:, lanes]
        dvs[:, lanes] = dv_ref[:, lanes]
        for i, t in ((0, 1), (1, 2)):
            at = slice(i * BLOCK, i * BLOCK + NODES)
            att, dq, dk, dv = attend_group(
                k_ref[at, lanes], v_ref[at, lanes], q_ref[t, :, lanes], da_ref[t, :, lanes],
                bias_ref, t, scratch,
            )
            att_ref[i, :, lanes] = att
            dq_ref[i, :, lanes] = dq
            dks[at, lanes] += dk
            dvs[at, lanes] += dv
        return carry

    lax.fori_loop(0, HEADS // GROUP, group, 0)
    dst = lax.broadcasted_iota(jnp.int32, (MIDDLE, MIDDLE), 0)
    src = lax.broadcasted_iota(jnp.int32, (MIDDLE, MIDDLE), 1)
    pick = jnp.where(src == node_of(dst), 1.0, 0.0).astype(BF)
    dk = mm(pick, (dks[...] * (1.0 / SCALE)).astype(BF), NN).astype(BF)
    dv = mm(pick, (dvs[...] * (1.0 / SCALE)).astype(BF), NN).astype(BF)
    for j in range(0, part_ref.shape[-1], 256):
        lanes = slice(j, j + 256)
        part_ref[:, lanes] = mm(dk, wk_ref[lanes, :], NT) + mm(dv, wv_ref[lanes, :], NT)


def merge_kernel(part_ref, left_ref, right_ref, low_ref, own_ref, high_ref):
    dst = lax.broadcasted_iota(jnp.int32, (MIDDLE, 2 * BLOCK), 0)
    src = lax.broadcasted_iota(jnp.int32, (MIDDLE, 2 * BLOCK), 1)
    place = node_of(dst)
    place = jnp.where(place >= 3 * BLOCK, place - 2 * BLOCK, jnp.where(place < BLOCK, place, -1))
    pick = jnp.where(place == src, 1.0, 0.0).astype(BF)
    rims = jnp.concatenate([left_ref[...], right_ref[...]], axis=0)
    for j in range(0, part_ref.shape[-1], 256):
        lanes = slice(j, j + 256)
        total = part_ref[:, lanes] + mm(pick, rims[:, lanes], NN)
        low_ref[:, lanes] = total[:BLOCK].astype(BF)
        own_ref[:, lanes] = total[BLOCK : 3 * BLOCK]
        high_ref[:, lanes] = total[3 * BLOCK :].astype(BF)


def outputs_kernel(x_ref, c_ref, ae_ref, am_ref, de_ref, dm_ref, wo_ref, wq_ref, out_ref, grad_ref):
    width = out_ref.shape[-1]
    att = jnp.concatenate([ae_ref[0], am_ref[0], am_ref[1], ae_ref[1]], axis=0)
    dq = jnp.concatenate([de_ref[0], dm_ref[0], dm_ref[1], de_ref[1]], axis=0)

    def ordered(rows):
        return from_tiles([rows[t * POINTS : (t + 1) * POINTS] for t in range(TILES)])

    for j in range(0, width, 256):
        lanes = slice(j, j + 256)
        a = ordered(mm(att, wo_ref[:, lanes], NN))
        out_ref[:, lanes] = (x_ref[:, lanes].astype(F32) + a).astype(BF)
        b = ordered(mm(dq, wq_ref[lanes, :], NT))
        grad_ref[:, lanes] = (c_ref[:, lanes].astype(F32) + b).astype(BF)


def finish_kernel(own_ref, low_ref, high_ref, out_ref):
    out_ref[:BLOCK] = (own_ref[:BLOCK] + low_ref[...].astype(F32)).astype(BF)
    out_ref[BLOCK:] = (own_ref[BLOCK:] + high_ref[...].astype(F32)).astype(BF)


def swap(low, high, axis, ring):
    count = lax.axis_size(axis)
    odd = lax.axis_index(axis) % 2 == 1
    even_pairs = [(i, i + 1) for i in range(0, count, 2)]
    odd_pairs = [(i, i + 1) for i in range(1, count - 1, 2)]
    if ring:
        odd_pairs.append((count - 1, 0))

    def both(pairs):
        return pairs + [(b, a) for a, b in pairs]

    a = lax.ppermute(jnp.where(odd, low, high), axis, both(even_pairs))
    b = lax.ppermute(jnp.where(odd, high, low), axis, both(odd_pairs))
    return jnp.where(odd, a, b), jnp.where(odd, b, a)


def local(grid_feat, mesh_feat, edges, edge_mask, w_query, w_key, w_value, w_out, cotangent):
    width = grid_feat.shape[-1]
    points = TILES * POINTS
    x = grid_feat.reshape(points, width)
    c = cotangent.reshape(points, width)
    own = mesh_feat.reshape(2 * BLOCK, width)
    product = 2 * width * width

    low, high = swap(own[:BLOCK], own[BLOCK:], "lat", False)
    q, da, bias = call(
        project_kernel, "project", (x, c, w_query, w_out, edges, edge_mask),
        [((TILES, POINTS, width), BF)] * 2 + [((TILES, NODES, POINTS), F32)],
        2 * points * product,
    )
    (mid,) = call(assemble_kernel, "assemble", (low, own, high), [((MIDDLE, width), BF)], 10**8)
    left, right = swap(mid[:BLOCK], mid[3 * BLOCK :], "lon", True)
    k, v = call(
        pair_kernel, "pair", (mid, w_key, w_value), [((MIDDLE, width), BF)] * 2,
        2 * MIDDLE * product,
    )
    half = ((2, POINTS, width), BF)
    att_e, dq_e, dk, dv, to_left, to_right = call(
        edges_kernel, "attend_edges", (left, right, k, v, w_key, w_value, q, da, bias),
        [half, half] + [((MIDDLE, width), F32)] * 2 + [((BLOCK, width), BF)] * 2,
        6 * 10**9,
        (pltpu.VMEM((2 * BLOCK, width), BF),) * 4 + ATTEND_SCRATCH,
    )
    left, right = swap(to_left, to_right, "lon", True)
    att_m, dq_m, part = call(
        middle_kernel, "attend_middle", (k, v, w_key, w_value, q, da, bias, dk, dv),
        [half, half, ((MIDDLE, width), F32)],
        6 * 10**9,
        (pltpu.VMEM((MIDDLE, width), F32),) * 2 + ATTEND_SCRATCH,
    )
    to_low, kept, to_high = call(
        merge_kernel, "merge", (part, left, right),
        [((BLOCK, width), BF), ((2 * BLOCK, width), F32), ((BLOCK, width), BF)],
        10**8,
    )
    low, high = swap(to_low, to_high, "lat", False)
    layer_out, grid_grad = call(
        outputs_kernel, "outputs", (x, c, att_e, att_m, dq_e, dq_m, w_out, w_query),
        [((points, width), BF)] * 2,
        2 * points * product,
    )
    (mesh_grad,) = call(finish_kernel, "finish", (kept, low, high), [((2 * BLOCK, width), BF)], 10**6)
    return (
        layer_out.reshape(grid_feat.shape),
        grid_grad.reshape(grid_feat.shape),
        mesh_grad.reshape(mesh_feat.shape),
    )


def solution(mesh):
    tiled = P("lat", "lon", None)
    placed = (tiled, tiled, P(None, "lat", "lon"), P(None, "lat", "lon")) + (P(),) * 4 + (tiled,)
    return jax.shard_map(
        local, mesh=mesh, in_specs=placed, out_specs=(tiled, tiled, tiled), check_vma=False
    )
```

```python
import jax
import jax.numpy as jnp
from jax import lax
from jax.experimental import pallas as pl
from jax.experimental.pallas import tpu as pltpu
from jax.sharding import PartitionSpec as P


HEADS = 16
HEAD = 64
SLOTS = 12
REACH = 4
NEG_FILL = -1e30
SCALE = 0.125
GROUP = 4
WIDE = GROUP * HEAD

TILES = 4
POINTS = 128
BLOCK = 64
NODES = 3 * BLOCK
MIDDLE = 4 * BLOCK

BF = jnp.bfloat16
F32 = jnp.float32
NT = (((1,), (1,)), ((), ()))
NN = (((1,), (0,)), ((), ()))
TN = (((0,), (0,)), ((), ()))
IN_VMEM = pl.BlockSpec(memory_space=pltpu.VMEM)
IN_HBM = pl.BlockSpec(memory_space=pltpu.MemorySpace.HBM)
IN_PLACE = pl.BlockSpec(memory_space=pl.ANY)


def mm(a, b, dims):
    return lax.dot_general(a, b, dims, preferred_element_type=F32)


def call(kernel, inputs, outs, flops, scratch=(), hbm=(), loose=(), hbm_out=(), limit=16 << 20):
    moved = sum(a.size * a.dtype.itemsize for a in inputs)

    def placed(i):
        return IN_HBM if i in hbm else IN_PLACE if i in loose else IN_VMEM

    return pl.pallas_call(
        kernel,
        in_specs=[placed(i) for i in range(len(inputs))],
        out_specs=[IN_HBM if i in hbm_out else IN_VMEM for i in range(len(outs))],
        out_shape=[
            jax.ShapeDtypeStruct(s, d) if i in hbm_out else pltpu.VMEM(s, d)
            for i, (s, d) in enumerate(outs)
        ],
        scratch_shapes=list(scratch),
        compiler_params=pltpu.CompilerParams(vmem_limit_bytes=limit),
        cost_estimate=pl.CostEstimate(flops=flops, bytes_accessed=moved, transcendentals=0),
    )(
        *(
            pltpu.with_memory_space_constraint(a, pltpu.MemorySpace.HBM) if i in hbm else a
            for i, a in enumerate(inputs)
        )
    )


def to_tiles(rows):
    cut = rows.reshape(16, TILES, 8, rows.shape[-1])
    return [cut[:, t].reshape(POINTS, rows.shape[-1]) for t in range(TILES)]


def from_tiles(tiles):
    n = tiles[0].shape[-1]
    cut = [t.reshape(16, 1, 8, n) for t in tiles]
    return jnp.concatenate(cut, axis=1).reshape(TILES * POINTS, n)


def node_of(index):
    row, col = index // 16, index % 16
    return (col // 4) * BLOCK + row * 4 + col % 4


def lead_kernel(mesh_ref, a_ref, b_ref, sem):
    odd = lax.axis_index("lat") % 2
    first = pltpu.make_async_copy(mesh_ref.at[pl.ds((1 - odd) * BLOCK, BLOCK)], a_ref, sem.at[0])
    second = pltpu.make_async_copy(mesh_ref.at[pl.ds(odd * BLOCK, BLOCK)], b_ref, sem.at[1])
    first.start()
    second.start()
    first.wait()
    second.wait()


def project_q_kernel(
    x_hbm, wq_hbm, c_hbm, wo_hbm, piece_ref, q_ref, c_ref, wo_ref, pass_ref, x_scr, wq_scr, sem
):
    copies = [pltpu.make_async_copy(x_hbm, x_scr, sem.at[0])]
    width = q_ref.shape[-1]
    blocks = [slice(j, j + 256) for j in range(0, width, 256)]
    for i, lanes in enumerate(blocks):
        copies.append(
            pltpu.make_async_copy(wq_hbm.at[:, lanes], wq_scr.at[:, lanes], sem.at[1 + i])
        )
    copies.append(pltpu.make_async_copy(c_hbm, c_ref, sem.at[5]))
    copies.append(pltpu.make_async_copy(wo_hbm, wo_ref, sem.at[6]))
    for copy in copies:
        copy.start()
    pass_ref[...] = piece_ref[...]
    copies[0].wait()
    for i, lanes in enumerate(blocks):
        copies[1 + i].wait()
        q = to_tiles(mm(x_scr[...], wq_scr[:, lanes], NN))
        for t in range(TILES):
            q_ref[t, :, lanes] = q[t].astype(BF) * SCALE
    copies[5].wait()
    copies[6].wait()


def project_d_kernel(c_ref, wo_ref, edges_ref, mask_ref, da_ref, bias_ref):
    lat_start = lax.axis_index("lat") * 8
    lon_start = lax.axis_index("lon") * 16
    edges = edges_ref[...]
    row = (edges >> 10) - lat_start + REACH
    col = (edges - lon_start + REACH) & 1023
    tile_of = lax.broadcasted_iota(jnp.int32, edges.shape, 2) >> 3
    slot = ((col >> 2) - tile_of) * BLOCK + row * 4 + (col & 3)
    slot = jnp.where(mask_ref[...] > 0, slot, -1).astype(F32).astype(BF)
    slot = slot.reshape(SLOTS * 16, 32)
    src = lax.broadcasted_iota(jnp.int32, (32, TILES * POINTS), 0)
    dst = lax.broadcasted_iota(jnp.int32, (32, TILES * POINTS), 1)
    pick = jnp.where(src == (dst >> 7) * 8 + (dst & 7), 1.0, 0.0).astype(BF)
    wide = mm(slot, pick, NN).reshape(SLOTS, 16, TILES * POINTS)
    r_of_lane = (lax.broadcasted_iota(jnp.int32, wide.shape, 2) >> 3) & 15
    own_row = lax.broadcasted_iota(jnp.int32, wide.shape, 1) == r_of_lane
    slots = jnp.sum(jnp.where(own_row, wide, 0.0), axis=1)
    node = lax.broadcasted_iota(jnp.int32, (NODES, POINTS), 0).astype(F32)
    for t in range(TILES):
        at = slice(t * POINTS, (t + 1) * POINTS)
        hit = node == slots[0:1, at]
        for e in range(1, SLOTS):
            hit = hit | (node == slots[e : e + 1, at])
        bias_ref[t] = jnp.where(hit, 0.0, NEG_FILL)
    for j in range(0, da_ref.shape[-1], 256):
        lanes = slice(j, j + 256)
        d = to_tiles(mm(c_ref[...], wo_ref[lanes, :], NT))
        for t in range(TILES):
            da_ref[t, :, lanes] = d[t].astype(BF) * SCALE


def sort_pair(axis, a, b):
    odd = lax.axis_index(axis) % 2 == 1
    return jnp.where(odd, a, b), jnp.where(odd, b, a)


def assemble_kernel(got_a, got_b, own_a, own_b, after_ref, mid_ref, send_a, send_b):
    low, high = sort_pair("lat", got_a[...], got_b[...])
    own_low, own_high = sort_pair("lat", own_a[...], own_b[...])
    rows = jnp.concatenate([low, own_low, own_high, high], axis=0)
    dst = lax.broadcasted_iota(jnp.int32, (MIDDLE, MIDDLE), 0)
    src = lax.broadcasted_iota(jnp.int32, (MIDDLE, MIDDLE), 1)
    pick = jnp.where(dst == node_of(src), 1.0, 0.0).astype(BF)
    for j in range(0, mid_ref.shape[-1], 256):
        lanes = slice(j, j + 256)
        mid = mm(pick, rows[:, lanes], NN).astype(BF)
        mid_ref[:, lanes] = mid
        send_a[:, lanes], send_b[:, lanes] = sort_pair("lon", mid[:BLOCK], mid[3 * BLOCK :])


def pair_kernel(mid_ref, wk_ref, wv_ref, k_ref, v_ref):
    for j in range(0, mid_ref.shape[-1], 256):
        lanes = slice(j, j + 256)
        k_ref[:, lanes] = mm(mid_ref[...], wk_ref[:, lanes], NN).astype(BF)
        v_ref[:, lanes] = mm(mid_ref[...], wv_ref[:, lanes], NN).astype(BF)


def spread(block):
    head = lax.broadcasted_iota(jnp.int32, (1, WIDE), 1) // HEAD
    return jnp.concatenate(
        [block * jnp.where(head == h, 1.0, 0.0).astype(BF) for h in range(GROUP)], axis=0
    )


def score(keys, values, q4, d4, bufs):
    s_ref, d_ref, qs_ref, gs_ref = bufs[:4]
    queries, grads = spread(q4), spread(d4)
    qs_ref[...] = queries
    gs_ref[...] = grads
    s_ref[...] = mm(keys, queries, NT)
    d_ref[...] = mm(values, grads, NT)


def soften(bias, bufs):
    s_ref, d_ref, _, _, pw, sw, pt, st = bufs
    for h in range(GROUP):
        at = slice(h * POINTS, (h + 1) * POINTS)
        s = s_ref[:, at] + bias
        e = jnp.exp(s - jnp.max(s, axis=0, keepdims=True))
        p = e * (1.0 / jnp.sum(e, axis=0, keepdims=True))
        half = p.astype(BF)
        dp = d_ref[:, at]
        centred = jnp.sum(p * dp, axis=0, keepdims=True)
        ds = (p * (dp - centred)).astype(BF)
        pw[:, at] = half
        sw[:, at] = ds
        tall = slice(h * NODES, (h + 1) * NODES)
        pt[tall, :] = half
        st[tall, :] = ds


def gather_grads(keys, values, bufs):
    _, _, qs_ref, gs_ref, pw, sw, pt, st = bufs
    att = mm(pt[...], spread(values), TN).astype(BF)
    dq = mm(st[...], spread(keys), TN).astype(BF)
    dk = mm(sw[...], qs_ref[...], NN)
    dv = mm(pw[...], gs_ref[...], NN)
    return att, dq, dk, dv


ITEM_SCRATCH = (
    (pltpu.VMEM((NODES, GROUP * POINTS), F32),) * 2
    + (pltpu.VMEM((GROUP * POINTS, WIDE), BF),) * 2
    + (pltpu.VMEM((NODES, GROUP * POINTS), BF),) * 2
    + (pltpu.VMEM((GROUP * NODES, POINTS), BF),) * 2
)
PAIR_SCRATCH = ITEM_SCRATCH * 2


def attend_pair(tiles, load, store, q_ref, da_ref, bias_ref, scratch):
    n = len(ITEM_SCRATCH)
    bufs = (scratch[:n], scratch[n:])
    groups = HEADS // GROUP

    def lanes_of(g):
        return pl.ds(pl.multiple_of(g * WIDE, WIDE), WIDE)

    def do_score(g, i):
        lanes = lanes_of(g)
        keys, values = load(i, lanes)
        t = tiles[i]
        score(keys, values, q_ref[t, :, lanes], da_ref[t, :, lanes], bufs[i])

    def do_grads(g, i):
        lanes = lanes_of(g)
        keys, values = load(i, lanes)
        store(i, lanes, *gather_grads(keys, values, bufs[i]))

    for ref in bufs[1][2:]:
        ref[...] = jnp.zeros_like(ref)
    do_score(0, 0)

    def step(g, carry):
        do_grads(jnp.maximum(g - 1, 0), 1)
        soften(bias_ref[tiles[0]], bufs[0])
        do_score(g, 1)
        do_grads(g, 0)
        soften(bias_ref[tiles[1]], bufs[1])
        do_score(jnp.minimum(g + 1, groups - 1), 0)
        return carry

    lax.fori_loop(0, groups, step, 0)
    do_grads(groups - 1, 1)


def edges_kernel(
    got_a, got_b, k_ref, v_ref, wk_ref, wv_ref, q_ref, da_ref, bias_ref,
    att_ref, dq_ref, dk_ref, dv_ref, send_a, send_b,
    kl, vl, dkl, dvl, *scratch,
):
    rim = jnp.concatenate(sort_pair("lon", got_a[...], got_b[...]), axis=0)
    for j in range(0, rim.shape[-1], 256):
        lanes = slice(j, j + 256)
        kl[:, lanes] = mm(rim, wk_ref[:, lanes], NN).astype(BF)
        vl[:, lanes] = mm(rim, wv_ref[:, lanes], NN).astype(BF)

    def load(i, lanes):
        def one(rim, mid):
            if i == 0:
                return jnp.concatenate([rim[:BLOCK, lanes], mid[: 2 * BLOCK, lanes]], axis=0)
            return jnp.concatenate([mid[2 * BLOCK :, lanes], rim[BLOCK:, lanes]], axis=0)

        return one(kl, k_ref), one(vl, v_ref)

    def store(i, lanes, att, dq, dk, dv):
        att_ref[i, :, lanes] = att
        dq_ref[i, :, lanes] = dq
        rim_at = slice(i * BLOCK, (i + 1) * BLOCK)
        mid_at = slice(i * 2 * BLOCK, (i + 1) * 2 * BLOCK)
        r = slice(0, BLOCK) if i == 0 else slice(2 * BLOCK, NODES)
        m = slice(BLOCK, NODES) if i == 0 else slice(0, 2 * BLOCK)
        dkl[rim_at, lanes] = (dk[r] * (1.0 / SCALE)).astype(BF)
        dvl[rim_at, lanes] = (dv[r] * (1.0 / SCALE)).astype(BF)
        dk_ref[mid_at, lanes] = dk[m]
        dv_ref[mid_at, lanes] = dv[m]

    attend_pair((0, 3), load, store, q_ref, da_ref, bias_ref, scratch)
    for j in range(0, rim.shape[-1], 256):
        lanes = slice(j, j + 256)
        part = mm(dkl[...], wk_ref[lanes, :], NT) + mm(dvl[...], wv_ref[lanes, :], NT)
        send_a[:, lanes], send_b[:, lanes] = sort_pair(
            "lon", part[:BLOCK].astype(BF), part[BLOCK:].astype(BF)
        )


def middle_kernel(
    k_ref, v_ref, wk_ref, wv_ref, q_ref, da_ref, bias_ref, dk_ref, dv_ref,
    att_ref, dq_ref, part_ref, dko_ref, dvo_ref,
    dks, dvs, *scratch,
):
    dks[...] = dk_ref[...]
    dvs[...] = dv_ref[...]

    def load(i, lanes):
        at = slice(i * BLOCK, i * BLOCK + NODES)
        return k_ref[at, lanes], v_ref[at, lanes]

    def store(i, lanes, att, dq, dk, dv):
        at = slice(i * BLOCK, i * BLOCK + NODES)
        att_ref[i, :, lanes] = att
        dq_ref[i, :, lanes] = dq
        dks[at, lanes] += dk
        dvs[at, lanes] += dv

    attend_pair((1, 2), load, store, q_ref, da_ref, bias_ref, scratch)
    row = lax.broadcasted_iota(jnp.int32, (MIDDLE, MIDDLE), 0)
    src = lax.broadcasted_iota(jnp.int32, (MIDDLE, MIDDLE), 1)
    nodes = jnp.where(
        row < BLOCK, row, jnp.where(row < 2 * BLOCK, row + 2 * BLOCK, row - BLOCK)
    )
    pick = jnp.where(src == node_of(nodes), 1.0, 0.0).astype(BF)
    dk = mm(pick, (dks[...] * (1.0 / SCALE)).astype(BF), NN).astype(BF)
    dv = mm(pick, (dvs[...] * (1.0 / SCALE)).astype(BF), NN).astype(BF)
    dko_ref[...] = dk[2 * BLOCK :]
    dvo_ref[...] = dv[2 * BLOCK :]
    for j in range(0, part_ref.shape[-1], 256):
        lanes = slice(j, j + 256)
        part_ref[:, lanes] = mm(dk[: 2 * BLOCK], wk_ref[lanes, :], NT) + mm(
            dv[: 2 * BLOCK], wv_ref[lanes, :], NT
        )


def rim_pick(first, count):
    row = lax.broadcasted_iota(jnp.int32, (count, 2 * BLOCK), 0)
    src = lax.broadcasted_iota(jnp.int32, (count, 2 * BLOCK), 1)
    place = node_of(row + first)
    place = jnp.where(place >= 3 * BLOCK, place - 2 * BLOCK, jnp.where(place < BLOCK, place, -1))
    return jnp.where(place == src, 1.0, 0.0).astype(BF)


def merge_kernel(part_ref, got_a, got_b, send_a, send_b):
    pick = jnp.concatenate([rim_pick(0, BLOCK), rim_pick(3 * BLOCK, BLOCK)], axis=0)
    rims = jnp.concatenate(sort_pair("lon", got_a[...], got_b[...]), axis=0)
    for j in range(0, part_ref.shape[-1], 256):
        lanes = slice(j, j + 256)
        total = part_ref[:, lanes] + mm(pick, rims[:, lanes], NN)
        send_a[:, lanes], send_b[:, lanes] = sort_pair(
            "lat", total[:BLOCK].astype(BF), total[BLOCK:].astype(BF)
        )


def emit(res_ref, rows_e, rows_m, w_ref, dims, out_hbm, out_scr, sem):
    rows = jnp.concatenate([rows_e[0], rows_m[0], rows_m[1], rows_e[1]], axis=0)
    copies = []
    for i, j in enumerate(range(0, out_scr.shape[-1], 256)):
        lanes = slice(j, j + 256)
        w = w_ref[:, lanes] if dims is NN else w_ref[lanes, :]
        product = mm(rows, w, dims)
        tiles = [product[t * POINTS : (t + 1) * POINTS] for t in range(TILES)]
        out_scr[:, lanes] = (res_ref[:, lanes].astype(F32) + from_tiles(tiles)).astype(BF)
        copy = pltpu.make_async_copy(out_scr.at[:, lanes], out_hbm.at[:, lanes], sem.at[i])
        copy.start()
        copies.append(copy)
    return copies


def layer_out_kernel(
    x_ref, ae_ref, am_ref, wo_ref, piece_ref, out_hbm, pass_ref, out_scr, sem
):
    pass_ref[...] = piece_ref[...]
    for copy in emit(x_ref, ae_ref, am_ref, wo_ref, NN, out_hbm, out_scr, sem):
        copy.wait()


def grid_grad_kernel(
    c_ref, de_ref, dm_ref, wq_ref, dk_ref, dv_ref, wk_ref, wv_ref, got_a, got_b,
    grad_hbm, own_ref, out_scr, sem,
):
    copies = emit(c_ref, de_ref, dm_ref, wq_ref, NT, grad_hbm, out_scr, sem)
    pick = rim_pick(BLOCK, 2 * BLOCK)
    rims = jnp.concatenate(sort_pair("lon", got_a[...], got_b[...]), axis=0)
    for j in range(0, own_ref.shape[-1], 256):
        lanes = slice(j, j + 256)
        own_ref[:, lanes] = (
            mm(dk_ref[...], wk_ref[lanes, :], NT)
            + mm(dv_ref[...], wv_ref[lanes, :], NT)
            + mm(pick, rims[:, lanes], NN)
        )
    for copy in copies:
        copy.wait()


def finish_kernel(own_ref, got_a, got_b, out_hbm, out_scr, sem):
    copies = []
    for i, part in enumerate(sort_pair("lat", got_a[...], got_b[...])):
        rows = slice(i * BLOCK, (i + 1) * BLOCK)
        out_scr[rows] = (own_ref[rows] + part.astype(F32)).astype(BF)
        copies.append(pltpu.make_async_copy(out_scr.at[rows], out_hbm.at[rows], sem.at[i]))
        copies[-1].start()
    for copy in copies:
        copy.wait()


def pairs_of(axis, ring):
    count = lax.axis_size(axis)
    even = [(i, i + 1) for i in range(0, count, 2)]
    odd = [(i, i + 1) for i in range(1, count - 1, 2)]
    if ring:
        odd.append((count - 1, 0))
    return tuple(pairs + [(b, a) for a, b in pairs] for pairs in (even, odd))


def local(grid_feat, mesh_feat, edges, edge_mask, w_query, w_key, w_value, w_out, cotangent):
    width = grid_feat.shape[-1]
    points = TILES * POINTS
    x = grid_feat.reshape(points, width)
    c = cotangent.reshape(points, width)
    own = mesh_feat.reshape(2 * BLOCK, width)
    product = 2 * width * width
    lat_a, lat_b = pairs_of("lat", False)
    lon_a, lon_b = pairs_of("lon", True)
    piece = ((BLOCK, width), BF)
    tiled = ((TILES, POINTS, width), BF)
    square = ((width, width), BF)

    send_a, send_b = call(
        lead_kernel, (own,), [piece, piece], 10**5,
        (pltpu.SemaphoreType.DMA((2,)),), hbm=(0,),
    )
    got_a = lax.ppermute(send_a, "lat", lat_a)
    q, c_near, wo_near, late_b = call(
        project_q_kernel, (x, w_query, c, w_out, send_b),
        [tiled, ((points, width), BF), square, piece],
        points * product,
        (
            pltpu.VMEM((points, width), BF),
            pltpu.VMEM((width, width), BF),
            pltpu.SemaphoreType.DMA((7,)),
        ),
        hbm=(0, 1, 2, 3),
    )
    got_b = lax.ppermute(late_b, "lat", lat_b)
    da, bias = call(
        project_d_kernel, (c_near, wo_near, edges, edge_mask),
        [tiled, ((TILES, NODES, POINTS), F32)],
        points * product,
    )
    mid, edge_a, edge_b = call(
        assemble_kernel, (got_a, got_b, send_a, send_b, da),
        [((MIDDLE, width), BF), piece, piece], 10**8, loose=(4,),
    )
    edge_a = lax.ppermute(edge_a, "lon", lon_a)
    edge_b = lax.ppermute(edge_b, "lon", lon_b)
    k, v = call(
        pair_kernel, (mid, w_key, w_value), [((MIDDLE, width), BF)] * 2,
        2 * MIDDLE * product,
    )
    half = ((2, POINTS, width), BF)
    att_e, dq_e, dk, dv, edge_a, edge_b = call(
        edges_kernel, (edge_a, edge_b, k, v, w_key, w_value, q, da, bias),
        [half, half] + [((MIDDLE, width), F32)] * 2 + [piece] * 2,
        6 * 10**9,
        (pltpu.VMEM((2 * BLOCK, width), BF),) * 4 + PAIR_SCRATCH,
    )
    edge_a = lax.ppermute(edge_a, "lon", lon_a)
    edge_b = lax.ppermute(edge_b, "lon", lon_b)
    att_m, dq_m, part, dk_own, dv_own = call(
        middle_kernel, (k, v, w_key, w_value, q, da, bias, dk, dv),
        [half, half, ((2 * BLOCK, width), F32)] + [((2 * BLOCK, width), BF)] * 2,
        6 * 10**9,
        (pltpu.VMEM((MIDDLE, width), F32),) * 2 + PAIR_SCRATCH,
    )
    send_a, send_b = call(merge_kernel, (part, edge_a, edge_b), [piece, piece], 10**8)
    got_a = lax.ppermute(send_a, "lat", lat_a)
    out_scratch = (pltpu.VMEM((points, width), BF), pltpu.SemaphoreType.DMA((4,)))
    layer_out, late_b = call(
        layer_out_kernel, (x, att_e, att_m, w_out, send_b),
        [((points, width), BF), piece],
        points * product, out_scratch, hbm_out=(0,),
    )
    got_b = lax.ppermute(late_b, "lat", lat_b)
    grid_grad, kept = call(
        grid_grad_kernel,
        (c, dq_e, dq_m, w_query, dk_own, dv_own, w_key, w_value, edge_a, edge_b),
        [((points, width), BF), ((2 * BLOCK, width), F32)],
        points * product, out_scratch, hbm_out=(0,),
    )
    (mesh_grad,) = call(
        finish_kernel, (kept, got_a, got_b), [((2 * BLOCK, width), BF)], 10**6,
        (pltpu.VMEM((2 * BLOCK, width), BF), pltpu.SemaphoreType.DMA((2,))), hbm_out=(0,),
    )
    return (
        layer_out.reshape(grid_feat.shape),
        grid_grad.reshape(grid_feat.shape),
        mesh_grad.reshape(mesh_feat.shape),
    )


def solution(mesh):
    tiled = P("lat", "lon", None)
    placed = (tiled, tiled, P(None, "lat", "lon"), P(None, "lat", "lon")) + (P(),) * 4 + (tiled,)
    return jax.shard_map(
        local, mesh=mesh, in_specs=placed, out_specs=(tiled, tiled, tiled), check_vma=False
    )
```

```python
import jax
import jax.numpy as jnp
from jax import lax
from jax.experimental import pallas as pl
from jax.experimental.pallas import tpu as pltpu
from jax.sharding import PartitionSpec as P


HEADS = 16
HEAD = 64
SLOTS = 12
REACH = 4
NEG_FILL = -1e30
SCALE = 0.125
GROUP = 4
WIDE = GROUP * HEAD

TILES = 4
POINTS = 128
BLOCK = 64
NODES = 3 * BLOCK
MIDDLE = 4 * BLOCK

BF = jnp.bfloat16
F32 = jnp.float32
NT = (((1,), (1,)), ((), ()))
NN = (((1,), (0,)), ((), ()))
TN = (((0,), (0,)), ((), ()))
IN_VMEM = pl.BlockSpec(memory_space=pltpu.VMEM)
IN_HBM = pl.BlockSpec(memory_space=pltpu.MemorySpace.HBM)
IN_PLACE = pl.BlockSpec(memory_space=pl.ANY)


def mm(a, b, dims):
    return lax.dot_general(a, b, dims, preferred_element_type=F32)


def call(kernel, inputs, outs, flops, scratch=(), hbm=(), loose=(), hbm_out=(), limit=16 << 20):
    moved = sum(a.size * a.dtype.itemsize for a in inputs)

    def placed(i):
        return IN_HBM if i in hbm else IN_PLACE if i in loose else IN_VMEM

    return pl.pallas_call(
        kernel,
        in_specs=[placed(i) for i in range(len(inputs))],
        out_specs=[IN_HBM if i in hbm_out else IN_VMEM for i in range(len(outs))],
        out_shape=[
            jax.ShapeDtypeStruct(s, d) if i in hbm_out else pltpu.VMEM(s, d)
            for i, (s, d) in enumerate(outs)
        ],
        scratch_shapes=list(scratch),
        compiler_params=pltpu.CompilerParams(vmem_limit_bytes=limit),
        cost_estimate=pl.CostEstimate(flops=flops, bytes_accessed=moved, transcendentals=0),
    )(
        *(
            pltpu.with_memory_space_constraint(a, pltpu.MemorySpace.HBM) if i in hbm else a
            for i, a in enumerate(inputs)
        )
    )


def to_tiles(rows):
    cut = rows.reshape(16, TILES, 8, rows.shape[-1])
    return [cut[:, t].reshape(POINTS, rows.shape[-1]) for t in range(TILES)]


def from_tiles(tiles):
    n = tiles[0].shape[-1]
    cut = [t.reshape(16, 1, 8, n) for t in tiles]
    return jnp.concatenate(cut, axis=1).reshape(TILES * POINTS, n)


def node_of(index):
    row, col = index // 16, index % 16
    return (col // 4) * BLOCK + row * 4 + col % 4


def lead_kernel(mesh_ref, a_ref, b_ref, sem):
    odd = lax.axis_index("lat") % 2
    first = pltpu.make_async_copy(mesh_ref.at[pl.ds((1 - odd) * BLOCK, BLOCK)], a_ref, sem.at[0])
    second = pltpu.make_async_copy(mesh_ref.at[pl.ds(odd * BLOCK, BLOCK)], b_ref, sem.at[1])
    first.start()
    second.start()
    first.wait()
    second.wait()


def project_q_kernel(
    x_hbm, wq_hbm, c_hbm, wo_hbm, piece_ref, q_ref, c_ref, wo_ref, pass_ref, x_scr, wq_scr, sem
):
    copies = [pltpu.make_async_copy(x_hbm, x_scr, sem.at[0])]
    width = q_ref.shape[-1]
    blocks = [slice(j, j + 256) for j in range(0, width, 256)]
    for i, lanes in enumerate(blocks):
        copies.append(
            pltpu.make_async_copy(wq_hbm.at[:, lanes], wq_scr.at[:, lanes], sem.at[1 + i])
        )
    copies.append(pltpu.make_async_copy(c_hbm, c_ref, sem.at[5]))
    copies.append(pltpu.make_async_copy(wo_hbm, wo_ref, sem.at[6]))
    for copy in copies:
        copy.start()
    pass_ref[...] = piece_ref[...]
    copies[0].wait()
    for i, lanes in enumerate(blocks):
        copies[1 + i].wait()
        q = to_tiles(mm(x_scr[...], wq_scr[:, lanes], NN))
        for t in range(TILES):
            q_ref[t, :, lanes] = q[t].astype(BF) * SCALE
    copies[5].wait()
    copies[6].wait()


def project_d_kernel(c_ref, wo_ref, edges_ref, mask_ref, da_ref, bias_ref):
    lat_start = lax.axis_index("lat") * 8
    lon_start = lax.axis_index("lon") * 16
    edges = edges_ref[...]
    row = (edges >> 10) - lat_start + REACH
    col = (edges - lon_start + REACH) & 1023
    tile_of = lax.broadcasted_iota(jnp.int32, edges.shape, 2) >> 3
    slot = ((col >> 2) - tile_of) * BLOCK + row * 4 + (col & 3)
    slot = jnp.where(mask_ref[...] > 0, slot, -1).astype(F32).astype(BF)
    slot = slot.reshape(SLOTS * 16, 32)
    src = lax.broadcasted_iota(jnp.int32, (32, TILES * POINTS), 0)
    dst = lax.broadcasted_iota(jnp.int32, (32, TILES * POINTS), 1)
    pick = jnp.where(src == (dst >> 7) * 8 + (dst & 7), 1.0, 0.0).astype(BF)
    wide = mm(slot, pick, NN).reshape(SLOTS, 16, TILES * POINTS)
    r_of_lane = (lax.broadcasted_iota(jnp.int32, wide.shape, 2) >> 3) & 15
    own_row = lax.broadcasted_iota(jnp.int32, wide.shape, 1) == r_of_lane
    slots = jnp.sum(jnp.where(own_row, wide, 0.0), axis=1)
    node = lax.broadcasted_iota(jnp.int32, (NODES, POINTS), 0).astype(F32)
    for t in range(TILES):
        at = slice(t * POINTS, (t + 1) * POINTS)
        hit = node == slots[0:1, at]
        for e in range(1, SLOTS):
            hit = hit | (node == slots[e : e + 1, at])
        bias_ref[t] = jnp.where(hit, 0.0, NEG_FILL)
    for j in range(0, da_ref.shape[-1], 256):
        lanes = slice(j, j + 256)
        d = to_tiles(mm(c_ref[...], wo_ref[lanes, :], NT))
        for t in range(TILES):
            da_ref[t, :, lanes] = d[t].astype(BF) * SCALE


def sort_pair(axis, a, b):
    odd = lax.axis_index(axis) % 2 == 1
    return jnp.where(odd, a, b), jnp.where(odd, b, a)


def assemble_kernel(got_a, got_b, own_a, own_b, after_ref, mid_ref, send_a, send_b):
    low, high = sort_pair("lat", got_a[...], got_b[...])
    own_low, own_high = sort_pair("lat", own_a[...], own_b[...])
    rows = jnp.concatenate([low, own_low, own_high, high], axis=0)
    dst = lax.broadcasted_iota(jnp.int32, (MIDDLE, MIDDLE), 0)
    src = lax.broadcasted_iota(jnp.int32, (MIDDLE, MIDDLE), 1)
    pick = jnp.where(dst == node_of(src), 1.0, 0.0).astype(BF)
    for j in range(0, mid_ref.shape[-1], 256):
        lanes = slice(j, j + 256)
        mid = mm(pick, rows[:, lanes], NN).astype(BF)
        mid_ref[:, lanes] = mid
        send_a[:, lanes], send_b[:, lanes] = sort_pair("lon", mid[:BLOCK], mid[3 * BLOCK :])


def half_masks():
    head = lax.broadcasted_iota(jnp.int32, (1, 2 * HEAD), 1) // HEAD
    return [jnp.where(head == h, 1.0, 0.0).astype(BF) for h in range(2)]


def spread_pair(block):
    return jnp.concatenate([block * m for m in half_masks()], axis=0)


def spread_group(block):
    zero = jnp.zeros((block.shape[0], 2 * HEAD), BF)
    low, high = block[:, : 2 * HEAD], block[:, 2 * HEAD :]
    masks = half_masks()
    rows = [jnp.concatenate([low * m, zero], axis=1) for m in masks]
    rows += [jnp.concatenate([zero, high * m], axis=1) for m in masks]
    return jnp.concatenate(rows, axis=0)


def pair_lanes(i):
    return slice(i * 2 * HEAD, (i + 1) * 2 * HEAD), slice(i * 2 * POINTS, (i + 1) * 2 * POINTS)


def score(keys, values, q4, d4, bufs):
    s_ref, d_ref, qs_ref, gs_ref = bufs[:4]
    for i in range(GROUP // 2):
        lanes, at = pair_lanes(i)
        qs_ref[at, :] = spread_pair(q4[:, lanes])
        gs_ref[at, :] = spread_pair(d4[:, lanes])
        s_ref[:, at] = mm(keys[:, lanes], qs_ref[at, :], NT)
        d_ref[:, at] = mm(values[:, lanes], gs_ref[at, :], NT)


def soften(bias, bufs):
    s_ref, d_ref, _, _, pw, sw, pt, st = bufs
    for h in range(GROUP):
        at = slice(h * POINTS, (h + 1) * POINTS)
        s = s_ref[:, at] + bias
        e = jnp.exp(s - jnp.max(s, axis=0, keepdims=True))
        p = e * (1.0 / jnp.sum(e, axis=0, keepdims=True))
        half = p.astype(BF)
        dp = d_ref[:, at]
        centred = jnp.sum(p * dp, axis=0, keepdims=True)
        ds = (p * (dp - centred)).astype(BF)
        pw[:, at] = half
        sw[:, at] = ds
        tall = slice(h * NODES, (h + 1) * NODES)
        pt[tall, :] = half
        st[tall, :] = ds


def gather_grads(keys, values, bufs):
    _, _, qs_ref, gs_ref, pw, sw, pt, st = bufs
    att = mm(pt[...], spread_group(values), TN).astype(BF)
    dq = mm(st[...], spread_group(keys), TN).astype(BF)
    dk, dv = [], []
    for i in range(GROUP // 2):
        _, at = pair_lanes(i)
        dk.append(mm(sw[:, at], qs_ref[at, :], NN))
        dv.append(mm(pw[:, at], gs_ref[at, :], NN))
    return att, dq, jnp.concatenate(dk, axis=1), jnp.concatenate(dv, axis=1)


ITEM_SCRATCH = (
    (pltpu.VMEM((NODES, GROUP * POINTS), F32),) * 2
    + (pltpu.VMEM((GROUP * POINTS, 2 * HEAD), BF),) * 2
    + (pltpu.VMEM((NODES, GROUP * POINTS), BF),) * 2
    + (pltpu.VMEM((GROUP * NODES, POINTS), BF),) * 2
)
PAIR_SCRATCH = ITEM_SCRATCH * 2


def attend(tiles, load, store, q_ref, da_ref, bias_ref, scratch):
    n = len(ITEM_SCRATCH)
    bufs = (scratch[:n], scratch[n:])
    items = [
        (i, t, slice(j, j + WIDE))
        for j in range(0, HEADS * HEAD, WIDE)
        for i, t in enumerate(tiles)
    ]

    def do_score(k):
        i, t, lanes = items[k]
        keys, values = load(i, lanes)
        score(keys, values, q_ref[t, :, lanes], da_ref[t, :, lanes], bufs[k % 2])

    def do_grads(k):
        i, _, lanes = items[k]
        keys, values = load(i, lanes)
        store(i, lanes, *gather_grads(keys, values, bufs[k % 2]))

    do_score(0)
    for k, (_, t, _) in enumerate(items):
        if k > 0:
            do_grads(k - 1)
        soften(bias_ref[t], bufs[k % 2])
        if k + 1 < len(items):
            do_score(k + 1)
    do_grads(len(items) - 1)


def first_kernel(
    mid_ref, wk_ref, wv_ref, q_ref, da_ref, bias_ref,
    k_ref, v_ref, att_ref, dq_ref, dk_ref, dv_ref, *scratch,
):
    for j in range(0, mid_ref.shape[-1], WIDE):
        lanes = slice(j, j + WIDE)
        k_ref[:, lanes] = mm(mid_ref[...], wk_ref[:, lanes], NN).astype(BF)
        v_ref[:, lanes] = mm(mid_ref[...], wv_ref[:, lanes], NN).astype(BF)

    def load(i, lanes):
        return k_ref[:NODES, lanes], v_ref[:NODES, lanes]

    def store(i, lanes, att, dq, dk, dv):
        att_ref[:, lanes] = att
        dq_ref[:, lanes] = dq
        dk_ref[:, lanes] = dk
        dv_ref[:, lanes] = dv

    attend((1,), load, store, q_ref, da_ref, bias_ref, scratch)


def edges_kernel(
    got_a, got_b, k_ref, v_ref, wk_ref, wv_ref, q_ref, da_ref, bias_ref, dk1_ref, dv1_ref,
    att_ref, dq_ref, dk_ref, dv_ref, send_a, send_b,
    kl, vl, dkl, dvl, *scratch,
):
    rim = jnp.concatenate(sort_pair("lon", got_a[...], got_b[...]), axis=0)
    for j in range(0, rim.shape[-1], WIDE):
        lanes = slice(j, j + WIDE)
        kl[:, lanes] = mm(rim, wk_ref[:, lanes], NN).astype(BF)
        vl[:, lanes] = mm(rim, wv_ref[:, lanes], NN).astype(BF)

    def load(i, lanes):
        def one(rim, mid):
            if i == 0:
                return jnp.concatenate([rim[:BLOCK, lanes], mid[: 2 * BLOCK, lanes]], axis=0)
            return jnp.concatenate([mid[2 * BLOCK :, lanes], rim[BLOCK:, lanes]], axis=0)

        return one(kl, k_ref), one(vl, v_ref)

    def store(i, lanes, att, dq, dk, dv):
        att_ref[i, :, lanes] = att
        dq_ref[i, :, lanes] = dq
        rows = slice(i * BLOCK, (i + 1) * BLOCK)
        for grad, rim, so_far, out in ((dk, dkl, dk1_ref, dk_ref), (dv, dvl, dv1_ref, dv_ref)):
            if i == 0:
                rim[rows, lanes] = (grad[:BLOCK] * (1.0 / SCALE)).astype(BF)
                out[: 2 * BLOCK, lanes] = grad[BLOCK:] + so_far[: 2 * BLOCK, lanes]
            else:
                rim[rows, lanes] = (grad[2 * BLOCK :] * (1.0 / SCALE)).astype(BF)
                out[2 * BLOCK : 3 * BLOCK, lanes] = grad[:BLOCK] + so_far[2 * BLOCK :, lanes]
                out[3 * BLOCK :, lanes] = grad[BLOCK : 2 * BLOCK]

    attend((0, 3), load, store, q_ref, da_ref, bias_ref, scratch)
    for j in range(0, rim.shape[-1], WIDE):
        lanes = slice(j, j + WIDE)
        part = mm(dkl[...], wk_ref[lanes, :], NT) + mm(dvl[...], wv_ref[lanes, :], NT)
        send_a[:, lanes], send_b[:, lanes] = sort_pair(
            "lon", part[:BLOCK].astype(BF), part[BLOCK:].astype(BF)
        )


def last_kernel(
    k_ref, v_ref, wk_ref, wv_ref, q_ref, da_ref, bias_ref, dk_ref, dv_ref,
    att_ref, dq_ref, part_ref, dko_ref, dvo_ref,
    dks, dvs, *scratch,
):
    def load(i, lanes):
        return k_ref[BLOCK:, lanes], v_ref[BLOCK:, lanes]

    def store(i, lanes, att, dq, dk, dv):
        att_ref[:, lanes] = att
        dq_ref[:, lanes] = dq
        for grad, so_far, out in ((dk, dk_ref, dks), (dv, dv_ref, dvs)):
            out[:BLOCK, lanes] = (so_far[:BLOCK, lanes] * (1.0 / SCALE)).astype(BF)
            total = grad + so_far[BLOCK:, lanes]
            out[BLOCK:, lanes] = (total * (1.0 / SCALE)).astype(BF)

    attend((2,), load, store, q_ref, da_ref, bias_ref, scratch)
    row = lax.broadcasted_iota(jnp.int32, (MIDDLE, MIDDLE), 0)
    src = lax.broadcasted_iota(jnp.int32, (MIDDLE, MIDDLE), 1)
    nodes = jnp.where(
        row < BLOCK, row, jnp.where(row < 2 * BLOCK, row + 2 * BLOCK, row - BLOCK)
    )
    pick = jnp.where(src == node_of(nodes), 1.0, 0.0).astype(BF)
    dk = mm(pick, dks[...], NN).astype(BF)
    dv = mm(pick, dvs[...], NN).astype(BF)
    dko_ref[...] = dk[2 * BLOCK :]
    dvo_ref[...] = dv[2 * BLOCK :]
    for j in range(0, part_ref.shape[-1], WIDE):
        lanes = slice(j, j + WIDE)
        part_ref[:, lanes] = mm(dk[: 2 * BLOCK], wk_ref[lanes, :], NT) + mm(
            dv[: 2 * BLOCK], wv_ref[lanes, :], NT
        )


def rim_pick(first, count):
    row = lax.broadcasted_iota(jnp.int32, (count, 2 * BLOCK), 0)
    src = lax.broadcasted_iota(jnp.int32, (count, 2 * BLOCK), 1)
    place = node_of(row + first)
    place = jnp.where(place >= 3 * BLOCK, place - 2 * BLOCK, jnp.where(place < BLOCK, place, -1))
    return jnp.where(place == src, 1.0, 0.0).astype(BF)


def merge_kernel(part_ref, got_a, got_b, send_a, send_b):
    pick = jnp.concatenate([rim_pick(0, BLOCK), rim_pick(3 * BLOCK, BLOCK)], axis=0)
    rims = jnp.concatenate(sort_pair("lon", got_a[...], got_b[...]), axis=0)
    for j in range(0, part_ref.shape[-1], 256):
        lanes = slice(j, j + 256)
        total = part_ref[:, lanes] + mm(pick, rims[:, lanes], NN)
        send_a[:, lanes], send_b[:, lanes] = sort_pair(
            "lat", total[:BLOCK].astype(BF), total[BLOCK:].astype(BF)
        )


def emit(res_ref, edge, first, last, w_ref, dims, out_hbm, out_scr, sem):
    rows = jnp.concatenate([edge[0], first[...], last[...], edge[1]], axis=0)
    copies = []
    for i, j in enumerate(range(0, out_scr.shape[-1], 256)):
        lanes = slice(j, j + 256)
        w = w_ref[:, lanes] if dims is NN else w_ref[lanes, :]
        product = mm(rows, w, dims)
        tiles = [product[t * POINTS : (t + 1) * POINTS] for t in range(TILES)]
        out_scr[:, lanes] = (res_ref[:, lanes].astype(F32) + from_tiles(tiles)).astype(BF)
        copy = pltpu.make_async_copy(out_scr.at[:, lanes], out_hbm.at[:, lanes], sem.at[i])
        copy.start()
        copies.append(copy)
    return copies


def layer_out_kernel(
    x_ref, ae_ref, af_ref, al_ref, wo_ref, piece_ref, out_hbm, pass_ref, out_scr, sem
):
    pass_ref[...] = piece_ref[...]
    for copy in emit(x_ref, ae_ref, af_ref, al_ref, wo_ref, NN, out_hbm, out_scr, sem):
        copy.wait()


def grid_grad_kernel(
    c_ref, de_ref, df_ref, dl_ref, wq_ref, dk_ref, dv_ref, wk_ref, wv_ref, got_a, got_b,
    grad_hbm, own_ref, out_scr, sem,
):
    copies = emit(c_ref, de_ref, df_ref, dl_ref, wq_ref, NT, grad_hbm, out_scr, sem)
    pick = rim_pick(BLOCK, 2 * BLOCK)
    rims = jnp.concatenate(sort_pair("lon", got_a[...], got_b[...]), axis=0)
    for j in range(0, own_ref.shape[-1], 256):
        lanes = slice(j, j + 256)
        own_ref[:, lanes] = (
            mm(dk_ref[...], wk_ref[lanes, :], NT)
            + mm(dv_ref[...], wv_ref[lanes, :], NT)
            + mm(pick, rims[:, lanes], NN)
        )
    for copy in copies:
        copy.wait()


def finish_kernel(own_ref, got_a, got_b, out_hbm, out_scr, sem):
    copies = []
    for i, part in enumerate(sort_pair("lat", got_a[...], got_b[...])):
        rows = slice(i * BLOCK, (i + 1) * BLOCK)
        out_scr[rows] = (own_ref[rows] + part.astype(F32)).astype(BF)
        copies.append(pltpu.make_async_copy(out_scr.at[rows], out_hbm.at[rows], sem.at[i]))
        copies[-1].start()
    for copy in copies:
        copy.wait()


def pairs_of(axis, ring):
    count = lax.axis_size(axis)
    even = [(i, i + 1) for i in range(0, count, 2)]
    odd = [(i, i + 1) for i in range(1, count - 1, 2)]
    if ring:
        odd.append((count - 1, 0))
    return tuple(pairs + [(b, a) for a, b in pairs] for pairs in (even, odd))


def local(grid_feat, mesh_feat, edges, edge_mask, w_query, w_key, w_value, w_out, cotangent):
    width = grid_feat.shape[-1]
    points = TILES * POINTS
    x = grid_feat.reshape(points, width)
    c = cotangent.reshape(points, width)
    own = mesh_feat.reshape(2 * BLOCK, width)
    product = 2 * width * width
    lat_a, lat_b = pairs_of("lat", False)
    lon_a, lon_b = pairs_of("lon", True)
    piece = ((BLOCK, width), BF)
    tiled = ((TILES, POINTS, width), BF)
    square = ((width, width), BF)

    send_a, send_b = call(
        lead_kernel, (own,), [piece, piece], 10**5,
        (pltpu.SemaphoreType.DMA((2,)),), hbm=(0,),
    )
    got_a = lax.ppermute(send_a, "lat", lat_a)
    q, c_near, wo_near, late_b = call(
        project_q_kernel, (x, w_query, c, w_out, send_b),
        [tiled, ((points, width), BF), square, piece],
        points * product,
        (
            pltpu.VMEM((points, width), BF),
            pltpu.VMEM((width, width), BF),
            pltpu.SemaphoreType.DMA((7,)),
        ),
        hbm=(0, 1, 2, 3),
    )
    got_b = lax.ppermute(late_b, "lat", lat_b)
    da, bias = call(
        project_d_kernel, (c_near, wo_near, edges, edge_mask),
        [tiled, ((TILES, NODES, POINTS), F32)],
        points * product,
    )
    mid, edge_a, edge_b = call(
        assemble_kernel, (got_a, got_b, send_a, send_b, da),
        [((MIDDLE, width), BF), piece, piece], 10**8, loose=(4,),
    )
    edge_a = lax.ppermute(edge_a, "lon", lon_a)
    edge_b = lax.ppermute(edge_b, "lon", lon_b)
    rows, total = ((POINTS, width), BF), ((MIDDLE, width), F32)
    k, v, att_f, dq_f, dk, dv = call(
        first_kernel, (mid, w_key, w_value, q, da, bias),
        [((MIDDLE, width), BF)] * 2 + [rows] * 2 + [((NODES, width), F32)] * 2,
        4 * 10**9,
        PAIR_SCRATCH,
    )
    both = ((2, POINTS, width), BF)
    att_e, dq_e, dk, dv, edge_a, edge_b = call(
        edges_kernel,
        (edge_a, edge_b, k, v, w_key, w_value, q, da, bias, dk, dv),
        [both] * 2 + [total] * 2 + [piece] * 2,
        6 * 10**9,
        (pltpu.VMEM((2 * BLOCK, width), BF),) * 4 + PAIR_SCRATCH,
    )
    edge_a = lax.ppermute(edge_a, "lon", lon_a)
    edge_b = lax.ppermute(edge_b, "lon", lon_b)
    att_l, dq_l, part, dk_own, dv_own = call(
        last_kernel, (k, v, w_key, w_value, q, da, bias, dk, dv),
        [rows] * 2 + [((2 * BLOCK, width), F32)] + [((2 * BLOCK, width), BF)] * 2,
        4 * 10**9,
        (pltpu.VMEM((MIDDLE, width), BF),) * 2 + PAIR_SCRATCH,
    )
    send_a, send_b = call(merge_kernel, (part, edge_a, edge_b), [piece, piece], 10**8)
    got_a = lax.ppermute(send_a, "lat", lat_a)
    out_scratch = (pltpu.VMEM((points, width), BF), pltpu.SemaphoreType.DMA((4,)))
    layer_out, late_b = call(
        layer_out_kernel, (x, att_e, att_f, att_l, w_out, send_b),
        [((points, width), BF), piece],
        points * product, out_scratch, hbm_out=(0,),
    )
    got_b = lax.ppermute(late_b, "lat", lat_b)
    grid_grad, kept = call(
        grid_grad_kernel,
        (c, dq_e, dq_f, dq_l, w_query, dk_own, dv_own, w_key, w_value, edge_a, edge_b),
        [((points, width), BF), ((2 * BLOCK, width), F32)],
        points * product, out_scratch, hbm_out=(0,),
    )
    (mesh_grad,) = call(
        finish_kernel, (kept, got_a, got_b), [((2 * BLOCK, width), BF)], 10**6,
        (pltpu.VMEM((2 * BLOCK, width), BF), pltpu.SemaphoreType.DMA((2,))), hbm_out=(0,),
    )
    return (
        layer_out.reshape(grid_feat.shape),
        grid_grad.reshape(grid_feat.shape),
        mesh_grad.reshape(mesh_feat.shape),
    )


def solution(mesh):
    tiled = P("lat", "lon", None)
    placed = (tiled, tiled, P(None, "lat", "lon"), P(None, "lat", "lon")) + (P(),) * 4 + (tiled,)
    return jax.shard_map(
        local, mesh=mesh, in_specs=placed, out_specs=(tiled, tiled, tiled), check_vma=False
    )
```

```python
import jax
import jax.numpy as jnp
from jax import lax
from jax.experimental import pallas as pl
from jax.experimental.pallas import tpu as pltpu
from jax.sharding import PartitionSpec as P


HEADS = 16
HEAD = 64
SLOTS = 12
REACH = 4
NEG_FILL = -1e30
SCALE = 0.125
GROUP = 4
WIDE = GROUP * HEAD

TILES = 4
POINTS = 128
BLOCK = 64
NODES = 3 * BLOCK
MIDDLE = 4 * BLOCK
HALO = 16
HALF = 48

BF = jnp.bfloat16
F32 = jnp.float32
NT = (((1,), (1,)), ((), ()))
NN = (((1,), (0,)), ((), ()))
TN = (((0,), (0,)), ((), ()))
IN_VMEM = pl.BlockSpec(memory_space=pltpu.VMEM)
IN_HBM = pl.BlockSpec(memory_space=pltpu.MemorySpace.HBM)
IN_PLACE = pl.BlockSpec(memory_space=pl.ANY)


def mm(a, b, dims):
    return lax.dot_general(a, b, dims, preferred_element_type=F32)


def call(kernel, inputs, outs, flops, scratch=(), hbm=(), loose=(), hbm_out=(), limit=16 << 20):
    moved = sum(a.size * a.dtype.itemsize for a in inputs)

    def placed(i):
        return IN_HBM if i in hbm else IN_PLACE if i in loose else IN_VMEM

    return pl.pallas_call(
        kernel,
        in_specs=[placed(i) for i in range(len(inputs))],
        out_specs=[IN_HBM if i in hbm_out else IN_VMEM for i in range(len(outs))],
        out_shape=[
            jax.ShapeDtypeStruct(s, d) if i in hbm_out else pltpu.VMEM(s, d)
            for i, (s, d) in enumerate(outs)
        ],
        scratch_shapes=list(scratch),
        compiler_params=pltpu.CompilerParams(vmem_limit_bytes=limit),
        cost_estimate=pl.CostEstimate(flops=flops, bytes_accessed=moved, transcendentals=0),
    )(
        *(
            pltpu.with_memory_space_constraint(a, pltpu.MemorySpace.HBM) if i in hbm else a
            for i, a in enumerate(inputs)
        )
    )


def to_tiles(rows):
    cut = rows.reshape(16, TILES, 8, rows.shape[-1])
    parts = (cut[:, 0], cut[:8, 1:3], cut[8:, 1:3], cut[:, 3])
    return [part.reshape(POINTS, rows.shape[-1]) for part in parts]


def from_tiles(tiles):
    n = tiles[0].shape[-1]
    upper, lower = (t.reshape(8, 2, 8, n) for t in tiles[1:3])
    left, right = (t.reshape(16, 1, 8, n) for t in (tiles[0], tiles[3]))
    middle = jnp.concatenate([upper, lower], axis=0)
    return jnp.concatenate([left, middle, right], axis=1).reshape(TILES * POINTS, n)


def select(count, dst_of_src):
    dst = lax.broadcasted_iota(jnp.int32, (count, count), 0)
    src = lax.broadcasted_iota(jnp.int32, (count, count), 1)
    return jnp.where(dst == dst_of_src(src), 1.0, 0.0).astype(BF)


def to_blocks(rows):
    return lambda i: ((i % 16) // 4) * (4 * rows) + (i // 16) * 4 + i % 4


def is_odd(axis):
    return lax.axis_index(axis) % 2 == 1


def lead_kernel(mesh_ref, a_ref, b_ref, sem):
    odd = lax.axis_index("lat") % 2
    first = pltpu.make_async_copy(mesh_ref.at[pl.ds((1 - odd) * BLOCK, BLOCK)], a_ref, sem.at[0])
    second = pltpu.make_async_copy(mesh_ref.at[pl.ds(odd * BLOCK, BLOCK)], b_ref, sem.at[1])
    first.start()
    second.start()
    first.wait()
    second.wait()


def project_q_kernel(
    x_hbm, wq_hbm, c_hbm, wo_hbm, q_ref, c_ref, wo_ref, x_scr, wq_scr, sem
):
    copies = [pltpu.make_async_copy(x_hbm, x_scr, sem.at[0])]
    width = q_ref.shape[-1]
    blocks = [slice(j, j + 256) for j in range(0, width, 256)]
    for i, lanes in enumerate(blocks):
        copies.append(
            pltpu.make_async_copy(wq_hbm.at[:, lanes], wq_scr.at[:, lanes], sem.at[1 + i])
        )
    copies.append(pltpu.make_async_copy(c_hbm, c_ref, sem.at[5]))
    copies.append(pltpu.make_async_copy(wo_hbm, wo_ref, sem.at[6]))
    for copy in copies:
        copy.start()
    copies[0].wait()
    for i, lanes in enumerate(blocks):
        copies[1 + i].wait()
        q = to_tiles(mm(x_scr[...], wq_scr[:, lanes], NN))
        for t in range(TILES):
            q_ref[t, :, lanes] = q[t].astype(BF) * SCALE
    copies[5].wait()
    copies[6].wait()


def project_d_kernel(c_ref, wo_ref, edges_ref, mask_ref, piece_ref, da_ref, bias_ref, pass_ref):
    pass_ref[...] = piece_ref[...]
    lat_start = lax.axis_index("lat") * 8
    lon_start = lax.axis_index("lon") * 16
    edges = edges_ref[...]
    row = (edges >> 10) - lat_start + REACH
    col = (edges - lon_start + REACH) & 1023
    point_row = lax.broadcasted_iota(jnp.int32, edges.shape, 1)
    point_col = lax.broadcasted_iota(jnp.int32, edges.shape, 2)
    block, inner = col >> 2, row * 4 + (col & 3)
    slot = jnp.where(
        point_col < 8,
        block * BLOCK + inner,
        jnp.where(
            point_col >= 24,
            jnp.where(block == 5, 0, block - 2) * BLOCK + inner,
            (block - 1) * HALF + inner - jnp.where(point_row < 8, 0, HALO),
        ),
    )
    slot = jnp.where(mask_ref[...] > 0, slot, -1).astype(F32).astype(BF)
    slot = slot.reshape(SLOTS * 16, 32)

    def point(lane):
        tile, i = lane >> 7, lane & 127
        outer = (tile == 0) | (tile == 3)
        row = jnp.where(outer, i >> 3, (i >> 4) + jnp.where(tile == 2, 8, 0))
        col = jnp.where(outer, (i & 7) + tile * 8, (i & 15) + 8)
        return row, col

    src = lax.broadcasted_iota(jnp.int32, (32, TILES * POINTS), 0)
    dst = lax.broadcasted_iota(jnp.int32, (32, TILES * POINTS), 1)
    pick = jnp.where(src == point(dst)[1], 1.0, 0.0).astype(BF)
    wide = mm(slot, pick, NN).reshape(SLOTS, 16, TILES * POINTS)
    lane = lax.broadcasted_iota(jnp.int32, (16, TILES * POINTS), 1)
    own_row = lax.broadcasted_iota(jnp.int32, lane.shape, 0) == point(lane)[0]
    slots = jnp.sum(jnp.where(own_row[None], wide, 0.0), axis=1)
    node = lax.broadcasted_iota(jnp.int32, (NODES, POINTS), 0).astype(F32)
    for t in range(TILES):
        at = slice(t * POINTS, (t + 1) * POINTS)
        hit = node == slots[0:1, at]
        for e in range(1, SLOTS):
            hit = hit | (node == slots[e : e + 1, at])
        bias_ref[t] = jnp.where(hit, 0.0, NEG_FILL)
    for j in range(0, da_ref.shape[-1], 256):
        lanes = slice(j, j + 256)
        d = to_tiles(mm(c_ref[...], wo_ref[lanes, :], NT))
        for t in range(TILES):
            da_ref[t, :, lanes] = d[t].astype(BF) * SCALE


def sort_pair(axis, a, b):
    odd = lax.axis_index(axis) % 2 == 1
    return jnp.where(odd, a, b), jnp.where(odd, b, a)


def assemble_kernel(half_ref, got_b, rest_ref, send_a, send_b):
    pick = select(BLOCK, to_blocks(4))
    first = is_odd("lat")
    for j in range(0, rest_ref.shape[-1], WIDE):
        lanes = slice(j, j + WIDE)
        rest = mm(pick, got_b[:, lanes], NN).astype(BF)
        rest_ref[:, lanes] = rest

        def column(i):
            most = half_ref[i * HALF : (i + 1) * HALF, lanes]
            few = rest[i * HALO : (i + 1) * HALO]
            return jnp.where(
                first, jnp.concatenate([most, few], axis=0), jnp.concatenate([few, most], axis=0)
            )

        send_a[:, lanes], send_b[:, lanes] = sort_pair("lon", column(0), column(3))


def half_masks():
    head = lax.broadcasted_iota(jnp.int32, (1, 2 * HEAD), 1) // HEAD
    return [jnp.where(head == h, 1.0, 0.0).astype(BF) for h in range(2)]


def spread_pair(block):
    return jnp.concatenate([block * m for m in half_masks()], axis=0)


def spread_group(block):
    zero = jnp.zeros((block.shape[0], 2 * HEAD), BF)
    low, high = block[:, : 2 * HEAD], block[:, 2 * HEAD :]
    masks = half_masks()
    rows = [jnp.concatenate([low * m, zero], axis=1) for m in masks]
    rows += [jnp.concatenate([zero, high * m], axis=1) for m in masks]
    return jnp.concatenate(rows, axis=0)


def pair_lanes(i):
    return slice(i * 2 * HEAD, (i + 1) * 2 * HEAD), slice(i * 2 * POINTS, (i + 1) * 2 * POINTS)


def score(keys, values, q4, d4, bufs):
    s_ref, d_ref, qs_ref, gs_ref = bufs[:4]
    for i in range(GROUP // 2):
        lanes, at = pair_lanes(i)
        qs_ref[at, :] = spread_pair(q4[:, lanes])
        gs_ref[at, :] = spread_pair(d4[:, lanes])
        s_ref[:, at] = mm(keys[:, lanes], qs_ref[at, :], NT)
        d_ref[:, at] = mm(values[:, lanes], gs_ref[at, :], NT)


def soften(bias, bufs):
    s_ref, d_ref, _, _, pw, sw, pt, st = bufs
    for h in range(GROUP):
        at = slice(h * POINTS, (h + 1) * POINTS)
        tall = slice(h * NODES, (h + 1) * NODES)
        top = jnp.max(s_ref[:, at] + bias, axis=0, keepdims=True)
        e = jnp.exp(s_ref[:, at] + bias - top)
        s_ref[:, at] = e
        inverse = 1.0 / jnp.sum(e, axis=0, keepdims=True)
        centred = jnp.sum(e * d_ref[:, at], axis=0, keepdims=True) * inverse
        p = s_ref[:, at] * inverse
        half = p.astype(BF)
        ds = (p * (d_ref[:, at] - centred)).astype(BF)
        pw[:, at] = half
        sw[:, at] = ds
        pt[tall, :] = half
        st[tall, :] = ds


def gather_grads(keys, values, bufs):
    _, _, qs_ref, gs_ref, pw, sw, pt, st = bufs
    att = mm(pt[...], spread_group(values), TN).astype(BF)
    dq = mm(st[...], spread_group(keys), TN).astype(BF)
    dk, dv = [], []
    for i in range(GROUP // 2):
        _, at = pair_lanes(i)
        dk.append(mm(sw[:, at], qs_ref[at, :], NN))
        dv.append(mm(pw[:, at], gs_ref[at, :], NN))
    return att, dq, jnp.concatenate(dk, axis=1), jnp.concatenate(dv, axis=1)


ITEM_SCRATCH = (
    (pltpu.VMEM((NODES, GROUP * POINTS), F32),) * 2
    + (pltpu.VMEM((GROUP * POINTS, 2 * HEAD), BF),) * 2
    + (pltpu.VMEM((NODES, GROUP * POINTS), BF),) * 2
    + (pltpu.VMEM((GROUP * NODES, POINTS), BF),) * 2
)
PAIR_SCRATCH = ITEM_SCRATCH * 2


def attend(tile, load, store, q_ref, da_ref, bias_ref, scratch):
    n = len(ITEM_SCRATCH)
    bufs = (scratch[:n], scratch[n:])
    items = [slice(j, j + WIDE) for j in range(0, HEADS * HEAD, WIDE)]

    def do_score(k):
        lanes = items[k]
        score(*load(lanes), q_ref[tile, :, lanes], da_ref[tile, :, lanes], bufs[k % 2])

    def do_grads(k):
        store(items[k], *gather_grads(*load(items[k]), bufs[k % 2]))

    do_score(0)
    for k in range(len(items)):
        if k > 0:
            do_grads(k - 1)
        soften(bias_ref[tile], bufs[k % 2])
        if k + 1 < len(items):
            do_score(k + 1)
    do_grads(len(items) - 1)


def store_all(*refs):
    def store(lanes, *values):
        for ref, value in zip(refs, values):
            ref[:, lanes] = value

    return store


def first_kernel(
    got_a, own_a, own_b, wk_ref, wv_ref, q_ref, da_ref, bias_ref,
    half_ref, k_ref, v_ref, att_ref, dq_ref, dk_ref, dv_ref, *scratch,
):
    upper = is_odd("lat")
    top = jnp.where(upper, got_a[...], own_b[...])
    bottom = jnp.where(upper, own_b[...], got_a[...])
    rows = jnp.concatenate([top, own_a[...], bottom], axis=0)
    pick = select(NODES, to_blocks(12))
    for j in range(0, half_ref.shape[-1], WIDE):
        lanes = slice(j, j + WIDE)
        half_ref[:, lanes] = mm(pick, rows[:, lanes], NN).astype(BF)
    for j in range(0, half_ref.shape[-1], WIDE):
        lanes = slice(j, j + WIDE)
        k_ref[:, lanes] = mm(half_ref[...], wk_ref[:, lanes], NN).astype(BF)
        v_ref[:, lanes] = mm(half_ref[...], wv_ref[:, lanes], NN).astype(BF)

    def load(lanes):
        return k_ref[:, lanes], v_ref[:, lanes]

    tile = jnp.where(upper, 1, 2)
    store = store_all(att_ref, dq_ref, dk_ref, dv_ref)
    attend(tile, load, store, q_ref, da_ref, bias_ref, scratch)


def edge_tile(left, k_ref, v_ref, kr, vr, outs, q_ref, da_ref, bias_ref, scratch):
    att_ref, dq_ref, dk_ref, dv_ref, dkr, dvr = outs
    start = pl.multiple_of(jnp.where(left, 0, 2 * BLOCK), 2 * BLOCK)

    def load(lanes):
        def one(rim, mid):
            return jnp.concatenate([rim[:, lanes], mid[pl.ds(start, 2 * BLOCK), lanes]], axis=0)

        return one(kr, k_ref), one(vr, v_ref)

    def store(lanes, att, dq, dk, dv):
        att_ref[:, lanes] = att
        dq_ref[:, lanes] = dq
        for grad, rim, out in ((dk, dkr, dk_ref), (dv, dvr, dv_ref)):
            rim[:, lanes] = (grad[:BLOCK] * (1.0 / SCALE)).astype(BF)
            out[:, lanes] = grad[BLOCK:]

    attend(jnp.where(left, 0, 3), load, store, q_ref, da_ref, bias_ref, scratch)


def near_kernel(
    got_a, rest_ref, kh_ref, vh_ref, wk_ref, wv_ref, q_ref, da_ref, bias_ref,
    k_ref, v_ref, att_ref, dq_ref, dk_ref, dv_ref, dkr, dvr,
    kr, vr, *scratch,
):
    rows = jnp.concatenate([got_a[...], rest_ref[...]], axis=0)
    first = is_odd("lat")
    for rim, mid, half, w in ((kr, k_ref, kh_ref, wk_ref), (vr, v_ref, vh_ref, wv_ref)):
        for j in range(0, rows.shape[-1], WIDE):
            lanes = slice(j, j + WIDE)
            made = mm(rows, w[:, lanes], NN).astype(BF)
            rim[:, lanes] = made[:BLOCK]
            for i in range(4):
                most = half[i * HALF : (i + 1) * HALF, lanes]
                few = made[BLOCK + i * HALO : BLOCK + (i + 1) * HALO]
                mid[i * BLOCK : (i + 1) * BLOCK, lanes] = jnp.where(
                    first,
                    jnp.concatenate([most, few], axis=0),
                    jnp.concatenate([few, most], axis=0),
                )
    outs = (att_ref, dq_ref, dk_ref, dv_ref, dkr, dvr)
    edge_tile(is_odd("lon"), k_ref, v_ref, kr, vr, outs, q_ref, da_ref, bias_ref, scratch)


def far_kernel(
    got_b, k_ref, v_ref, wk_ref, wv_ref, q_ref, da_ref, bias_ref, near_dkr, near_dvr,
    att_ref, dq_ref, dk_ref, dv_ref, send_a, send_b,
    kr, vr, dkr, dvr, *scratch,
):
    for j in range(0, kr.shape[-1], WIDE):
        lanes = slice(j, j + WIDE)
        kr[:, lanes] = mm(got_b[...], wk_ref[:, lanes], NN).astype(BF)
        vr[:, lanes] = mm(got_b[...], wv_ref[:, lanes], NN).astype(BF)
    outs = (att_ref, dq_ref, dk_ref, dv_ref, dkr, dvr)
    left = lax.axis_index("lon") % 2 == 0
    edge_tile(left, k_ref, v_ref, kr, vr, outs, q_ref, da_ref, bias_ref, scratch)
    dk = jnp.concatenate([near_dkr[...], dkr[...]], axis=0)
    dv = jnp.concatenate([near_dvr[...], dvr[...]], axis=0)
    for j in range(0, kr.shape[-1], WIDE):
        lanes = slice(j, j + WIDE)
        part = mm(dk, wk_ref[lanes, :], NT) + mm(dv, wv_ref[lanes, :], NT)
        send_a[:, lanes] = part[:BLOCK].astype(BF)
        send_b[:, lanes] = part[BLOCK:].astype(BF)


def last_kernel(
    k_ref, v_ref, wk_ref, wv_ref, q_ref, da_ref, bias_ref,
    dkh_ref, dvh_ref, dkn_ref, dvn_ref, dkf_ref, dvf_ref,
    att_ref, dq_ref, part_ref, dko_ref, dvo_ref,
    dkr, dvr, *scratch,
):
    upper_done = is_odd("lat")
    offset = jnp.where(upper_done, HALO, 0)

    def load(lanes):
        def one(ref):
            starts = [pl.multiple_of(i * BLOCK + offset, HALO) for i in range(4)]
            return jnp.concatenate([ref[pl.ds(at, HALF), lanes] for at in starts], axis=0)

        return one(k_ref), one(v_ref)

    def store(lanes, att, dq, dk, dv):
        att_ref[:, lanes] = att
        dq_ref[:, lanes] = dq
        for grad, half, near, far, rims, own in (
            (dk, dkh_ref, dkn_ref, dkf_ref, dkr, dko_ref),
            (dv, dvh_ref, dvn_ref, dvf_ref, dvr, dvo_ref),
        ):
            sides = sort_pair("lon", near[:, lanes], far[:, lanes])
            for i in range(4):
                edge = sides[i // 2][(i % 2) * BLOCK : (i % 2 + 1) * BLOCK]
                a = half[i * HALF : (i + 1) * HALF, lanes]
                b = grad[i * HALF : (i + 1) * HALF]
                up = jnp.where(upper_done, a, b)
                down = jnp.where(upper_done, b, a)
                low = edge[:HALO] + up[:HALO]
                mine = edge[HALO:HALF] + up[HALO:] + down[: HALF - HALO]
                high = edge[HALF:] + down[HALF - HALO :]
                low, mine, high = ((x * (1.0 / SCALE)).astype(BF) for x in (low, mine, high))
                rims[i * HALO : (i + 1) * HALO, lanes] = low
                rims[BLOCK + i * HALO : BLOCK + (i + 1) * HALO, lanes] = high
                own[i * 2 * HALO : (i + 1) * 2 * HALO, lanes] = mine

    attend(jnp.where(upper_done, 2, 1), load, store, q_ref, da_ref, bias_ref, scratch)
    for j in range(0, part_ref.shape[-1], WIDE):
        lanes = slice(j, j + WIDE)
        part_ref[:, lanes] = mm(dkr[...], wk_ref[lanes, :], NT) + mm(dvr[...], wv_ref[lanes, :], NT)


def merge_kernel(part_ref, got_a, got_b, send_a, send_b):
    left, right = (x.astype(F32) for x in sort_pair("lon", got_a[...], got_b[...]))
    sides = []
    for i, rows in enumerate((slice(0, HALO), slice(HALF, BLOCK))):
        part = part_ref[i * BLOCK : (i + 1) * BLOCK]
        parts = [part[:HALO] + left[rows], part[HALO:HALF], part[HALF:] + right[rows]]
        sides.append(jnp.concatenate(parts, axis=0).astype(BF))
    send_a[...], send_b[...] = sort_pair("lat", *sides)


def emit(res_ref, tiles, w_ref, dims, out_hbm, out_scr, sem):
    first, near, far, last = (ref[...] for ref in tiles)
    rows = jnp.concatenate(
        [*sort_pair("lon", near, far)[:1], *sort_pair("lat", first, last), sort_pair("lon", near, far)[1]],
        axis=0,
    )
    copies = []
    for i, j in enumerate(range(0, out_scr.shape[-1], 256)):
        lanes = slice(j, j + 256)
        w = w_ref[:, lanes] if dims is NN else w_ref[lanes, :]
        product = mm(rows, w, dims)
        tiles = [product[t * POINTS : (t + 1) * POINTS] for t in range(TILES)]
        out_scr[:, lanes] = (res_ref[:, lanes].astype(F32) + from_tiles(tiles)).astype(BF)
        copy = pltpu.make_async_copy(out_scr.at[:, lanes], out_hbm.at[:, lanes], sem.at[i])
        copy.start()
        copies.append(copy)
    return copies


def layer_out_kernel(
    x_ref, first, near, far, last, wo_ref, piece_ref, out_hbm, pass_ref, out_scr, sem
):
    pass_ref[...] = piece_ref[...]
    for copy in emit(x_ref, (first, near, far, last), wo_ref, NN, out_hbm, out_scr, sem):
        copy.wait()


def grid_grad_kernel(
    c_ref, first, near, far, last, wq_ref, dk_ref, dv_ref, wk_ref, wv_ref, got_a, got_b,
    grad_hbm, own_ref, out_scr, sem,
):
    copies = emit(c_ref, (first, near, far, last), wq_ref, NT, grad_hbm, out_scr, sem)
    left, right = (x.astype(F32)[HALO:HALF] for x in sort_pair("lon", got_a[...], got_b[...]))
    none = jnp.zeros((BLOCK, WIDE), F32)
    for j in range(0, own_ref.shape[-1], WIDE):
        lanes = slice(j, j + WIDE)
        rims = jnp.concatenate([left[:, lanes], none, right[:, lanes]], axis=0)
        own_ref[:, lanes] = (
            mm(dk_ref[...], wk_ref[lanes, :], NT) + mm(dv_ref[...], wv_ref[lanes, :], NT) + rims
        )
    for copy in copies:
        copy.wait()


def finish_kernel(own_ref, got_a, got_b, out_hbm, out_scr, sem):
    sides = [x.astype(F32) for x in sort_pair("lat", got_a[...], got_b[...])]
    parts = [side[i * HALO : (i + 1) * HALO] for i in range(4) for side in sides]
    total = (own_ref[...] + jnp.concatenate(parts, axis=0)).astype(BF)
    dst = lax.broadcasted_iota(jnp.int32, (2 * BLOCK, 2 * BLOCK), 0)
    src = lax.broadcasted_iota(jnp.int32, (2 * BLOCK, 2 * BLOCK), 1)
    pick = jnp.where(src == to_blocks(8)(dst), 1.0, 0.0).astype(BF)
    out_scr[...] = mm(pick, total, NN).astype(BF)
    copy = pltpu.make_async_copy(out_scr, out_hbm, sem)
    copy.start()
    copy.wait()


def pairs_of(axis, ring):
    count = lax.axis_size(axis)
    even = [(i, i + 1) for i in range(0, count, 2)]
    odd = [(i, i + 1) for i in range(1, count - 1, 2)]
    if ring:
        odd.append((count - 1, 0))
    return tuple(pairs + [(b, a) for a, b in pairs] for pairs in (even, odd))


def local(grid_feat, mesh_feat, edges, edge_mask, w_query, w_key, w_value, w_out, cotangent):
    width = grid_feat.shape[-1]
    points = TILES * POINTS
    x = grid_feat.reshape(points, width)
    c = cotangent.reshape(points, width)
    own = mesh_feat.reshape(2 * BLOCK, width)
    product = 2 * width * width
    lat_a, lat_b = pairs_of("lat", False)
    lon_a, lon_b = pairs_of("lon", True)
    piece = ((BLOCK, width), BF)
    tiled = ((TILES, POINTS, width), BF)
    square = ((width, width), BF)

    send_a, send_b = call(
        lead_kernel, (own,), [piece, piece], 10**5,
        (pltpu.SemaphoreType.DMA((2,)),), hbm=(0,),
    )
    got_a = lax.ppermute(send_a, "lat", lat_a)
    q, c_near, wo_near = call(
        project_q_kernel, (x, w_query, c, w_out),
        [tiled, ((points, width), BF), square],
        points * product,
        (
            pltpu.VMEM((points, width), BF),
            pltpu.VMEM((width, width), BF),
            pltpu.SemaphoreType.DMA((7,)),
        ),
        hbm=(0, 1, 2, 3),
    )
    da, bias, late_b = call(
        project_d_kernel, (c_near, wo_near, edges, edge_mask, send_b),
        [tiled, ((TILES, NODES, POINTS), F32), piece],
        points * product,
    )
    got_b = lax.ppermute(late_b, "lat", lat_b)
    common = (w_key, w_value, q, da, bias)
    rows = ((POINTS, width), BF)
    half, half_grad = ((NODES, width), BF), ((NODES, width), F32)
    mid, mid_grad = ((MIDDLE, width), BF), ((2 * BLOCK, width), F32)
    half_rows, kh, vh, att_first, dq_first, dkh, dvh = call(
        first_kernel, (got_a, send_a, send_b, *common),
        [half] * 3 + [rows] * 2 + [half_grad] * 2,
        4 * 10**9, PAIR_SCRATCH,
    )
    rest, edge_a, edge_b = call(assemble_kernel, (half_rows, got_b), [piece] * 3, 10**8)
    edge_a = lax.ppermute(edge_a, "lon", lon_a)
    edge_b = lax.ppermute(edge_b, "lon", lon_b)
    k, v, att_near, dq_near, dkn, dvn, rim_dk, rim_dv = call(
        near_kernel, (edge_a, rest, kh, vh, *common),
        [mid] * 2 + [rows] * 2 + [mid_grad] * 2 + [piece] * 2,
        4 * 10**9, (pltpu.VMEM((BLOCK, width), BF),) * 2 + PAIR_SCRATCH,
    )
    att_far, dq_far, dkf, dvf, edge_a, edge_b = call(
        far_kernel, (edge_b, k, v, *common, rim_dk, rim_dv),
        [rows] * 2 + [mid_grad] * 2 + [piece] * 2,
        4 * 10**9, (pltpu.VMEM((BLOCK, width), BF),) * 4 + PAIR_SCRATCH,
    )
    edge_a = lax.ppermute(edge_a, "lon", lon_a)
    edge_b = lax.ppermute(edge_b, "lon", lon_b)
    att_last, dq_last, part, dk_own, dv_own = call(
        last_kernel, (k, v, *common, dkh, dvh, dkn, dvn, dkf, dvf),
        [rows] * 2 + [mid_grad] + [((2 * BLOCK, width), BF)] * 2,
        4 * 10**9, (pltpu.VMEM((2 * BLOCK, width), BF),) * 2 + PAIR_SCRATCH,
    )
    send_a, send_b = call(merge_kernel, (part, edge_a, edge_b), [piece, piece], 10**8)
    got_a = lax.ppermute(send_a, "lat", lat_a)
    out_scratch = (pltpu.VMEM((points, width), BF), pltpu.SemaphoreType.DMA((4,)))
    layer_out, late_b = call(
        layer_out_kernel, (x, att_first, att_near, att_far, att_last, w_out, send_b),
        [((points, width), BF), piece],
        points * product, out_scratch, hbm_out=(0,),
    )
    got_b = lax.ppermute(late_b, "lat", lat_b)
    grid_grad, kept = call(
        grid_grad_kernel,
        (c, dq_first, dq_near, dq_far, dq_last, w_query, dk_own, dv_own, w_key, w_value, edge_a, edge_b),
        [((points, width), BF), ((2 * BLOCK, width), F32)],
        points * product, out_scratch, hbm_out=(0,),
    )
    (mesh_grad,) = call(
        finish_kernel, (kept, got_a, got_b), [((2 * BLOCK, width), BF)], 10**6,
        (pltpu.VMEM((2 * BLOCK, width), BF), pltpu.SemaphoreType.DMA), hbm_out=(0,),
    )
    return (
        layer_out.reshape(grid_feat.shape),
        grid_grad.reshape(grid_feat.shape),
        mesh_grad.reshape(mesh_feat.shape),
    )


def solution(mesh):
    tiled = P("lat", "lon", None)
    placed = (tiled, tiled, P(None, "lat", "lon"), P(None, "lat", "lon")) + (P(),) * 4 + (tiled,)
    return jax.shard_map(
        local, mesh=mesh, in_specs=placed, out_specs=(tiled, tiled, tiled), check_vma=False
    )
```

```python
import jax
import jax.numpy as jnp
from jax import lax
from jax.experimental import pallas as pl
from jax.experimental.pallas import tpu as pltpu
from jax.sharding import PartitionSpec as P


HEADS = 16
HEAD = 64
SLOTS = 12
REACH = 4
NEG_FILL = -1e30
SCALE = 0.125
GROUP = 4
WIDE = GROUP * HEAD

TILES = 4
POINTS = 128
BLOCK = 64
NODES = 3 * BLOCK
MIDDLE = 4 * BLOCK
HALO = 16
HALF = 48

BF = jnp.bfloat16
F32 = jnp.float32
NT = (((1,), (1,)), ((), ()))
NN = (((1,), (0,)), ((), ()))
TN = (((0,), (0,)), ((), ()))
IN_VMEM = pl.BlockSpec(memory_space=pltpu.VMEM)
IN_HBM = pl.BlockSpec(memory_space=pltpu.MemorySpace.HBM)
IN_PLACE = pl.BlockSpec(memory_space=pl.ANY)


def mm(a, b, dims):
    return lax.dot_general(a, b, dims, preferred_element_type=F32)


def call(kernel, inputs, outs, flops, scratch=(), hbm=(), loose=(), hbm_out=(), limit=16 << 20):
    moved = sum(a.size * a.dtype.itemsize for a in inputs)

    def placed(i):
        return IN_HBM if i in hbm else IN_PLACE if i in loose else IN_VMEM

    return pl.pallas_call(
        kernel,
        in_specs=[placed(i) for i in range(len(inputs))],
        out_specs=[IN_HBM if i in hbm_out else IN_VMEM for i in range(len(outs))],
        out_shape=[
            jax.ShapeDtypeStruct(s, d) if i in hbm_out else pltpu.VMEM(s, d)
            for i, (s, d) in enumerate(outs)
        ],
        scratch_shapes=list(scratch),
        compiler_params=pltpu.CompilerParams(vmem_limit_bytes=limit),
        cost_estimate=pl.CostEstimate(flops=flops, bytes_accessed=moved, transcendentals=0),
    )(
        *(
            pltpu.with_memory_space_constraint(a, pltpu.MemorySpace.HBM) if i in hbm else a
            for i, a in enumerate(inputs)
        )
    )


def to_tiles(rows):
    cut = rows.reshape(16, TILES, 8, rows.shape[-1])
    parts = (cut[:, 0], cut[:8, 1:3], cut[8:, 1:3], cut[:, 3])
    return [part.reshape(POINTS, rows.shape[-1]) for part in parts]


def from_tiles(tiles):
    n = tiles[0].shape[-1]
    upper, lower = (t.reshape(8, 2, 8, n) for t in tiles[1:3])
    left, right = (t.reshape(16, 1, 8, n) for t in (tiles[0], tiles[3]))
    middle = jnp.concatenate([upper, lower], axis=0)
    return jnp.concatenate([left, middle, right], axis=1).reshape(TILES * POINTS, n)


def select(count, dst_of_src):
    dst = lax.broadcasted_iota(jnp.int32, (count, count), 0)
    src = lax.broadcasted_iota(jnp.int32, (count, count), 1)
    return jnp.where(dst == dst_of_src(src), 1.0, 0.0).astype(BF)


def to_blocks(rows):
    return lambda i: ((i % 16) // 4) * (4 * rows) + (i // 16) * 4 + i % 4


def is_odd(axis):
    return lax.axis_index(axis) % 2 == 1


def lead_kernel(mesh_ref, a_ref, b_ref, sem):
    odd = lax.axis_index("lat") % 2
    first = pltpu.make_async_copy(mesh_ref.at[pl.ds((1 - odd) * BLOCK, BLOCK)], a_ref, sem.at[0])
    second = pltpu.make_async_copy(mesh_ref.at[pl.ds(odd * BLOCK, BLOCK)], b_ref, sem.at[1])
    first.start()
    second.start()
    first.wait()
    second.wait()


def project_kernel(
    edges_hbm, mask_hbm, x_hbm, wq_hbm, c_hbm, wo_hbm, wk_hbm, wv_hbm, piece_ref,
    q_ref, da_ref, bias_ref, pass_ref, wk_ref, wv_ref,
    edges_scr, mask_scr, x_scr, wq_scr, c_scr, wo_scr, sem,
):
    pairs = (
        (edges_hbm, edges_scr), (mask_hbm, mask_scr), (x_hbm, x_scr), (wq_hbm, wq_scr),
        (c_hbm, c_scr), (wo_hbm, wo_scr), (wk_hbm, wk_ref), (wv_hbm, wv_ref),
    )
    copies = [pltpu.make_async_copy(a, b, sem.at[i]) for i, (a, b) in enumerate(pairs)]
    for copy in copies:
        copy.start()
    pass_ref[...] = piece_ref[...]
    copies[0].wait()
    copies[1].wait()
    make_bias(edges_scr, mask_scr, bias_ref)
    for first, out_ref, project in (
        (2, q_ref, lambda lanes: mm(x_scr[...], wq_scr[:, lanes], NN)),
        (4, da_ref, lambda lanes: mm(c_scr[...], wo_scr[lanes, :], NT)),
    ):
        copies[first].wait()
        copies[first + 1].wait()
        for j in range(0, q_ref.shape[-1], 256):
            lanes = slice(j, j + 256)
            for t, rows in enumerate(to_tiles(project(lanes))):
                out_ref[t, :, lanes] = rows.astype(BF) * SCALE
    copies[6].wait()
    copies[7].wait()


def make_bias(edges_ref, mask_ref, bias_ref):
    lat_start = lax.axis_index("lat") * 8
    lon_start = lax.axis_index("lon") * 16
    edges = edges_ref[...]
    row = (edges >> 10) - lat_start + REACH
    col = (edges - lon_start + REACH) & 1023
    point_row = lax.broadcasted_iota(jnp.int32, edges.shape, 1)
    point_col = lax.broadcasted_iota(jnp.int32, edges.shape, 2)
    block, inner = col >> 2, row * 4 + (col & 3)
    slot = jnp.where(
        point_col < 8,
        block * BLOCK + inner,
        jnp.where(
            point_col >= 24,
            jnp.where(block == 5, 0, block - 2) * BLOCK + inner,
            (block - 1) * HALF + inner - jnp.where(point_row < 8, 0, HALO),
        ),
    )
    slot = jnp.where(mask_ref[...] > 0, slot, -1).astype(F32).astype(BF)
    slot = slot.reshape(SLOTS * 16, 32)

    def point(lane):
        tile, i = lane >> 7, lane & 127
        outer = (tile == 0) | (tile == 3)
        row = jnp.where(outer, i >> 3, (i >> 4) + jnp.where(tile == 2, 8, 0))
        col = jnp.where(outer, (i & 7) + tile * 8, (i & 15) + 8)
        return row, col

    src = lax.broadcasted_iota(jnp.int32, (32, TILES * POINTS), 0)
    dst = lax.broadcasted_iota(jnp.int32, (32, TILES * POINTS), 1)
    pick = jnp.where(src == point(dst)[1], 1.0, 0.0).astype(BF)
    wide = mm(slot, pick, NN).reshape(SLOTS, 16, TILES * POINTS)
    lane = lax.broadcasted_iota(jnp.int32, (16, TILES * POINTS), 1)
    own_row = lax.broadcasted_iota(jnp.int32, lane.shape, 0) == point(lane)[0]
    slots = jnp.sum(jnp.where(own_row[None], wide, 0.0), axis=1)
    node = lax.broadcasted_iota(jnp.int32, (NODES, POINTS), 0).astype(F32)
    for t in range(TILES):
        at = slice(t * POINTS, (t + 1) * POINTS)
        hit = node == slots[0:1, at]
        for e in range(1, SLOTS):
            hit = hit | (node == slots[e : e + 1, at])
        bias_ref[t] = jnp.where(hit, 0.0, NEG_FILL)


def sort_pair(axis, a, b):
    odd = lax.axis_index(axis) % 2 == 1
    return jnp.where(odd, a, b), jnp.where(odd, b, a)


def assemble_kernel(half_ref, got_b, rest_ref, send_a, send_b):
    pick = select(BLOCK, to_blocks(4))
    first = is_odd("lat")
    for j in range(0, rest_ref.shape[-1], WIDE):
        lanes = slice(j, j + WIDE)
        rest = mm(pick, got_b[:, lanes], NN).astype(BF)
        rest_ref[:, lanes] = rest

        def column(i):
            most = half_ref[i * HALF : (i + 1) * HALF, lanes]
            few = rest[i * HALO : (i + 1) * HALO]
            return jnp.where(
                first, jnp.concatenate([most, few], axis=0), jnp.concatenate([few, most], axis=0)
            )

        send_a[:, lanes], send_b[:, lanes] = sort_pair("lon", column(0), column(3))


def half_masks():
    head = lax.broadcasted_iota(jnp.int32, (1, 2 * HEAD), 1) // HEAD
    return [jnp.where(head == h, 1.0, 0.0).astype(BF) for h in range(2)]


def spread_pair(block):
    return jnp.concatenate([block * m for m in half_masks()], axis=0)


def spread_group(block):
    zero = jnp.zeros((block.shape[0], 2 * HEAD), BF)
    low, high = block[:, : 2 * HEAD], block[:, 2 * HEAD :]
    masks = half_masks()
    rows = [jnp.concatenate([low * m, zero], axis=1) for m in masks]
    rows += [jnp.concatenate([zero, high * m], axis=1) for m in masks]
    return jnp.concatenate(rows, axis=0)


def pair_lanes(i):
    return slice(i * 2 * HEAD, (i + 1) * 2 * HEAD), slice(i * 2 * POINTS, (i + 1) * 2 * POINTS)


def score(keys, values, q4, d4, bufs):
    s_ref, d_ref, qs_ref, gs_ref = bufs[:4]
    for i in range(GROUP // 2):
        lanes, at = pair_lanes(i)
        qs_ref[at, :] = spread_pair(q4[:, lanes])
        gs_ref[at, :] = spread_pair(d4[:, lanes])
        s_ref[:, at] = mm(keys[:, lanes], qs_ref[at, :], NT)
        d_ref[:, at] = mm(values[:, lanes], gs_ref[at, :], NT)


def soften(bias, bufs):
    s_ref, d_ref, _, _, pw, sw, pt, st = bufs
    for h in range(GROUP):
        at = slice(h * POINTS, (h + 1) * POINTS)
        tall = slice(h * NODES, (h + 1) * NODES)
        top = jnp.max(s_ref[:, at] + bias, axis=0, keepdims=True)
        e = jnp.exp(s_ref[:, at] + bias - top)
        s_ref[:, at] = e
        inverse = 1.0 / jnp.sum(e, axis=0, keepdims=True)
        centred = jnp.sum(e * d_ref[:, at], axis=0, keepdims=True) * inverse
        p = s_ref[:, at] * inverse
        half = p.astype(BF)
        ds = (p * (d_ref[:, at] - centred)).astype(BF)
        pw[:, at] = half
        sw[:, at] = ds
        pt[tall, :] = half
        st[tall, :] = ds


def gather_grads(keys, values, bufs):
    _, _, qs_ref, gs_ref, pw, sw, pt, st = bufs
    att = mm(pt[...], spread_group(values), TN).astype(BF)
    dq = mm(st[...], spread_group(keys), TN).astype(BF)
    dk, dv = [], []
    for i in range(GROUP // 2):
        _, at = pair_lanes(i)
        dk.append(mm(sw[:, at], qs_ref[at, :], NN))
        dv.append(mm(pw[:, at], gs_ref[at, :], NN))
    return att, dq, jnp.concatenate(dk, axis=1), jnp.concatenate(dv, axis=1)


ITEM_SCRATCH = (
    (pltpu.VMEM((NODES, GROUP * POINTS), F32),) * 2
    + (pltpu.VMEM((GROUP * POINTS, 2 * HEAD), BF),) * 2
    + (pltpu.VMEM((NODES, GROUP * POINTS), BF),) * 2
    + (pltpu.VMEM((GROUP * NODES, POINTS), BF),) * 2
)
PAIR_SCRATCH = ITEM_SCRATCH * 2


def attend(tile, load, store, q_ref, da_ref, bias_ref, scratch):
    n = len(ITEM_SCRATCH)
    bufs = (scratch[:n], scratch[n:])
    items = [slice(j, j + WIDE) for j in range(0, HEADS * HEAD, WIDE)]

    def do_score(k):
        lanes = items[k]
        score(*load(lanes), q_ref[tile, :, lanes], da_ref[tile, :, lanes], bufs[k % 2])

    def do_grads(k):
        store(items[k], *gather_grads(*load(items[k]), bufs[k % 2]))

    do_score(0)
    for k in range(len(items)):
        if k > 0:
            do_grads(k - 1)
        soften(bias_ref[tile], bufs[k % 2])
        if k + 1 < len(items):
            do_score(k + 1)
    do_grads(len(items) - 1)


def store_all(*refs):
    def store(lanes, *values):
        for ref, value in zip(refs, values):
            ref[:, lanes] = value

    return store


def first_kernel(
    got_a, own_a, own_b, wk_ref, wv_ref, q_ref, da_ref, bias_ref,
    half_ref, k_ref, v_ref, att_ref, dq_ref, dk_ref, dv_ref, wkt_ref, wvt_ref, *scratch,
):
    upper = is_odd("lat")
    top = jnp.where(upper, got_a[...], own_b[...])
    bottom = jnp.where(upper, own_b[...], got_a[...])
    rows = jnp.concatenate([top, own_a[...], bottom], axis=0)
    pick = select(NODES, to_blocks(12))
    for j in range(0, half_ref.shape[-1], WIDE):
        lanes = slice(j, j + WIDE)
        half_ref[:, lanes] = mm(pick, rows[:, lanes], NN).astype(BF)
    for j in range(0, half_ref.shape[-1], WIDE):
        lanes = slice(j, j + WIDE)
        k_ref[:, lanes] = mm(half_ref[...], wk_ref[:, lanes], NN).astype(BF)
        v_ref[:, lanes] = mm(half_ref[...], wv_ref[:, lanes], NN).astype(BF)
        for i in range(0, half_ref.shape[-1], WIDE):
            rows = slice(i, i + WIDE)
            wkt_ref[lanes, rows] = wk_ref[rows, lanes].T
            wvt_ref[lanes, rows] = wv_ref[rows, lanes].T

    def load(lanes):
        return k_ref[:, lanes], v_ref[:, lanes]

    tile = jnp.where(upper, 1, 2)
    store = store_all(att_ref, dq_ref, dk_ref, dv_ref)
    attend(tile, load, store, q_ref, da_ref, bias_ref, scratch)


def edge_tile(left, k_ref, v_ref, kr, vr, outs, q_ref, da_ref, bias_ref, scratch):
    att_ref, dq_ref, dk_ref, dv_ref, dkr, dvr = outs
    start = pl.multiple_of(jnp.where(left, 0, 2 * BLOCK), 2 * BLOCK)

    def load(lanes):
        def one(rim, mid):
            return jnp.concatenate([rim[:, lanes], mid[pl.ds(start, 2 * BLOCK), lanes]], axis=0)

        return one(kr, k_ref), one(vr, v_ref)

    def store(lanes, att, dq, dk, dv):
        att_ref[:, lanes] = att
        dq_ref[:, lanes] = dq
        for grad, rim, out in ((dk, dkr, dk_ref), (dv, dvr, dv_ref)):
            rim[:, lanes] = (grad[:BLOCK] * (1.0 / SCALE)).astype(BF)
            out[:, lanes] = grad[BLOCK:]

    attend(jnp.where(left, 0, 3), load, store, q_ref, da_ref, bias_ref, scratch)


def near_kernel(
    got_a, rest_ref, kh_ref, vh_ref, wk_ref, wv_ref, q_ref, da_ref, bias_ref,
    k_ref, v_ref, att_ref, dq_ref, dk_ref, dv_ref, dkr, dvr,
    kr, vr, *scratch,
):
    rows = jnp.concatenate([got_a[...], rest_ref[...]], axis=0)
    first = is_odd("lat")
    for rim, mid, half, w in ((kr, k_ref, kh_ref, wk_ref), (vr, v_ref, vh_ref, wv_ref)):
        for j in range(0, rows.shape[-1], WIDE):
            lanes = slice(j, j + WIDE)
            made = mm(rows, w[:, lanes], NN).astype(BF)
            rim[:, lanes] = made[:BLOCK]
            for i in range(4):
                most = half[i * HALF : (i + 1) * HALF, lanes]
                few = made[BLOCK + i * HALO : BLOCK + (i + 1) * HALO]
                mid[i * BLOCK : (i + 1) * BLOCK, lanes] = jnp.where(
                    first,
                    jnp.concatenate([most, few], axis=0),
                    jnp.concatenate([few, most], axis=0),
                )
    outs = (att_ref, dq_ref, dk_ref, dv_ref, dkr, dvr)
    edge_tile(is_odd("lon"), k_ref, v_ref, kr, vr, outs, q_ref, da_ref, bias_ref, scratch)


def far_kernel(
    got_b, k_ref, v_ref, wk_ref, wv_ref, q_ref, da_ref, bias_ref, near_dkr, near_dvr,
    wkt_ref, wvt_ref,
    att_ref, dq_ref, dk_ref, dv_ref, send_a, send_b,
    kr, vr, dkr, dvr, *scratch,
):
    for j in range(0, kr.shape[-1], WIDE):
        lanes = slice(j, j + WIDE)
        kr[:, lanes] = mm(got_b[...], wk_ref[:, lanes], NN).astype(BF)
        vr[:, lanes] = mm(got_b[...], wv_ref[:, lanes], NN).astype(BF)
    outs = (att_ref, dq_ref, dk_ref, dv_ref, dkr, dvr)
    left = lax.axis_index("lon") % 2 == 0
    edge_tile(left, k_ref, v_ref, kr, vr, outs, q_ref, da_ref, bias_ref, scratch)
    dk = jnp.concatenate([near_dkr[...], dkr[...]], axis=0)
    dv = jnp.concatenate([near_dvr[...], dvr[...]], axis=0)
    for j in range(0, kr.shape[-1], WIDE):
        lanes = slice(j, j + WIDE)
        part = mm(dk, wkt_ref[:, lanes], NN) + mm(dv, wvt_ref[:, lanes], NN)
        send_a[:, lanes] = part[:BLOCK].astype(BF)
        send_b[:, lanes] = part[BLOCK:].astype(BF)


def last_kernel(
    k_ref, v_ref, wkt_ref, wvt_ref, q_ref, da_ref, bias_ref,
    dkh_ref, dvh_ref, dkn_ref, dvn_ref, dkf_ref, dvf_ref,
    att_ref, dq_ref, part_ref, dko_ref, dvo_ref,
    dkr, dvr, *scratch,
):
    upper_done = is_odd("lat")
    offset = jnp.where(upper_done, HALO, 0)

    def load(lanes):
        def one(ref):
            starts = [pl.multiple_of(i * BLOCK + offset, HALO) for i in range(4)]
            return jnp.concatenate([ref[pl.ds(at, HALF), lanes] for at in starts], axis=0)

        return one(k_ref), one(v_ref)

    def store(lanes, att, dq, dk, dv):
        att_ref[:, lanes] = att
        dq_ref[:, lanes] = dq
        for grad, half, near, far, rims, own in (
            (dk, dkh_ref, dkn_ref, dkf_ref, dkr, dko_ref),
            (dv, dvh_ref, dvn_ref, dvf_ref, dvr, dvo_ref),
        ):
            sides = sort_pair("lon", near[:, lanes], far[:, lanes])
            for i in range(4):
                edge = sides[i // 2][(i % 2) * BLOCK : (i % 2 + 1) * BLOCK]
                a = half[i * HALF : (i + 1) * HALF, lanes]
                b = grad[i * HALF : (i + 1) * HALF]
                up = jnp.where(upper_done, a, b)
                down = jnp.where(upper_done, b, a)
                low = edge[:HALO] + up[:HALO]
                mine = edge[HALO:HALF] + up[HALO:] + down[: HALF - HALO]
                high = edge[HALF:] + down[HALF - HALO :]
                low, mine, high = ((x * (1.0 / SCALE)).astype(BF) for x in (low, mine, high))
                rims[i * HALO : (i + 1) * HALO, lanes] = low
                rims[BLOCK + i * HALO : BLOCK + (i + 1) * HALO, lanes] = high
                own[i * 2 * HALO : (i + 1) * 2 * HALO, lanes] = mine

    attend(jnp.where(upper_done, 2, 1), load, store, q_ref, da_ref, bias_ref, scratch)
    for j in range(0, part_ref.shape[-1], WIDE):
        lanes = slice(j, j + WIDE)
        part_ref[:, lanes] = mm(dkr[...], wkt_ref[:, lanes], NN) + mm(dvr[...], wvt_ref[:, lanes], NN)


def merge_kernel(part_ref, got_a, got_b, send_a, send_b):
    left, right = (x.astype(F32) for x in sort_pair("lon", got_a[...], got_b[...]))
    sides = []
    for i, rows in enumerate((slice(0, HALO), slice(HALF, BLOCK))):
        part = part_ref[i * BLOCK : (i + 1) * BLOCK]
        parts = [part[:HALO] + left[rows], part[HALO:HALF], part[HALF:] + right[rows]]
        sides.append(jnp.concatenate(parts, axis=0).astype(BF))
    send_a[...], send_b[...] = sort_pair("lat", *sides)


def emit(res_ref, tiles, w_ref, dims, out_hbm, out_scr, sem):
    first, near, far, last = (ref[...] for ref in tiles)
    rows = jnp.concatenate(
        [*sort_pair("lon", near, far)[:1], *sort_pair("lat", first, last), sort_pair("lon", near, far)[1]],
        axis=0,
    )
    copies = []
    for i, j in enumerate(range(0, out_scr.shape[-1], 256)):
        lanes = slice(j, j + 256)
        w = w_ref[:, lanes] if dims is NN else w_ref[lanes, :]
        product = mm(rows, w, dims)
        tiles = [product[t * POINTS : (t + 1) * POINTS] for t in range(TILES)]
        out_scr[:, lanes] = (res_ref[:, lanes].astype(F32) + from_tiles(tiles)).astype(BF)
        copy = pltpu.make_async_copy(out_scr.at[:, lanes], out_hbm.at[:, lanes], sem.at[i])
        copy.start()
        copies.append(copy)
    return copies


def layer_out_kernel(
    x_ref, first, near, far, last, wo_ref, piece_ref, out_hbm, pass_ref, out_scr, sem
):
    pass_ref[...] = piece_ref[...]
    for copy in emit(x_ref, (first, near, far, last), wo_ref, NN, out_hbm, out_scr, sem):
        copy.wait()


def grid_grad_kernel(
    c_ref, first, near, far, last, wq_ref, dk_ref, dv_ref, wkt_ref, wvt_ref, got_a, got_b,
    grad_hbm, own_ref, out_scr, sem,
):
    copies = emit(c_ref, (first, near, far, last), wq_ref, NT, grad_hbm, out_scr, sem)
    left, right = (x.astype(F32)[HALO:HALF] for x in sort_pair("lon", got_a[...], got_b[...]))
    none = jnp.zeros((BLOCK, WIDE), F32)
    for j in range(0, own_ref.shape[-1], WIDE):
        lanes = slice(j, j + WIDE)
        rims = jnp.concatenate([left[:, lanes], none, right[:, lanes]], axis=0)
        own_ref[:, lanes] = (
            mm(dk_ref[...], wkt_ref[:, lanes], NN) + mm(dv_ref[...], wvt_ref[:, lanes], NN) + rims
        )
    for copy in copies:
        copy.wait()


def finish_kernel(own_ref, got_a, got_b, out_hbm, out_scr, sem):
    sides = [x.astype(F32) for x in sort_pair("lat", got_a[...], got_b[...])]
    parts = [side[i * HALO : (i + 1) * HALO] for i in range(4) for side in sides]
    total = (own_ref[...] + jnp.concatenate(parts, axis=0)).astype(BF)
    dst = lax.broadcasted_iota(jnp.int32, (2 * BLOCK, 2 * BLOCK), 0)
    src = lax.broadcasted_iota(jnp.int32, (2 * BLOCK, 2 * BLOCK), 1)
    pick = jnp.where(src == to_blocks(8)(dst), 1.0, 0.0).astype(BF)
    copies = []
    for i, j in enumerate(range(0, out_scr.shape[-1], 256)):
        lanes = slice(j, j + 256)
        out_scr[:, lanes] = mm(pick, total[:, lanes], NN).astype(BF)
        copy = pltpu.make_async_copy(out_scr.at[:, lanes], out_hbm.at[:, lanes], sem.at[i])
        copy.start()
        copies.append(copy)
    for copy in copies:
        copy.wait()


def pairs_of(axis, ring):
    count = lax.axis_size(axis)
    even = [(i, i + 1) for i in range(0, count, 2)]
    odd = [(i, i + 1) for i in range(1, count - 1, 2)]
    alone = [] if ring else [(0, 0), (count - 1, count - 1)]
    if ring:
        odd.append((count - 1, 0))
    even, odd = (pairs + [(b, a) for a, b in pairs] for pairs in (even, odd))
    return even, odd + alone


def local(grid_feat, mesh_feat, edges, edge_mask, w_query, w_key, w_value, w_out, cotangent):
    width = grid_feat.shape[-1]
    points = TILES * POINTS
    x = grid_feat.reshape(points, width)
    c = cotangent.reshape(points, width)
    own = mesh_feat.reshape(2 * BLOCK, width)
    product = 2 * width * width
    lat_a, lat_b = pairs_of("lat", False)
    lon_a, lon_b = pairs_of("lon", True)
    piece = ((BLOCK, width), BF)
    tiled = ((TILES, POINTS, width), BF)
    square = ((width, width), BF)

    send_a, send_b = call(
        lead_kernel, (own,), [piece, piece], 10**5,
        (pltpu.SemaphoreType.DMA((2,)),), hbm=(0,),
    )
    got_a = lax.ppermute(send_a, "lat", lat_a)
    q, da, bias, late_b, wk, wv = call(
        project_kernel,
        (edges, edge_mask, x, w_query, c, w_out, w_key, w_value, send_b),
        [tiled, tiled, ((TILES, NODES, POINTS), F32), piece, square, square],
        2 * points * product,
        (pltpu.VMEM(edges.shape, jnp.int32),) * 2
        + (pltpu.VMEM((points, width), BF), pltpu.VMEM((width, width), BF)) * 2
        + (pltpu.SemaphoreType.DMA((8,)),),
        hbm=tuple(range(8)),
    )
    got_b = lax.ppermute(late_b, "lat", lat_b)
    common = (wk, wv, q, da, bias)
    rows = ((POINTS, width), BF)
    half, half_grad = ((NODES, width), BF), ((NODES, width), F32)
    mid, mid_grad = ((MIDDLE, width), BF), ((2 * BLOCK, width), F32)
    half_rows, kh, vh, att_first, dq_first, dkh, dvh, wkt, wvt = call(
        first_kernel, (got_a, send_a, send_b, *common),
        [half] * 3 + [rows] * 2 + [half_grad] * 2 + [square] * 2,
        4 * 10**9, PAIR_SCRATCH,
    )
    rest, edge_a, edge_b = call(assemble_kernel, (half_rows, got_b), [piece] * 3, 10**8)
    edge_a = lax.ppermute(edge_a, "lon", lon_a)
    edge_b = lax.ppermute(edge_b, "lon", lon_b)
    k, v, att_near, dq_near, dkn, dvn, rim_dk, rim_dv = call(
        near_kernel, (edge_a, rest, kh, vh, *common),
        [mid] * 2 + [rows] * 2 + [mid_grad] * 2 + [piece] * 2,
        4 * 10**9, (pltpu.VMEM((BLOCK, width), BF),) * 2 + PAIR_SCRATCH,
    )
    att_far, dq_far, dkf, dvf, edge_a, edge_b = call(
        far_kernel, (edge_b, k, v, *common, rim_dk, rim_dv, wkt, wvt),
        [rows] * 2 + [mid_grad] * 2 + [piece] * 2,
        4 * 10**9, (pltpu.VMEM((BLOCK, width), BF),) * 4 + PAIR_SCRATCH,
    )
    edge_a = lax.ppermute(edge_a, "lon", lon_a)
    edge_b = lax.ppermute(edge_b, "lon", lon_b)
    att_last, dq_last, part, dk_own, dv_own = call(
        last_kernel, (k, v, wkt, wvt, q, da, bias, dkh, dvh, dkn, dvn, dkf, dvf),
        [rows] * 2 + [mid_grad] + [((2 * BLOCK, width), BF)] * 2,
        4 * 10**9, (pltpu.VMEM((2 * BLOCK, width), BF),) * 2 + PAIR_SCRATCH,
    )
    send_a, send_b = call(merge_kernel, (part, edge_a, edge_b), [piece, piece], 10**8)
    got_a = lax.ppermute(send_a, "lat", lat_a)
    out_scratch = (pltpu.VMEM((points, width), BF), pltpu.SemaphoreType.DMA((4,)))
    layer_out, late_b = call(
        layer_out_kernel, (x, att_first, att_near, att_far, att_last, w_out, send_b),
        [((points, width), BF), piece],
        points * product, out_scratch, hbm_out=(0,),
    )
    got_b = lax.ppermute(late_b, "lat", lat_b)
    grid_grad, kept = call(
        grid_grad_kernel,
        (c, dq_first, dq_near, dq_far, dq_last, w_query, dk_own, dv_own, wkt, wvt, edge_a, edge_b),
        [((points, width), BF), ((2 * BLOCK, width), F32)],
        points * product, out_scratch, hbm_out=(0,),
    )
    (mesh_grad,) = call(
        finish_kernel, (kept, got_a, got_b), [((2 * BLOCK, width), BF)], 10**6,
        (pltpu.VMEM((2 * BLOCK, width), BF), pltpu.SemaphoreType.DMA((4,))), hbm_out=(0,),
    )
    return (
        layer_out.reshape(grid_feat.shape),
        grid_grad.reshape(grid_feat.shape),
        mesh_grad.reshape(mesh_feat.shape),
    )


def solution(mesh):
    tiled = P("lat", "lon", None)
    placed = (tiled, tiled, P(None, "lat", "lon"), P(None, "lat", "lon")) + (P(),) * 4 + (tiled,)
    return jax.shard_map(
        local, mesh=mesh, in_specs=placed, out_specs=(tiled, tiled, tiled), check_vma=False
    )
```

```python
import jax
import jax.numpy as jnp
from jax import lax
from jax.experimental import pallas as pl
from jax.experimental.pallas import tpu as pltpu
from jax.sharding import PartitionSpec as P


HEADS = 16
HEAD = 64
SLOTS = 12
REACH = 4
NEG_FILL = -1e30
SCALE = 0.125
GROUP = 4
WIDE = GROUP * HEAD

TILES = 4
POINTS = 128
BLOCK = 64
NODES = 3 * BLOCK
MIDDLE = 4 * BLOCK
HALO = 16
HALF = 48

BF = jnp.bfloat16
F32 = jnp.float32
NT = (((1,), (1,)), ((), ()))
NN = (((1,), (0,)), ((), ()))
TN = (((0,), (0,)), ((), ()))
IN_VMEM = pl.BlockSpec(memory_space=pltpu.VMEM)
IN_HBM = pl.BlockSpec(memory_space=pltpu.MemorySpace.HBM)
IN_PLACE = pl.BlockSpec(memory_space=pl.ANY)


def mm(a, b, dims):
    return lax.dot_general(a, b, dims, preferred_element_type=F32)


def call(kernel, inputs, outs, flops, scratch=(), hbm=(), loose=(), hbm_out=(), limit=16 << 20):
    moved = sum(a.size * a.dtype.itemsize for a in inputs)

    def placed(i):
        return IN_HBM if i in hbm else IN_PLACE if i in loose else IN_VMEM

    return pl.pallas_call(
        kernel,
        in_specs=[placed(i) for i in range(len(inputs))],
        out_specs=[IN_HBM if i in hbm_out else IN_VMEM for i in range(len(outs))],
        out_shape=[
            jax.ShapeDtypeStruct(s, d) if i in hbm_out else pltpu.VMEM(s, d)
            for i, (s, d) in enumerate(outs)
        ],
        scratch_shapes=list(scratch),
        compiler_params=pltpu.CompilerParams(vmem_limit_bytes=limit),
        cost_estimate=pl.CostEstimate(flops=flops, bytes_accessed=moved, transcendentals=0),
    )(
        *(
            pltpu.with_memory_space_constraint(a, pltpu.MemorySpace.HBM) if i in hbm else a
            for i, a in enumerate(inputs)
        )
    )


def to_tiles(rows):
    cut = rows.reshape(16, TILES, 8, rows.shape[-1])
    parts = (cut[:, 0], cut[:8, 1:3], cut[8:, 1:3], cut[:, 3])
    return [part.reshape(POINTS, rows.shape[-1]) for part in parts]


def from_tiles(tiles):
    n = tiles[0].shape[-1]
    upper, lower = (t.reshape(8, 2, 8, n) for t in tiles[1:3])
    left, right = (t.reshape(16, 1, 8, n) for t in (tiles[0], tiles[3]))
    middle = jnp.concatenate([upper, lower], axis=0)
    return jnp.concatenate([left, middle, right], axis=1).reshape(TILES * POINTS, n)


def select(count, dst_of_src):
    dst = lax.broadcasted_iota(jnp.int32, (count, count), 0)
    src = lax.broadcasted_iota(jnp.int32, (count, count), 1)
    return jnp.where(dst == dst_of_src(src), 1.0, 0.0).astype(BF)


def to_blocks(rows):
    return lambda i: ((i % 16) // 4) * (4 * rows) + (i // 16) * 4 + i % 4


def is_odd(axis):
    return lax.axis_index(axis) % 2 == 1


def lead_kernel(mesh_ref, a_ref, b_ref, sem):
    odd = lax.axis_index("lat") % 2
    first = pltpu.make_async_copy(mesh_ref.at[pl.ds((1 - odd) * BLOCK, BLOCK)], a_ref, sem.at[0])
    second = pltpu.make_async_copy(mesh_ref.at[pl.ds(odd * BLOCK, BLOCK)], b_ref, sem.at[1])
    first.start()
    second.start()
    first.wait()
    second.wait()


def project_kernel(
    edges_hbm, mask_hbm, x_hbm, wq_hbm, c_hbm, wo_hbm, wk_hbm, wv_hbm, piece_ref,
    q_ref, da_ref, bias_ref, pass_ref, wk_ref, wv_ref,
    edges_scr, mask_scr, x_scr, wq_scr, c_scr, wo_scr, sem,
):
    pairs = (
        (edges_hbm, edges_scr), (mask_hbm, mask_scr), (x_hbm, x_scr), (wq_hbm, wq_scr),
        (c_hbm, c_scr), (wo_hbm, wo_scr), (wk_hbm, wk_ref), (wv_hbm, wv_ref),
    )
    copies = [pltpu.make_async_copy(a, b, sem.at[i]) for i, (a, b) in enumerate(pairs)]
    for copy in copies:
        copy.start()
    pass_ref[...] = piece_ref[...]
    copies[0].wait()
    copies[1].wait()
    make_bias(edges_scr, mask_scr, bias_ref)
    for first, out_ref, project in (
        (2, q_ref, lambda lanes: mm(x_scr[...], wq_scr[:, lanes], NN)),
        (4, da_ref, lambda lanes: mm(c_scr[...], wo_scr[lanes, :], NT)),
    ):
        copies[first].wait()
        copies[first + 1].wait()
        for j in range(0, q_ref.shape[-1], 256):
            lanes = slice(j, j + 256)
            for t, rows in enumerate(to_tiles(project(lanes))):
                out_ref[t, :, lanes] = rows.astype(BF) * SCALE
    copies[6].wait()
    copies[7].wait()


def make_bias(edges_ref, mask_ref, bias_ref):
    lat_start = lax.axis_index("lat") * 8
    lon_start = lax.axis_index("lon") * 16
    edges = edges_ref[...]
    row = (edges >> 10) - lat_start + REACH
    col = (edges - lon_start + REACH) & 1023
    point_row = lax.broadcasted_iota(jnp.int32, edges.shape, 1)
    point_col = lax.broadcasted_iota(jnp.int32, edges.shape, 2)
    block, inner = col >> 2, row * 4 + (col & 3)
    slot = jnp.where(
        point_col < 8,
        block * BLOCK + inner,
        jnp.where(
            point_col >= 24,
            jnp.where(block == 5, 0, block - 2) * BLOCK + inner,
            (block - 1) * HALF + inner - jnp.where(point_row < 8, 0, HALO),
        ),
    )
    slot = jnp.where(mask_ref[...] > 0, slot, -1).astype(F32).astype(BF)
    slot = slot.reshape(SLOTS * 16, 32)

    def point(lane):
        tile, i = lane >> 7, lane & 127
        outer = (tile == 0) | (tile == 3)
        row = jnp.where(outer, i >> 3, (i >> 4) + jnp.where(tile == 2, 8, 0))
        col = jnp.where(outer, (i & 7) + tile * 8, (i & 15) + 8)
        return row, col

    src = lax.broadcasted_iota(jnp.int32, (32, TILES * POINTS), 0)
    dst = lax.broadcasted_iota(jnp.int32, (32, TILES * POINTS), 1)
    pick = jnp.where(src == point(dst)[1], 1.0, 0.0).astype(BF)
    wide = mm(slot, pick, NN).reshape(SLOTS, 16, TILES * POINTS)
    lane = lax.broadcasted_iota(jnp.int32, (16, TILES * POINTS), 1)
    own_row = lax.broadcasted_iota(jnp.int32, lane.shape, 0) == point(lane)[0]
    slots = jnp.sum(jnp.where(own_row[None], wide, 0.0), axis=1)
    node = lax.broadcasted_iota(jnp.int32, (NODES, POINTS), 0).astype(F32)
    for t in range(TILES):
        at = slice(t * POINTS, (t + 1) * POINTS)
        hit = node == slots[0:1, at]
        for e in range(1, SLOTS):
            hit = hit | (node == slots[e : e + 1, at])
        bias_ref[t] = jnp.where(hit, 0.0, NEG_FILL)


def sort_pair(axis, a, b):
    odd = lax.axis_index(axis) % 2 == 1
    return jnp.where(odd, a, b), jnp.where(odd, b, a)


def assemble_kernel(half_ref, got_b, rest_ref, send_a, send_b):
    pick = select(BLOCK, to_blocks(4))
    first = is_odd("lat")
    for j in range(0, rest_ref.shape[-1], WIDE):
        lanes = slice(j, j + WIDE)
        rest = mm(pick, got_b[:, lanes], NN).astype(BF)
        rest_ref[:, lanes] = rest

        def column(i):
            most = half_ref[i * HALF : (i + 1) * HALF, lanes]
            few = rest[i * HALO : (i + 1) * HALO]
            return jnp.where(
                first, jnp.concatenate([most, few], axis=0), jnp.concatenate([few, most], axis=0)
            )

        send_a[:, lanes], send_b[:, lanes] = sort_pair("lon", column(0), column(3))


def half_masks():
    head = lax.broadcasted_iota(jnp.int32, (1, 2 * HEAD), 1) // HEAD
    return [jnp.where(head == h, 1.0, 0.0).astype(BF) for h in range(2)]


def spread_pair(block):
    return jnp.concatenate([block * m for m in half_masks()], axis=0)


def spread_group(block):
    zero = jnp.zeros((block.shape[0], 2 * HEAD), BF)
    low, high = block[:, : 2 * HEAD], block[:, 2 * HEAD :]
    masks = half_masks()
    rows = [jnp.concatenate([low * m, zero], axis=1) for m in masks]
    rows += [jnp.concatenate([zero, high * m], axis=1) for m in masks]
    return jnp.concatenate(rows, axis=0)


def pair_lanes(i):
    return slice(i * 2 * HEAD, (i + 1) * 2 * HEAD), slice(i * 2 * POINTS, (i + 1) * 2 * POINTS)


def score(keys, values, q4, d4, bufs):
    s_ref, d_ref, qs_ref, gs_ref = bufs[:4]
    for i in range(GROUP // 2):
        lanes, at = pair_lanes(i)
        qs_ref[at, :] = spread_pair(q4[:, lanes])
        gs_ref[at, :] = spread_pair(d4[:, lanes])
        s_ref[:, at] = mm(keys[:, lanes], qs_ref[at, :], NT)
        d_ref[:, at] = mm(values[:, lanes], gs_ref[at, :], NT)


def soften(bias, bufs):
    s_ref, d_ref, _, _, pw, sw, pt, st = bufs
    for h in range(GROUP):
        at = slice(h * POINTS, (h + 1) * POINTS)
        tall = slice(h * NODES, (h + 1) * NODES)
        top = jnp.max(s_ref[:, at] + bias, axis=0, keepdims=True)
        e = jnp.exp(s_ref[:, at] + bias - top)
        s_ref[:, at] = e
        inverse = 1.0 / jnp.sum(e, axis=0, keepdims=True)
        centred = jnp.sum(e * d_ref[:, at], axis=0, keepdims=True) * inverse
        p = s_ref[:, at] * inverse
        half = p.astype(BF)
        ds = (p * (d_ref[:, at] - centred)).astype(BF)
        pw[:, at] = half
        sw[:, at] = ds
        pt[tall, :] = half
        st[tall, :] = ds


def gather_grads(keys, values, bufs):
    _, _, qs_ref, gs_ref, pw, sw, pt, st = bufs
    att = mm(pt[...], spread_group(values), TN).astype(BF)
    dq = mm(st[...], spread_group(keys), TN).astype(BF)
    dk, dv = [], []
    for i in range(GROUP // 2):
        _, at = pair_lanes(i)
        dk.append(mm(sw[:, at], qs_ref[at, :], NN))
        dv.append(mm(pw[:, at], gs_ref[at, :], NN))
    return att, dq, jnp.concatenate(dk, axis=1), jnp.concatenate(dv, axis=1)


ITEM_SCRATCH = (
    (pltpu.VMEM((NODES, GROUP * POINTS), F32),) * 2
    + (pltpu.VMEM((GROUP * POINTS, 2 * HEAD), BF),) * 2
    + (pltpu.VMEM((NODES, GROUP * POINTS), BF),) * 2
    + (pltpu.VMEM((GROUP * NODES, POINTS), BF),) * 2
)
PAIR_SCRATCH = ITEM_SCRATCH * 2


def attend(tile, load, store, q_ref, da_ref, bias_ref, scratch):
    n = len(ITEM_SCRATCH)
    bufs = (scratch[:n], scratch[n:])
    items = [slice(j, j + WIDE) for j in range(0, HEADS * HEAD, WIDE)]

    def do_score(k):
        lanes = items[k]
        score(*load(lanes), q_ref[tile, :, lanes], da_ref[tile, :, lanes], bufs[k % 2])

    def do_grads(k):
        store(items[k], *gather_grads(*load(items[k]), bufs[k % 2]))

    do_score(0)
    for k in range(len(items)):
        if k > 0:
            do_grads(k - 1)
        soften(bias_ref[tile], bufs[k % 2])
        if k + 1 < len(items):
            do_score(k + 1)
    do_grads(len(items) - 1)


def store_all(*refs):
    def store(lanes, *values):
        for ref, value in zip(refs, values):
            ref[:, lanes] = value

    return store


def first_kernel(
    got_a, own_a, own_b, wk_ref, wv_ref, q_ref, da_ref, bias_ref,
    half_ref, k_ref, v_ref, att_ref, dq_ref, dk_ref, dv_ref, wkt_ref, wvt_ref, *scratch,
):
    upper = is_odd("lat")
    top = jnp.where(upper, got_a[...], own_b[...])
    bottom = jnp.where(upper, own_b[...], got_a[...])
    rows = jnp.concatenate([top, own_a[...], bottom], axis=0)
    pick = select(NODES, to_blocks(12))
    for j in range(0, half_ref.shape[-1], WIDE):
        lanes = slice(j, j + WIDE)
        half_ref[:, lanes] = mm(pick, rows[:, lanes], NN).astype(BF)
    for j in range(0, half_ref.shape[-1], WIDE):
        lanes = slice(j, j + WIDE)
        k_ref[:, lanes] = mm(half_ref[...], wk_ref[:, lanes], NN).astype(BF)
        v_ref[:, lanes] = mm(half_ref[...], wv_ref[:, lanes], NN).astype(BF)
        for i in range(0, half_ref.shape[-1], WIDE):
            rows = slice(i, i + WIDE)
            wkt_ref[lanes, rows] = wk_ref[rows, lanes].T
            wvt_ref[lanes, rows] = wv_ref[rows, lanes].T

    def load(lanes):
        return k_ref[:, lanes], v_ref[:, lanes]

    tile = jnp.where(upper, 1, 2)
    store = store_all(att_ref, dq_ref, dk_ref, dv_ref)
    attend(tile, load, store, q_ref, da_ref, bias_ref, scratch)


def edge_tile(left, k_ref, v_ref, kr, vr, outs, q_ref, da_ref, bias_ref, scratch):
    att_ref, dq_ref, dk_ref, dv_ref, dkr, dvr = outs
    start = pl.multiple_of(jnp.where(left, 0, 2 * BLOCK), 2 * BLOCK)

    def load(lanes):
        def one(rim, mid):
            return jnp.concatenate([rim[:, lanes], mid[pl.ds(start, 2 * BLOCK), lanes]], axis=0)

        return one(kr, k_ref), one(vr, v_ref)

    def store(lanes, att, dq, dk, dv):
        att_ref[:, lanes] = att
        dq_ref[:, lanes] = dq
        for grad, rim, out in ((dk, dkr, dk_ref), (dv, dvr, dv_ref)):
            rim[:, lanes] = (grad[:BLOCK] * (1.0 / SCALE)).astype(BF)
            out[:, lanes] = grad[BLOCK:]

    attend(jnp.where(left, 0, 3), load, store, q_ref, da_ref, bias_ref, scratch)


def near_kernel(
    got_a, rest_ref, kh_ref, vh_ref, wk_ref, wv_ref, q_ref, da_ref, bias_ref,
    k_ref, v_ref, att_ref, dq_ref, dk_ref, dv_ref, dkr, dvr,
    kr, vr, *scratch,
):
    rows = jnp.concatenate([got_a[...], rest_ref[...]], axis=0)
    first = is_odd("lat")
    for rim, mid, half, w in ((kr, k_ref, kh_ref, wk_ref), (vr, v_ref, vh_ref, wv_ref)):
        for j in range(0, rows.shape[-1], WIDE):
            lanes = slice(j, j + WIDE)
            made = mm(rows, w[:, lanes], NN).astype(BF)
            rim[:, lanes] = made[:BLOCK]
            for i in range(4):
                most = half[i * HALF : (i + 1) * HALF, lanes]
                few = made[BLOCK + i * HALO : BLOCK + (i + 1) * HALO]
                mid[i * BLOCK : (i + 1) * BLOCK, lanes] = jnp.where(
                    first,
                    jnp.concatenate([most, few], axis=0),
                    jnp.concatenate([few, most], axis=0),
                )
    outs = (att_ref, dq_ref, dk_ref, dv_ref, dkr, dvr)
    edge_tile(is_odd("lon"), k_ref, v_ref, kr, vr, outs, q_ref, da_ref, bias_ref, scratch)


def far_kernel(
    got_b, k_ref, v_ref, wk_ref, wv_ref, q_ref, da_ref, bias_ref, near_dkr, near_dvr,
    wkt_ref, wvt_ref,
    att_ref, dq_ref, dk_ref, dv_ref, send_a, send_b,
    kr, vr, dkr, dvr, *scratch,
):
    for j in range(0, kr.shape[-1], WIDE):
        lanes = slice(j, j + WIDE)
        kr[:, lanes] = mm(got_b[...], wk_ref[:, lanes], NN).astype(BF)
        vr[:, lanes] = mm(got_b[...], wv_ref[:, lanes], NN).astype(BF)
    outs = (att_ref, dq_ref, dk_ref, dv_ref, dkr, dvr)
    left = lax.axis_index("lon") % 2 == 0
    edge_tile(left, k_ref, v_ref, kr, vr, outs, q_ref, da_ref, bias_ref, scratch)
    dk = jnp.concatenate([near_dkr[...], dkr[...]], axis=0)
    dv = jnp.concatenate([near_dvr[...], dvr[...]], axis=0)
    for j in range(0, kr.shape[-1], WIDE):
        lanes = slice(j, j + WIDE)
        part = mm(dk, wkt_ref[:, lanes], NN) + mm(dv, wvt_ref[:, lanes], NN)
        send_a[:, lanes] = part[:BLOCK].astype(BF)
        send_b[:, lanes] = part[BLOCK:].astype(BF)


def last_kernel(
    k_ref, v_ref, wkt_ref, wvt_ref, q_ref, da_ref, bias_ref,
    dkh_ref, dvh_ref, dkn_ref, dvn_ref, dkf_ref, dvf_ref,
    att_ref, dq_ref, part_ref, dko_ref, dvo_ref,
    dkr, dvr, *scratch,
):
    upper_done = is_odd("lat")
    offset = jnp.where(upper_done, HALO, 0)

    def load(lanes):
        def one(ref):
            starts = [pl.multiple_of(i * BLOCK + offset, HALO) for i in range(4)]
            return jnp.concatenate([ref[pl.ds(at, HALF), lanes] for at in starts], axis=0)

        return one(k_ref), one(v_ref)

    def store(lanes, att, dq, dk, dv):
        att_ref[:, lanes] = att
        dq_ref[:, lanes] = dq
        for grad, half, near, far, rims, own in (
            (dk, dkh_ref, dkn_ref, dkf_ref, dkr, dko_ref),
            (dv, dvh_ref, dvn_ref, dvf_ref, dvr, dvo_ref),
        ):
            sides = sort_pair("lon", near[:, lanes], far[:, lanes])
            for i in range(4):
                edge = sides[i // 2][(i % 2) * BLOCK : (i % 2 + 1) * BLOCK]
                a = half[i * HALF : (i + 1) * HALF, lanes]
                b = grad[i * HALF : (i + 1) * HALF]
                up = jnp.where(upper_done, a, b)
                down = jnp.where(upper_done, b, a)
                low = edge[:HALO] + up[:HALO]
                mine = edge[HALO:HALF] + up[HALO:] + down[: HALF - HALO]
                high = edge[HALF:] + down[HALF - HALO :]
                low, mine, high = ((x * (1.0 / SCALE)).astype(BF) for x in (low, mine, high))
                rims[i * HALO : (i + 1) * HALO, lanes] = low
                rims[BLOCK + i * HALO : BLOCK + (i + 1) * HALO, lanes] = high
                own[i * 2 * HALO : (i + 1) * 2 * HALO, lanes] = mine

    attend(jnp.where(upper_done, 2, 1), load, store, q_ref, da_ref, bias_ref, scratch)
    for j in range(0, part_ref.shape[-1], WIDE):
        lanes = slice(j, j + WIDE)
        part_ref[:, lanes] = mm(dkr[...], wkt_ref[:, lanes], NN) + mm(dvr[...], wvt_ref[:, lanes], NN)


def merge_kernel(part_ref, got_a, got_b, send_a, send_b):
    left, right = (x.astype(F32) for x in sort_pair("lon", got_a[...], got_b[...]))
    sides = []
    for i, rows in enumerate((slice(0, HALO), slice(HALF, BLOCK))):
        part = part_ref[i * BLOCK : (i + 1) * BLOCK]
        parts = [part[:HALO] + left[rows], part[HALO:HALF], part[HALF:] + right[rows]]
        sides.append(jnp.concatenate(parts, axis=0).astype(BF))
    send_a[...], send_b[...] = sort_pair("lat", *sides)


def emit(res_ref, tiles, w_ref, dims, out_hbm, out_scr, sem):
    first, near, far, last = (ref[...] for ref in tiles)
    rows = jnp.concatenate(
        [*sort_pair("lon", near, far)[:1], *sort_pair("lat", first, last), sort_pair("lon", near, far)[1]],
        axis=0,
    )
    copies = []
    for i, j in enumerate(range(0, out_scr.shape[-1], 256)):
        lanes = slice(j, j + 256)
        w = w_ref[:, lanes] if dims is NN else w_ref[lanes, :]
        product = mm(rows, w, dims)
        tiles = [product[t * POINTS : (t + 1) * POINTS] for t in range(TILES)]
        out_scr[:, lanes] = (res_ref[:, lanes].astype(F32) + from_tiles(tiles)).astype(BF)
        copy = pltpu.make_async_copy(out_scr.at[:, lanes], out_hbm.at[:, lanes], sem.at[i])
        copy.start()
        copies.append(copy)
    return copies


def layer_out_kernel(
    x_ref, first, near, far, last, wo_ref, piece_ref, out_hbm, pass_ref, out_scr, sem
):
    pass_ref[...] = piece_ref[...]
    for copy in emit(x_ref, (first, near, far, last), wo_ref, NN, out_hbm, out_scr, sem):
        copy.wait()


def grid_grad_kernel(
    c_ref, first, near, far, last, wq_ref, dk_ref, dv_ref, wkt_ref, wvt_ref, got_a, got_b,
    grad_hbm, own_ref, out_scr, sem,
):
    copies = emit(c_ref, (first, near, far, last), wq_ref, NT, grad_hbm, out_scr, sem)
    left, right = (x.astype(F32)[HALO:HALF] for x in sort_pair("lon", got_a[...], got_b[...]))
    none = jnp.zeros((BLOCK, WIDE), F32)
    for j in range(0, own_ref.shape[-1], WIDE):
        lanes = slice(j, j + WIDE)
        rims = jnp.concatenate([left[:, lanes], none, right[:, lanes]], axis=0)
        own_ref[:, lanes] = (
            mm(dk_ref[...], wkt_ref[:, lanes], NN) + mm(dv_ref[...], wvt_ref[:, lanes], NN) + rims
        )
    for copy in copies:
        copy.wait()


def finish_kernel(own_ref, got_a, got_b, out_hbm, out_scr, sem):
    sides = [x.astype(F32) for x in sort_pair("lat", got_a[...], got_b[...])]
    parts = [side[i * HALO : (i + 1) * HALO] for i in range(4) for side in sides]
    total = (own_ref[...] + jnp.concatenate(parts, axis=0)).astype(BF)
    dst = lax.broadcasted_iota(jnp.int32, (2 * BLOCK, 2 * BLOCK), 0)
    src = lax.broadcasted_iota(jnp.int32, (2 * BLOCK, 2 * BLOCK), 1)
    pick = jnp.where(src == to_blocks(8)(dst), 1.0, 0.0).astype(BF)
    copies = []
    for i, j in enumerate(range(0, out_scr.shape[-1], 256)):
        lanes = slice(j, j + 256)
        out_scr[:, lanes] = mm(pick, total[:, lanes], NN).astype(BF)
        copy = pltpu.make_async_copy(out_scr.at[:, lanes], out_hbm.at[:, lanes], sem.at[i])
        copy.start()
        copies.append(copy)
    for copy in copies:
        copy.wait()


def pairs_of(axis):
    count = lax.axis_size(axis)
    even = [(i, i + 1) for i in range(0, count, 2)]
    odd = [(i, (i + 1) % count) for i in range(1, count, 2)]
    return [pairs + [(b, a) for a, b in pairs] for pairs in (even, odd)]


def local(grid_feat, mesh_feat, edges, edge_mask, w_query, w_key, w_value, w_out, cotangent):
    width = grid_feat.shape[-1]
    points = TILES * POINTS
    x = grid_feat.reshape(points, width)
    c = cotangent.reshape(points, width)
    own = mesh_feat.reshape(2 * BLOCK, width)
    product = 2 * width * width
    lat_a, lat_b = pairs_of("lat")
    lon_a, lon_b = pairs_of("lon")
    piece = ((BLOCK, width), BF)
    tiled = ((TILES, POINTS, width), BF)
    square = ((width, width), BF)

    send_a, send_b = call(
        lead_kernel, (own,), [piece, piece], 10**5,
        (pltpu.SemaphoreType.DMA((2,)),), hbm=(0,),
    )
    got_a = lax.ppermute(send_a, "lat", lat_a)
    q, da, bias, late_b, wk, wv = call(
        project_kernel,
        (edges, edge_mask, x, w_query, c, w_out, w_key, w_value, send_b),
        [tiled, tiled, ((TILES, NODES, POINTS), F32), piece, square, square],
        2 * points * product,
        (pltpu.VMEM(edges.shape, jnp.int32),) * 2
        + (pltpu.VMEM((points, width), BF), pltpu.VMEM((width, width), BF)) * 2
        + (pltpu.SemaphoreType.DMA((8,)),),
        hbm=tuple(range(8)),
    )
    got_b = lax.ppermute(late_b, "lat", lat_b)
    common = (wk, wv, q, da, bias)
    rows = ((POINTS, width), BF)
    half, half_grad = ((NODES, width), BF), ((NODES, width), F32)
    mid, mid_grad = ((MIDDLE, width), BF), ((2 * BLOCK, width), F32)
    half_rows, kh, vh, att_first, dq_first, dkh, dvh, wkt, wvt = call(
        first_kernel, (got_a, send_a, send_b, *common),
        [half] * 3 + [rows] * 2 + [half_grad] * 2 + [square] * 2,
        4 * 10**9, PAIR_SCRATCH,
    )
    rest, edge_a, edge_b = call(assemble_kernel, (half_rows, got_b), [piece] * 3, 10**8)
    edge_a = lax.ppermute(edge_a, "lon", lon_a)
    edge_b = lax.ppermute(edge_b, "lon", lon_b)
    k, v, att_near, dq_near, dkn, dvn, rim_dk, rim_dv = call(
        near_kernel, (edge_a, rest, kh, vh, *common),
        [mid] * 2 + [rows] * 2 + [mid_grad] * 2 + [piece] * 2,
        4 * 10**9, (pltpu.VMEM((BLOCK, width), BF),) * 2 + PAIR_SCRATCH,
    )
    att_far, dq_far, dkf, dvf, edge_a, edge_b = call(
        far_kernel, (edge_b, k, v, *common, rim_dk, rim_dv, wkt, wvt),
        [rows] * 2 + [mid_grad] * 2 + [piece] * 2,
        4 * 10**9, (pltpu.VMEM((BLOCK, width), BF),) * 4 + PAIR_SCRATCH,
    )
    edge_a = lax.ppermute(edge_a, "lon", lon_a)
    edge_b = lax.ppermute(edge_b, "lon", lon_b)
    att_last, dq_last, part, dk_own, dv_own = call(
        last_kernel, (k, v, wkt, wvt, q, da, bias, dkh, dvh, dkn, dvn, dkf, dvf),
        [rows] * 2 + [mid_grad] + [((2 * BLOCK, width), BF)] * 2,
        4 * 10**9, (pltpu.VMEM((2 * BLOCK, width), BF),) * 2 + PAIR_SCRATCH,
    )
    send_a, send_b = call(merge_kernel, (part, edge_a, edge_b), [piece, piece], 10**8)
    got_a = lax.ppermute(send_a, "lat", lat_a)
    out_scratch = (pltpu.VMEM((points, width), BF), pltpu.SemaphoreType.DMA((4,)))
    layer_out, late_b = call(
        layer_out_kernel, (x, att_first, att_near, att_far, att_last, w_out, send_b),
        [((points, width), BF), piece],
        points * product, out_scratch, hbm_out=(0,),
    )
    got_b = lax.ppermute(late_b, "lat", lat_b)
    grid_grad, kept = call(
        grid_grad_kernel,
        (c, dq_first, dq_near, dq_far, dq_last, w_query, dk_own, dv_own, wkt, wvt, edge_a, edge_b),
        [((points, width), BF), ((2 * BLOCK, width), F32)],
        points * product, out_scratch, hbm_out=(0,),
    )
    (mesh_grad,) = call(
        finish_kernel, (kept, got_a, got_b), [((2 * BLOCK, width), BF)], 10**6,
        (pltpu.VMEM((2 * BLOCK, width), BF), pltpu.SemaphoreType.DMA((4,))), hbm_out=(0,),
    )
    return (
        layer_out.reshape(grid_feat.shape),
        grid_grad.reshape(grid_feat.shape),
        mesh_grad.reshape(mesh_feat.shape),
    )


def solution(mesh):
    tiled = P("lat", "lon", None)
    placed = (tiled, tiled, P(None, "lat", "lon"), P(None, "lat", "lon")) + (P(),) * 4 + (tiled,)
    return jax.shard_map(
        local, mesh=mesh, in_specs=placed, out_specs=(tiled, tiled, tiled), check_vma=False
    )
```

```python
import jax
import jax.numpy as jnp
from jax import lax
from jax.experimental import pallas as pl
from jax.experimental.pallas import tpu as pltpu
from jax.sharding import PartitionSpec as P


HEADS = 16
HEAD = 64
SLOTS = 12
REACH = 4
NEG_FILL = -1e30
SCALE = 0.125
GROUP = 4
WIDE = GROUP * HEAD

TILES = 4
POINTS = 128
BLOCK = 64
NODES = 3 * BLOCK
MIDDLE = 4 * BLOCK
HALO = 16
HALF = 48

BF = jnp.bfloat16
F32 = jnp.float32
NT = (((1,), (1,)), ((), ()))
NN = (((1,), (0,)), ((), ()))
TN = (((0,), (0,)), ((), ()))
IN_VMEM = pl.BlockSpec(memory_space=pltpu.VMEM)
IN_HBM = pl.BlockSpec(memory_space=pltpu.MemorySpace.HBM)
IN_PLACE = pl.BlockSpec(memory_space=pl.ANY)


def mm(a, b, dims):
    return lax.dot_general(a, b, dims, preferred_element_type=F32)


def call(kernel, inputs, outs, flops, scratch=(), hbm=(), loose=(), hbm_out=(), limit=16 << 20):
    moved = sum(a.size * a.dtype.itemsize for a in inputs)

    def placed(i):
        return IN_HBM if i in hbm else IN_PLACE if i in loose else IN_VMEM

    return pl.pallas_call(
        kernel,
        in_specs=[placed(i) for i in range(len(inputs))],
        out_specs=[IN_HBM if i in hbm_out else IN_VMEM for i in range(len(outs))],
        out_shape=[
            jax.ShapeDtypeStruct(s, d) if i in hbm_out else pltpu.VMEM(s, d)
            for i, (s, d) in enumerate(outs)
        ],
        scratch_shapes=list(scratch),
        compiler_params=pltpu.CompilerParams(vmem_limit_bytes=limit),
        cost_estimate=pl.CostEstimate(flops=flops, bytes_accessed=moved, transcendentals=0),
    )(
        *(
            pltpu.with_memory_space_constraint(a, pltpu.MemorySpace.HBM) if i in hbm else a
            for i, a in enumerate(inputs)
        )
    )


def to_tiles(rows):
    cut = rows.reshape(16, TILES, 8, rows.shape[-1])
    parts = (cut[:, 0], cut[:8, 1:3], cut[8:, 1:3], cut[:, 3])
    return [part.reshape(POINTS, rows.shape[-1]) for part in parts]


def from_tiles(tiles):
    n = tiles[0].shape[-1]
    upper, lower = (t.reshape(8, 2, 8, n) for t in tiles[1:3])
    left, right = (t.reshape(16, 1, 8, n) for t in (tiles[0], tiles[3]))
    middle = jnp.concatenate([upper, lower], axis=0)
    return jnp.concatenate([left, middle, right], axis=1).reshape(TILES * POINTS, n)


def select(count, dst_of_src):
    dst = lax.broadcasted_iota(jnp.int32, (count, count), 0)
    src = lax.broadcasted_iota(jnp.int32, (count, count), 1)
    return jnp.where(dst == dst_of_src(src), 1.0, 0.0).astype(BF)


def to_blocks(rows):
    return lambda i: ((i % 16) // 4) * (4 * rows) + (i // 16) * 4 + i % 4


def is_odd(axis):
    return lax.axis_index(axis) % 2 == 1


def lead_kernel(mesh_ref, a_ref, b_ref, sem):
    odd = lax.axis_index("lat") % 2
    first = pltpu.make_async_copy(mesh_ref.at[pl.ds((1 - odd) * BLOCK, BLOCK)], a_ref, sem.at[0])
    second = pltpu.make_async_copy(mesh_ref.at[pl.ds(odd * BLOCK, BLOCK)], b_ref, sem.at[1])
    first.start()
    second.start()
    first.wait()
    second.wait()


def project_kernel(
    edges_hbm, mask_hbm, x_hbm, wq_hbm, c_hbm, wo_hbm, wk_hbm, wv_hbm,
    q_ref, da_ref, bias_ref, wk_ref, wv_ref,
    edges_scr, mask_scr, x_scr, wq_scr, c_scr, wo_scr, sem,
):
    pairs = (
        (edges_hbm, edges_scr), (mask_hbm, mask_scr), (x_hbm, x_scr), (wq_hbm, wq_scr),
        (c_hbm, c_scr), (wo_hbm, wo_scr), (wk_hbm, wk_ref), (wv_hbm, wv_ref),
    )
    copies = [pltpu.make_async_copy(a, b, sem.at[i]) for i, (a, b) in enumerate(pairs)]
    for copy in copies:
        copy.start()
    copies[0].wait()
    copies[1].wait()
    make_bias(edges_scr, mask_scr, bias_ref)
    for first, out_ref, project in (
        (2, q_ref, lambda lanes: mm(x_scr[...], wq_scr[:, lanes], NN)),
        (4, da_ref, lambda lanes: mm(c_scr[...], wo_scr[lanes, :], NT)),
    ):
        copies[first].wait()
        copies[first + 1].wait()
        for j in range(0, q_ref.shape[-1], 256):
            lanes = slice(j, j + 256)
            for t, rows in enumerate(to_tiles(project(lanes))):
                out_ref[t, :, lanes] = rows.astype(BF) * SCALE
    copies[6].wait()
    copies[7].wait()


def make_bias(edges_ref, mask_ref, bias_ref):
    lat_start = lax.axis_index("lat") * 8
    lon_start = lax.axis_index("lon") * 16
    edges = edges_ref[...]
    row = (edges >> 10) - lat_start + REACH
    col = (edges - lon_start + REACH) & 1023
    point_row = lax.broadcasted_iota(jnp.int32, edges.shape, 1)
    point_col = lax.broadcasted_iota(jnp.int32, edges.shape, 2)
    block, inner = col >> 2, row * 4 + (col & 3)
    slot = jnp.where(
        point_col < 8,
        block * BLOCK + inner,
        jnp.where(
            point_col >= 24,
            jnp.where(block == 5, 0, block - 2) * BLOCK + inner,
            (block - 1) * HALF + inner - jnp.where(point_row < 8, 0, HALO),
        ),
    )
    slot = jnp.where(mask_ref[...] > 0, slot, -1).astype(F32).astype(BF)
    slot = slot.reshape(SLOTS * 16, 32)

    def point(lane):
        tile, i = lane >> 7, lane & 127
        outer = (tile == 0) | (tile == 3)
        row = jnp.where(outer, i >> 3, (i >> 4) + jnp.where(tile == 2, 8, 0))
        col = jnp.where(outer, (i & 7) + tile * 8, (i & 15) + 8)
        return row, col

    src = lax.broadcasted_iota(jnp.int32, (32, TILES * POINTS), 0)
    dst = lax.broadcasted_iota(jnp.int32, (32, TILES * POINTS), 1)
    pick = jnp.where(src == point(dst)[1], 1.0, 0.0).astype(BF)
    wide = mm(slot, pick, NN).reshape(SLOTS, 16, TILES * POINTS)
    lane = lax.broadcasted_iota(jnp.int32, (16, TILES * POINTS), 1)
    own_row = lax.broadcasted_iota(jnp.int32, lane.shape, 0) == point(lane)[0]
    slots = jnp.sum(jnp.where(own_row[None], wide, 0.0), axis=1)
    node = lax.broadcasted_iota(jnp.int32, (NODES, POINTS), 0).astype(F32)
    for t in range(TILES):
        at = slice(t * POINTS, (t + 1) * POINTS)
        hit = node == slots[0:1, at]
        for e in range(1, SLOTS):
            hit = hit | (node == slots[e : e + 1, at])
        bias_ref[t] = jnp.where(hit, 0.0, NEG_FILL)


def sort_pair(axis, a, b):
    odd = lax.axis_index(axis) % 2 == 1
    return jnp.where(odd, a, b), jnp.where(odd, b, a)


def assemble_kernel(half_ref, got_b, rest_ref, send_a, send_b):
    pick = select(BLOCK, to_blocks(4))
    first = is_odd("lat")
    for j in range(0, rest_ref.shape[-1], WIDE):
        lanes = slice(j, j + WIDE)
        rest = mm(pick, got_b[:, lanes], NN).astype(BF)
        rest_ref[:, lanes] = rest

        def column(i):
            most = half_ref[i * HALF : (i + 1) * HALF, lanes]
            few = rest[i * HALO : (i + 1) * HALO]
            return jnp.where(
                first, jnp.concatenate([most, few], axis=0), jnp.concatenate([few, most], axis=0)
            )

        send_a[:, lanes], send_b[:, lanes] = sort_pair("lon", column(0), column(3))


def half_masks():
    head = lax.broadcasted_iota(jnp.int32, (1, 2 * HEAD), 1) // HEAD
    return [jnp.where(head == h, 1.0, 0.0).astype(BF) for h in range(2)]


def spread_pair(block):
    return jnp.concatenate([block * m for m in half_masks()], axis=0)


def spread_group(block):
    zero = jnp.zeros((block.shape[0], 2 * HEAD), BF)
    low, high = block[:, : 2 * HEAD], block[:, 2 * HEAD :]
    masks = half_masks()
    rows = [jnp.concatenate([low * m, zero], axis=1) for m in masks]
    rows += [jnp.concatenate([zero, high * m], axis=1) for m in masks]
    return jnp.concatenate(rows, axis=0)


def pair_lanes(i):
    return slice(i * 2 * HEAD, (i + 1) * 2 * HEAD), slice(i * 2 * POINTS, (i + 1) * 2 * POINTS)


def score(keys, values, q4, d4, bufs):
    s_ref, d_ref, qs_ref, gs_ref = bufs[:4]
    for i in range(GROUP // 2):
        lanes, at = pair_lanes(i)
        qs_ref[at, :] = spread_pair(q4[:, lanes])
        gs_ref[at, :] = spread_pair(d4[:, lanes])
        s_ref[:, at] = mm(keys[:, lanes], qs_ref[at, :], NT)
        d_ref[:, at] = mm(values[:, lanes], gs_ref[at, :], NT)


def soften(bias, bufs):
    s_ref, d_ref, _, _, pw, sw, pt, st = bufs
    for h in range(GROUP):
        at = slice(h * POINTS, (h + 1) * POINTS)
        tall = slice(h * NODES, (h + 1) * NODES)
        top = jnp.max(s_ref[:, at] + bias, axis=0, keepdims=True)
        e = jnp.exp(s_ref[:, at] + bias - top)
        s_ref[:, at] = e
        inverse = 1.0 / jnp.sum(e, axis=0, keepdims=True)
        centred = jnp.sum(e * d_ref[:, at], axis=0, keepdims=True) * inverse
        p = s_ref[:, at] * inverse
        half = p.astype(BF)
        ds = (p * (d_ref[:, at] - centred)).astype(BF)
        pw[:, at] = half
        sw[:, at] = ds
        pt[tall, :] = half
        st[tall, :] = ds


def gather_grads(keys, values, bufs):
    _, _, qs_ref, gs_ref, pw, sw, pt, st = bufs
    att = mm(pt[...], spread_group(values), TN).astype(BF)
    dq = mm(st[...], spread_group(keys), TN).astype(BF)
    dk, dv = [], []
    for i in range(GROUP // 2):
        _, at = pair_lanes(i)
        dk.append(mm(sw[:, at], qs_ref[at, :], NN))
        dv.append(mm(pw[:, at], gs_ref[at, :], NN))
    return att, dq, jnp.concatenate(dk, axis=1), jnp.concatenate(dv, axis=1)


ITEM_SCRATCH = (
    (pltpu.VMEM((NODES, GROUP * POINTS), F32),) * 2
    + (pltpu.VMEM((GROUP * POINTS, 2 * HEAD), BF),) * 2
    + (pltpu.VMEM((NODES, GROUP * POINTS), BF),) * 2
    + (pltpu.VMEM((GROUP * NODES, POINTS), BF),) * 2
)
PAIR_SCRATCH = ITEM_SCRATCH * 2


def attend(tile, load, store, q_ref, da_ref, bias_ref, scratch):
    n = len(ITEM_SCRATCH)
    bufs = (scratch[:n], scratch[n:])
    items = [slice(j, j + WIDE) for j in range(0, HEADS * HEAD, WIDE)]

    def do_score(k):
        lanes = items[k]
        score(*load(lanes), q_ref[tile, :, lanes], da_ref[tile, :, lanes], bufs[k % 2])

    def do_grads(k):
        store(items[k], *gather_grads(*load(items[k]), bufs[k % 2]))

    do_score(0)
    for k in range(len(items)):
        if k > 0:
            do_grads(k - 1)
        soften(bias_ref[tile], bufs[k % 2])
        if k + 1 < len(items):
            do_score(k + 1)
    do_grads(len(items) - 1)


def store_all(*refs):
    def store(lanes, *values):
        for ref, value in zip(refs, values):
            ref[:, lanes] = value

    return store


def first_kernel(
    got_a, own_a, own_b, wk_ref, wv_ref, q_ref, da_ref, bias_ref,
    half_ref, k_ref, v_ref, att_ref, dq_ref, dk_ref, dv_ref, wkt_ref, wvt_ref, *scratch,
):
    upper = is_odd("lat")
    top = jnp.where(upper, got_a[...], own_b[...])
    bottom = jnp.where(upper, own_b[...], got_a[...])
    rows = jnp.concatenate([top, own_a[...], bottom], axis=0)
    pick = select(NODES, to_blocks(12))
    for j in range(0, half_ref.shape[-1], WIDE):
        lanes = slice(j, j + WIDE)
        half_ref[:, lanes] = mm(pick, rows[:, lanes], NN).astype(BF)
    for j in range(0, half_ref.shape[-1], WIDE):
        lanes = slice(j, j + WIDE)
        k_ref[:, lanes] = mm(half_ref[...], wk_ref[:, lanes], NN).astype(BF)
        v_ref[:, lanes] = mm(half_ref[...], wv_ref[:, lanes], NN).astype(BF)
        for i in range(0, half_ref.shape[-1], WIDE):
            rows = slice(i, i + WIDE)
            wkt_ref[lanes, rows] = wk_ref[rows, lanes].T
            wvt_ref[lanes, rows] = wv_ref[rows, lanes].T

    def load(lanes):
        return k_ref[:, lanes], v_ref[:, lanes]

    tile = jnp.where(upper, 1, 2)
    store = store_all(att_ref, dq_ref, dk_ref, dv_ref)
    attend(tile, load, store, q_ref, da_ref, bias_ref, scratch)


def edge_tile(left, k_ref, v_ref, kr, vr, outs, q_ref, da_ref, bias_ref, scratch):
    att_ref, dq_ref, dk_ref, dv_ref, dkr, dvr = outs
    start = pl.multiple_of(jnp.where(left, 0, 2 * BLOCK), 2 * BLOCK)

    def load(lanes):
        def one(rim, mid):
            return jnp.concatenate([rim[:, lanes], mid[pl.ds(start, 2 * BLOCK), lanes]], axis=0)

        return one(kr, k_ref), one(vr, v_ref)

    def store(lanes, att, dq, dk, dv):
        att_ref[:, lanes] = att
        dq_ref[:, lanes] = dq
        for grad, rim, out in ((dk, dkr, dk_ref), (dv, dvr, dv_ref)):
            rim[:, lanes] = (grad[:BLOCK] * (1.0 / SCALE)).astype(BF)
            out[:, lanes] = grad[BLOCK:]

    attend(jnp.where(left, 0, 3), load, store, q_ref, da_ref, bias_ref, scratch)


def near_kernel(
    got_a, rest_ref, kh_ref, vh_ref, wk_ref, wv_ref, q_ref, da_ref, bias_ref,
    k_ref, v_ref, att_ref, dq_ref, dk_ref, dv_ref, dkr, dvr,
    kr, vr, *scratch,
):
    rows = jnp.concatenate([got_a[...], rest_ref[...]], axis=0)
    first = is_odd("lat")
    for rim, mid, half, w in ((kr, k_ref, kh_ref, wk_ref), (vr, v_ref, vh_ref, wv_ref)):
        for j in range(0, rows.shape[-1], WIDE):
            lanes = slice(j, j + WIDE)
            made = mm(rows, w[:, lanes], NN).astype(BF)
            rim[:, lanes] = made[:BLOCK]
            for i in range(4):
                most = half[i * HALF : (i + 1) * HALF, lanes]
                few = made[BLOCK + i * HALO : BLOCK + (i + 1) * HALO]
                mid[i * BLOCK : (i + 1) * BLOCK, lanes] = jnp.where(
                    first,
                    jnp.concatenate([most, few], axis=0),
                    jnp.concatenate([few, most], axis=0),
                )
    outs = (att_ref, dq_ref, dk_ref, dv_ref, dkr, dvr)
    edge_tile(is_odd("lon"), k_ref, v_ref, kr, vr, outs, q_ref, da_ref, bias_ref, scratch)


def far_kernel(
    got_b, k_ref, v_ref, wk_ref, wv_ref, q_ref, da_ref, bias_ref, near_dkr, near_dvr,
    wkt_ref, wvt_ref,
    att_ref, dq_ref, dk_ref, dv_ref, send_a, send_b,
    kr, vr, dkr, dvr, *scratch,
):
    for j in range(0, kr.shape[-1], WIDE):
        lanes = slice(j, j + WIDE)
        kr[:, lanes] = mm(got_b[...], wk_ref[:, lanes], NN).astype(BF)
        vr[:, lanes] = mm(got_b[...], wv_ref[:, lanes], NN).astype(BF)
    outs = (att_ref, dq_ref, dk_ref, dv_ref, dkr, dvr)
    left = lax.axis_index("lon") % 2 == 0
    edge_tile(left, k_ref, v_ref, kr, vr, outs, q_ref, da_ref, bias_ref, scratch)
    dk = jnp.concatenate([near_dkr[...], dkr[...]], axis=0)
    dv = jnp.concatenate([near_dvr[...], dvr[...]], axis=0)
    for j in range(0, kr.shape[-1], WIDE):
        lanes = slice(j, j + WIDE)
        part = mm(dk, wkt_ref[:, lanes], NN) + mm(dv, wvt_ref[:, lanes], NN)
        send_a[:, lanes] = part[:BLOCK].astype(BF)
        send_b[:, lanes] = part[BLOCK:].astype(BF)


def last_kernel(
    k_ref, v_ref, wkt_ref, wvt_ref, q_ref, da_ref, bias_ref,
    dkh_ref, dvh_ref, dkn_ref, dvn_ref, dkf_ref, dvf_ref,
    att_ref, dq_ref, part_ref, dko_ref, dvo_ref,
    dkr, dvr, *scratch,
):
    upper_done = is_odd("lat")
    offset = jnp.where(upper_done, HALO, 0)

    def load(lanes):
        def one(ref):
            starts = [pl.multiple_of(i * BLOCK + offset, HALO) for i in range(4)]
            return jnp.concatenate([ref[pl.ds(at, HALF), lanes] for at in starts], axis=0)

        return one(k_ref), one(v_ref)

    def store(lanes, att, dq, dk, dv):
        att_ref[:, lanes] = att
        dq_ref[:, lanes] = dq
        for grad, half, near, far, rims, own in (
            (dk, dkh_ref, dkn_ref, dkf_ref, dkr, dko_ref),
            (dv, dvh_ref, dvn_ref, dvf_ref, dvr, dvo_ref),
        ):
            sides = sort_pair("lon", near[:, lanes], far[:, lanes])
            for i in range(4):
                edge = sides[i // 2][(i % 2) * BLOCK : (i % 2 + 1) * BLOCK]
                a = half[i * HALF : (i + 1) * HALF, lanes]
                b = grad[i * HALF : (i + 1) * HALF]
                up = jnp.where(upper_done, a, b)
                down = jnp.where(upper_done, b, a)
                low = edge[:HALO] + up[:HALO]
                mine = edge[HALO:HALF] + up[HALO:] + down[: HALF - HALO]
                high = edge[HALF:] + down[HALF - HALO :]
                low, mine, high = ((x * (1.0 / SCALE)).astype(BF) for x in (low, mine, high))
                rims[i * HALO : (i + 1) * HALO, lanes] = low
                rims[BLOCK + i * HALO : BLOCK + (i + 1) * HALO, lanes] = high
                own[i * 2 * HALO : (i + 1) * 2 * HALO, lanes] = mine

    attend(jnp.where(upper_done, 2, 1), load, store, q_ref, da_ref, bias_ref, scratch)
    for j in range(0, part_ref.shape[-1], WIDE):
        lanes = slice(j, j + WIDE)
        part_ref[:, lanes] = mm(dkr[...], wkt_ref[:, lanes], NN) + mm(dvr[...], wvt_ref[:, lanes], NN)


def merge_kernel(part_ref, got_a, got_b, send_a, send_b):
    left, right = (x.astype(F32) for x in sort_pair("lon", got_a[...], got_b[...]))
    sides = []
    for i, rows in enumerate((slice(0, HALO), slice(HALF, BLOCK))):
        part = part_ref[i * BLOCK : (i + 1) * BLOCK]
        parts = [part[:HALO] + left[rows], part[HALO:HALF], part[HALF:] + right[rows]]
        sides.append(jnp.concatenate(parts, axis=0).astype(BF))
    send_a[...], send_b[...] = sort_pair("lat", *sides)


def emit(res_ref, tiles, w_ref, dims, out_hbm, out_scr, sem):
    first, near, far, last = (ref[...] for ref in tiles)
    rows = jnp.concatenate(
        [*sort_pair("lon", near, far)[:1], *sort_pair("lat", first, last), sort_pair("lon", near, far)[1]],
        axis=0,
    )
    copies = []
    for i, j in enumerate(range(0, out_scr.shape[-1], 256)):
        lanes = slice(j, j + 256)
        w = w_ref[:, lanes] if dims is NN else w_ref[lanes, :]
        product = mm(rows, w, dims)
        tiles = [product[t * POINTS : (t + 1) * POINTS] for t in range(TILES)]
        out_scr[:, lanes] = (res_ref[:, lanes].astype(F32) + from_tiles(tiles)).astype(BF)
        copy = pltpu.make_async_copy(out_scr.at[:, lanes], out_hbm.at[:, lanes], sem.at[i])
        copy.start()
        copies.append(copy)
    return copies


def layer_out_kernel(x_ref, first, near, far, last, wo_ref, out_hbm, out_scr, sem):
    for copy in emit(x_ref, (first, near, far, last), wo_ref, NN, out_hbm, out_scr, sem):
        copy.wait()


def grid_grad_kernel(
    c_ref, first, near, far, last, wq_ref, dk_ref, dv_ref, wkt_ref, wvt_ref, got_a, got_b,
    grad_hbm, own_ref, out_scr, sem,
):
    copies = emit(c_ref, (first, near, far, last), wq_ref, NT, grad_hbm, out_scr, sem)
    left, right = (x.astype(F32)[HALO:HALF] for x in sort_pair("lon", got_a[...], got_b[...]))
    none = jnp.zeros((BLOCK, WIDE), F32)
    for j in range(0, own_ref.shape[-1], WIDE):
        lanes = slice(j, j + WIDE)
        rims = jnp.concatenate([left[:, lanes], none, right[:, lanes]], axis=0)
        own_ref[:, lanes] = (
            mm(dk_ref[...], wkt_ref[:, lanes], NN) + mm(dv_ref[...], wvt_ref[:, lanes], NN) + rims
        )
    for copy in copies:
        copy.wait()


def finish_kernel(own_ref, got_a, got_b, out_hbm, out_scr, sem):
    sides = [x.astype(F32) for x in sort_pair("lat", got_a[...], got_b[...])]
    parts = [side[i * HALO : (i + 1) * HALO] for i in range(4) for side in sides]
    total = (own_ref[...] + jnp.concatenate(parts, axis=0)).astype(BF)
    dst = lax.broadcasted_iota(jnp.int32, (2 * BLOCK, 2 * BLOCK), 0)
    src = lax.broadcasted_iota(jnp.int32, (2 * BLOCK, 2 * BLOCK), 1)
    pick = jnp.where(src == to_blocks(8)(dst), 1.0, 0.0).astype(BF)
    copies = []
    for i, j in enumerate(range(0, out_scr.shape[-1], 256)):
        lanes = slice(j, j + 256)
        out_scr[:, lanes] = mm(pick, total[:, lanes], NN).astype(BF)
        copy = pltpu.make_async_copy(out_scr.at[:, lanes], out_hbm.at[:, lanes], sem.at[i])
        copy.start()
        copies.append(copy)
    for copy in copies:
        copy.wait()


def pairs_of(axis):
    count = lax.axis_size(axis)
    even = [(i, i + 1) for i in range(0, count, 2)]
    odd = [(i, (i + 1) % count) for i in range(1, count, 2)]
    return [pairs + [(b, a) for a, b in pairs] for pairs in (even, odd)]


def local(grid_feat, mesh_feat, edges, edge_mask, w_query, w_key, w_value, w_out, cotangent):
    width = grid_feat.shape[-1]
    points = TILES * POINTS
    x = grid_feat.reshape(points, width)
    c = cotangent.reshape(points, width)
    own = mesh_feat.reshape(2 * BLOCK, width)
    product = 2 * width * width
    lat_a, lat_b = pairs_of("lat")
    lon_a, lon_b = pairs_of("lon")
    piece = ((BLOCK, width), BF)
    tiled = ((TILES, POINTS, width), BF)
    square = ((width, width), BF)

    send_a, send_b = call(
        lead_kernel, (own,), [piece, piece], 10**5,
        (pltpu.SemaphoreType.DMA((2,)),), hbm=(0,),
    )
    got_a = lax.ppermute(send_a, "lat", lat_a)
    got_b = lax.ppermute(send_b, "lat", lat_b)
    q, da, bias, wk, wv = call(
        project_kernel,
        (edges, edge_mask, x, w_query, c, w_out, w_key, w_value),
        [tiled, tiled, ((TILES, NODES, POINTS), F32), square, square],
        2 * points * product,
        (pltpu.VMEM(edges.shape, jnp.int32),) * 2
        + (pltpu.VMEM((points, width), BF), pltpu.VMEM((width, width), BF)) * 2
        + (pltpu.SemaphoreType.DMA((8,)),),
        hbm=tuple(range(8)),
    )
    common = (wk, wv, q, da, bias)
    rows = ((POINTS, width), BF)
    half, half_grad = ((NODES, width), BF), ((NODES, width), F32)
    mid, mid_grad = ((MIDDLE, width), BF), ((2 * BLOCK, width), F32)
    half_rows, kh, vh, att_first, dq_first, dkh, dvh, wkt, wvt = call(
        first_kernel, (got_a, send_a, send_b, *common),
        [half] * 3 + [rows] * 2 + [half_grad] * 2 + [square] * 2,
        4 * 10**9, PAIR_SCRATCH,
    )
    rest, edge_a, edge_b = call(assemble_kernel, (half_rows, got_b), [piece] * 3, 10**8)
    edge_a = lax.ppermute(edge_a, "lon", lon_a)
    edge_b = lax.ppermute(edge_b, "lon", lon_b)
    k, v, att_near, dq_near, dkn, dvn, rim_dk, rim_dv = call(
        near_kernel, (edge_a, rest, kh, vh, *common),
        [mid] * 2 + [rows] * 2 + [mid_grad] * 2 + [piece] * 2,
        4 * 10**9, (pltpu.VMEM((BLOCK, width), BF),) * 2 + PAIR_SCRATCH,
    )
    att_far, dq_far, dkf, dvf, edge_a, edge_b = call(
        far_kernel, (edge_b, k, v, *common, rim_dk, rim_dv, wkt, wvt),
        [rows] * 2 + [mid_grad] * 2 + [piece] * 2,
        4 * 10**9, (pltpu.VMEM((BLOCK, width), BF),) * 4 + PAIR_SCRATCH,
    )
    edge_a = lax.ppermute(edge_a, "lon", lon_a)
    edge_b = lax.ppermute(edge_b, "lon", lon_b)
    att_last, dq_last, part, dk_own, dv_own = call(
        last_kernel, (k, v, wkt, wvt, q, da, bias, dkh, dvh, dkn, dvn, dkf, dvf),
        [rows] * 2 + [mid_grad] + [((2 * BLOCK, width), BF)] * 2,
        4 * 10**9, (pltpu.VMEM((2 * BLOCK, width), BF),) * 2 + PAIR_SCRATCH,
    )
    send_a, send_b = call(merge_kernel, (part, edge_a, edge_b), [piece, piece], 10**8)
    got_a = lax.ppermute(send_a, "lat", lat_a)
    out_scratch = (pltpu.VMEM((points, width), BF), pltpu.SemaphoreType.DMA((4,)))
    got_b = lax.ppermute(send_b, "lat", lat_b)
    (layer_out,) = call(
        layer_out_kernel, (x, att_first, att_near, att_far, att_last, w_out),
        [((points, width), BF)],
        points * product, out_scratch, hbm_out=(0,),
    )
    grid_grad, kept = call(
        grid_grad_kernel,
        (c, dq_first, dq_near, dq_far, dq_last, w_query, dk_own, dv_own, wkt, wvt, edge_a, edge_b),
        [((points, width), BF), ((2 * BLOCK, width), F32)],
        points * product, out_scratch, hbm_out=(0,),
    )
    (mesh_grad,) = call(
        finish_kernel, (kept, got_a, got_b), [((2 * BLOCK, width), BF)], 10**6,
        (pltpu.VMEM((2 * BLOCK, width), BF), pltpu.SemaphoreType.DMA((4,))), hbm_out=(0,),
    )
    return (
        layer_out.reshape(grid_feat.shape),
        grid_grad.reshape(grid_feat.shape),
        mesh_grad.reshape(mesh_feat.shape),
    )


def solution(mesh):
    tiled = P("lat", "lon", None)
    placed = (tiled, tiled, P(None, "lat", "lon"), P(None, "lat", "lon")) + (P(),) * 4 + (tiled,)
    return jax.shard_map(
        local, mesh=mesh, in_specs=placed, out_specs=(tiled, tiled, tiled), check_vma=False
    )
```

```python
import jax
import jax.numpy as jnp
from jax import lax
from jax.experimental import pallas as pl
from jax.experimental.pallas import tpu as pltpu
from jax.sharding import PartitionSpec as P


HEADS = 16
HEAD = 64
SLOTS = 12
REACH = 4
NEG_FILL = -1e30
SCALE = 0.125
GROUP = 4
WIDE = GROUP * HEAD

TILES = 4
POINTS = 128
BLOCK = 64
NODES = 3 * BLOCK
MIDDLE = 4 * BLOCK
HALO = 16
HALF = 48

BF = jnp.bfloat16
F32 = jnp.float32
NT = (((1,), (1,)), ((), ()))
NN = (((1,), (0,)), ((), ()))
TN = (((0,), (0,)), ((), ()))
IN_VMEM = pl.BlockSpec(memory_space=pltpu.VMEM)
IN_HBM = pl.BlockSpec(memory_space=pltpu.MemorySpace.HBM)
IN_PLACE = pl.BlockSpec(memory_space=pl.ANY)


def mm(a, b, dims):
    return lax.dot_general(a, b, dims, preferred_element_type=F32)


def call(kernel, inputs, outs, flops, scratch=(), hbm=(), loose=(), hbm_out=(), limit=16 << 20):
    moved = sum(a.size * a.dtype.itemsize for a in inputs)

    def placed(i):
        return IN_HBM if i in hbm else IN_PLACE if i in loose else IN_VMEM

    return pl.pallas_call(
        kernel,
        in_specs=[placed(i) for i in range(len(inputs))],
        out_specs=[IN_HBM if i in hbm_out else IN_VMEM for i in range(len(outs))],
        out_shape=[
            jax.ShapeDtypeStruct(s, d) if i in hbm_out else pltpu.VMEM(s, d)
            for i, (s, d) in enumerate(outs)
        ],
        scratch_shapes=list(scratch),
        compiler_params=pltpu.CompilerParams(vmem_limit_bytes=limit),
        cost_estimate=pl.CostEstimate(flops=flops, bytes_accessed=moved, transcendentals=0),
    )(
        *(
            pltpu.with_memory_space_constraint(a, pltpu.MemorySpace.HBM) if i in hbm else a
            for i, a in enumerate(inputs)
        )
    )


def to_tiles(rows):
    cut = rows.reshape(16, TILES, 8, rows.shape[-1])
    parts = (cut[:, 0], cut[:8, 1:3], cut[8:, 1:3], cut[:, 3])
    return [part.reshape(POINTS, rows.shape[-1]) for part in parts]


def from_tiles(tiles):
    n = tiles[0].shape[-1]
    upper, lower = (t.reshape(8, 2, 8, n) for t in tiles[1:3])
    left, right = (t.reshape(16, 1, 8, n) for t in (tiles[0], tiles[3]))
    middle = jnp.concatenate([upper, lower], axis=0)
    return jnp.concatenate([left, middle, right], axis=1).reshape(TILES * POINTS, n)


def select(count, dst_of_src):
    dst = lax.broadcasted_iota(jnp.int32, (count, count), 0)
    src = lax.broadcasted_iota(jnp.int32, (count, count), 1)
    return jnp.where(dst == dst_of_src(src), 1.0, 0.0).astype(BF)


def to_blocks(rows):
    return lambda i: ((i % 16) // 4) * (4 * rows) + (i // 16) * 4 + i % 4


def is_odd(axis):
    return lax.axis_index(axis) % 2 == 1


def lead_kernel(mesh_ref, a_ref, b_ref, sem):
    odd = lax.axis_index("lat") % 2
    first = pltpu.make_async_copy(mesh_ref.at[pl.ds((1 - odd) * BLOCK, BLOCK)], a_ref, sem.at[0])
    second = pltpu.make_async_copy(mesh_ref.at[pl.ds(odd * BLOCK, BLOCK)], b_ref, sem.at[1])
    first.start()
    second.start()
    first.wait()
    second.wait()


def project_kernel(
    edges_hbm, mask_hbm, x_hbm, wq_hbm, c_hbm, wo_hbm, wk_hbm, wv_hbm,
    q_ref, da_ref, bias_ref, wk_ref, wv_ref,
    edges_scr, mask_scr, x_scr, wq_scr, c_scr, wo_scr, sem,
):
    pairs = (
        (edges_hbm, edges_scr), (mask_hbm, mask_scr), (x_hbm, x_scr), (wq_hbm, wq_scr),
        (c_hbm, c_scr), (wo_hbm, wo_scr), (wk_hbm, wk_ref), (wv_hbm, wv_ref),
    )
    copies = [pltpu.make_async_copy(a, b, sem.at[i]) for i, (a, b) in enumerate(pairs)]
    for copy in copies:
        copy.start()
    copies[0].wait()
    copies[1].wait()
    make_bias(edges_scr, mask_scr, bias_ref)
    for first, out_ref, project in (
        (2, q_ref, lambda lanes: mm(x_scr[...], wq_scr[:, lanes], NN)),
        (4, da_ref, lambda lanes: mm(c_scr[...], wo_scr[lanes, :], NT)),
    ):
        copies[first].wait()
        copies[first + 1].wait()
        for j in range(0, q_ref.shape[-1], 256):
            lanes = slice(j, j + 256)
            for t, rows in enumerate(to_tiles(project(lanes))):
                out_ref[t, :, lanes] = rows.astype(BF) * SCALE
    copies[6].wait()
    copies[7].wait()


def make_bias(edges_ref, mask_ref, bias_ref):
    lat_start = lax.axis_index("lat") * 8
    lon_start = lax.axis_index("lon") * 16
    edges = edges_ref[...]
    row = (edges >> 10) - lat_start + REACH
    col = (edges - lon_start + REACH) & 1023
    point_row = lax.broadcasted_iota(jnp.int32, edges.shape, 1)
    point_col = lax.broadcasted_iota(jnp.int32, edges.shape, 2)
    block, inner = col >> 2, row * 4 + (col & 3)
    slot = jnp.where(
        point_col < 8,
        block * BLOCK + inner,
        jnp.where(
            point_col >= 24,
            jnp.where(block == 5, 0, block - 2) * BLOCK + inner,
            (block - 1) * HALF + inner - jnp.where(point_row < 8, 0, HALO),
        ),
    )
    slot = jnp.where(mask_ref[...] > 0, slot, -1).astype(F32).astype(BF)
    slot = slot.reshape(SLOTS * 16, 32)

    def point(lane):
        tile, i = lane >> 7, lane & 127
        outer = (tile == 0) | (tile == 3)
        row = jnp.where(outer, i >> 3, (i >> 4) + jnp.where(tile == 2, 8, 0))
        col = jnp.where(outer, (i & 7) + tile * 8, (i & 15) + 8)
        return row, col

    src = lax.broadcasted_iota(jnp.int32, (32, TILES * POINTS), 0)
    dst = lax.broadcasted_iota(jnp.int32, (32, TILES * POINTS), 1)
    pick = jnp.where(src == point(dst)[1], 1.0, 0.0).astype(BF)
    wide = mm(slot, pick, NN).reshape(SLOTS, 16, TILES * POINTS)
    lane = lax.broadcasted_iota(jnp.int32, (16, TILES * POINTS), 1)
    own_row = lax.broadcasted_iota(jnp.int32, lane.shape, 0) == point(lane)[0]
    slots = jnp.sum(jnp.where(own_row[None], wide, 0.0), axis=1)
    node = lax.broadcasted_iota(jnp.int32, (NODES, POINTS), 0).astype(F32)
    for t in range(TILES):
        at = slice(t * POINTS, (t + 1) * POINTS)
        hit = node == slots[0:1, at]
        for e in range(1, SLOTS):
            hit = hit | (node == slots[e : e + 1, at])
        bias_ref[t] = jnp.where(hit, 0.0, NEG_FILL)


def sort_pair(axis, a, b):
    odd = lax.axis_index(axis) % 2 == 1
    return jnp.where(odd, a, b), jnp.where(odd, b, a)


def assemble_kernel(got_a, got_b, own_a, own_b, half_ref, rest_ref, send_a, send_b):
    first = is_odd("lat")
    top = jnp.where(first, got_a[...], own_b[...])
    bottom = jnp.where(first, own_b[...], got_a[...])
    rows = jnp.concatenate([top, own_a[...], bottom], axis=0)
    pick_most, pick_few = select(NODES, to_blocks(12)), select(BLOCK, to_blocks(4))
    for j in range(0, rest_ref.shape[-1], WIDE):
        lanes = slice(j, j + WIDE)
        half = mm(pick_most, rows[:, lanes], NN).astype(BF)
        rest = mm(pick_few, got_b[:, lanes], NN).astype(BF)
        half_ref[:, lanes] = half
        rest_ref[:, lanes] = rest

        def column(i):
            most = half[i * HALF : (i + 1) * HALF]
            few = rest[i * HALO : (i + 1) * HALO]
            return jnp.where(
                first, jnp.concatenate([most, few], axis=0), jnp.concatenate([few, most], axis=0)
            )

        send_a[:, lanes], send_b[:, lanes] = sort_pair("lon", column(0), column(3))


def half_masks():
    head = lax.broadcasted_iota(jnp.int32, (1, 2 * HEAD), 1) // HEAD
    return [jnp.where(head == h, 1.0, 0.0).astype(BF) for h in range(2)]


def spread_pair(block):
    return jnp.concatenate([block * m for m in half_masks()], axis=0)


def spread_group(block):
    zero = jnp.zeros((block.shape[0], 2 * HEAD), BF)
    low, high = block[:, : 2 * HEAD], block[:, 2 * HEAD :]
    masks = half_masks()
    rows = [jnp.concatenate([low * m, zero], axis=1) for m in masks]
    rows += [jnp.concatenate([zero, high * m], axis=1) for m in masks]
    return jnp.concatenate(rows, axis=0)


def pair_lanes(i):
    return slice(i * 2 * HEAD, (i + 1) * 2 * HEAD), slice(i * 2 * POINTS, (i + 1) * 2 * POINTS)


def score(keys, values, q4, d4, bufs):
    s_ref, d_ref, qs_ref, gs_ref = bufs[:4]
    for i in range(GROUP // 2):
        lanes, at = pair_lanes(i)
        qs_ref[at, :] = spread_pair(q4[:, lanes])
        gs_ref[at, :] = spread_pair(d4[:, lanes])
        s_ref[:, at] = mm(keys[:, lanes], qs_ref[at, :], NT)
        d_ref[:, at] = mm(values[:, lanes], gs_ref[at, :], NT)


def soften(bias, bufs):
    s_ref, d_ref, _, _, pw, sw, pt, st = bufs
    for h in range(GROUP):
        at = slice(h * POINTS, (h + 1) * POINTS)
        tall = slice(h * NODES, (h + 1) * NODES)
        top = jnp.max(s_ref[:, at] + bias, axis=0, keepdims=True)
        e = jnp.exp(s_ref[:, at] + bias - top)
        s_ref[:, at] = e
        inverse = 1.0 / jnp.sum(e, axis=0, keepdims=True)
        centred = jnp.sum(e * d_ref[:, at], axis=0, keepdims=True) * inverse
        p = s_ref[:, at] * inverse
        half = p.astype(BF)
        ds = (p * (d_ref[:, at] - centred)).astype(BF)
        pw[:, at] = half
        sw[:, at] = ds
        pt[tall, :] = half
        st[tall, :] = ds


def gather_grads(keys, values, bufs):
    _, _, qs_ref, gs_ref, pw, sw, pt, st = bufs
    att = mm(pt[...], spread_group(values), TN).astype(BF)
    dq = mm(st[...], spread_group(keys), TN).astype(BF)
    dk, dv = [], []
    for i in range(GROUP // 2):
        _, at = pair_lanes(i)
        dk.append(mm(sw[:, at], qs_ref[at, :], NN))
        dv.append(mm(pw[:, at], gs_ref[at, :], NN))
    return att, dq, jnp.concatenate(dk, axis=1), jnp.concatenate(dv, axis=1)


ITEM_SCRATCH = (
    (pltpu.VMEM((NODES, GROUP * POINTS), F32),) * 2
    + (pltpu.VMEM((GROUP * POINTS, 2 * HEAD), BF),) * 2
    + (pltpu.VMEM((NODES, GROUP * POINTS), BF),) * 2
    + (pltpu.VMEM((GROUP * NODES, POINTS), BF),) * 2
)
PAIR_SCRATCH = ITEM_SCRATCH * 2


def attend(tile, load, store, q_ref, da_ref, bias_ref, scratch):
    n = len(ITEM_SCRATCH)
    bufs = (scratch[:n], scratch[n:])
    items = [slice(j, j + WIDE) for j in range(0, HEADS * HEAD, WIDE)]

    def do_score(k):
        lanes = items[k]
        score(*load(lanes), q_ref[tile, :, lanes], da_ref[tile, :, lanes], bufs[k % 2])

    def do_grads(k):
        store(items[k], *gather_grads(*load(items[k]), bufs[k % 2]))

    do_score(0)
    for k in range(len(items)):
        if k > 0:
            do_grads(k - 1)
        soften(bias_ref[tile], bufs[k % 2])
        if k + 1 < len(items):
            do_score(k + 1)
    do_grads(len(items) - 1)


def store_all(*refs):
    def store(lanes, *values):
        for ref, value in zip(refs, values):
            ref[:, lanes] = value

    return store


def first_kernel(
    half_ref, wk_ref, wv_ref, q_ref, da_ref, bias_ref,
    k_ref, v_ref, att_ref, dq_ref, dk_ref, dv_ref, wkt_ref, wvt_ref, *scratch,
):
    for j in range(0, half_ref.shape[-1], WIDE):
        lanes = slice(j, j + WIDE)
        k_ref[:, lanes] = mm(half_ref[...], wk_ref[:, lanes], NN).astype(BF)
        v_ref[:, lanes] = mm(half_ref[...], wv_ref[:, lanes], NN).astype(BF)
        for i in range(0, half_ref.shape[-1], WIDE):
            rows = slice(i, i + WIDE)
            wkt_ref[lanes, rows] = wk_ref[rows, lanes].T
            wvt_ref[lanes, rows] = wv_ref[rows, lanes].T

    def load(lanes):
        return k_ref[:, lanes], v_ref[:, lanes]

    tile = jnp.where(is_odd("lat"), 1, 2)
    store = store_all(att_ref, dq_ref, dk_ref, dv_ref)
    attend(tile, load, store, q_ref, da_ref, bias_ref, scratch)


def edge_tile(left, k_ref, v_ref, kr, vr, outs, q_ref, da_ref, bias_ref, scratch):
    att_ref, dq_ref, dk_ref, dv_ref, dkr, dvr = outs
    start = pl.multiple_of(jnp.where(left, 0, 2 * BLOCK), 2 * BLOCK)

    def load(lanes):
        def one(rim, mid):
            return jnp.concatenate([rim[:, lanes], mid[pl.ds(start, 2 * BLOCK), lanes]], axis=0)

        return one(kr, k_ref), one(vr, v_ref)

    def store(lanes, att, dq, dk, dv):
        att_ref[:, lanes] = att
        dq_ref[:, lanes] = dq
        for grad, rim, out in ((dk, dkr, dk_ref), (dv, dvr, dv_ref)):
            rim[:, lanes] = (grad[:BLOCK] * (1.0 / SCALE)).astype(BF)
            out[:, lanes] = grad[BLOCK:]

    attend(jnp.where(left, 0, 3), load, store, q_ref, da_ref, bias_ref, scratch)


def near_kernel(
    got_a, rest_ref, kh_ref, vh_ref, wk_ref, wv_ref, q_ref, da_ref, bias_ref,
    k_ref, v_ref, att_ref, dq_ref, dk_ref, dv_ref, dkr, dvr,
    kr, vr, *scratch,
):
    rows = jnp.concatenate([got_a[...], rest_ref[...]], axis=0)
    first = is_odd("lat")
    for rim, mid, half, w in ((kr, k_ref, kh_ref, wk_ref), (vr, v_ref, vh_ref, wv_ref)):
        for j in range(0, rows.shape[-1], WIDE):
            lanes = slice(j, j + WIDE)
            made = mm(rows, w[:, lanes], NN).astype(BF)
            rim[:, lanes] = made[:BLOCK]
            for i in range(4):
                most = half[i * HALF : (i + 1) * HALF, lanes]
                few = made[BLOCK + i * HALO : BLOCK + (i + 1) * HALO]
                mid[i * BLOCK : (i + 1) * BLOCK, lanes] = jnp.where(
                    first,
                    jnp.concatenate([most, few], axis=0),
                    jnp.concatenate([few, most], axis=0),
                )
    outs = (att_ref, dq_ref, dk_ref, dv_ref, dkr, dvr)
    edge_tile(is_odd("lon"), k_ref, v_ref, kr, vr, outs, q_ref, da_ref, bias_ref, scratch)


def far_kernel(
    got_b, k_ref, v_ref, wk_ref, wv_ref, q_ref, da_ref, bias_ref, near_dkr, near_dvr,
    wkt_ref, wvt_ref,
    att_ref, dq_ref, dk_ref, dv_ref, send_a, send_b,
    kr, vr, dkr, dvr, *scratch,
):
    for j in range(0, kr.shape[-1], WIDE):
        lanes = slice(j, j + WIDE)
        kr[:, lanes] = mm(got_b[...], wk_ref[:, lanes], NN).astype(BF)
        vr[:, lanes] = mm(got_b[...], wv_ref[:, lanes], NN).astype(BF)
    outs = (att_ref, dq_ref, dk_ref, dv_ref, dkr, dvr)
    left = lax.axis_index("lon") % 2 == 0
    edge_tile(left, k_ref, v_ref, kr, vr, outs, q_ref, da_ref, bias_ref, scratch)
    dk = jnp.concatenate([near_dkr[...], dkr[...]], axis=0)
    dv = jnp.concatenate([near_dvr[...], dvr[...]], axis=0)
    for j in range(0, kr.shape[-1], WIDE):
        lanes = slice(j, j + WIDE)
        part = mm(dk, wkt_ref[:, lanes], NN) + mm(dv, wvt_ref[:, lanes], NN)
        send_a[:, lanes] = part[:BLOCK].astype(BF)
        send_b[:, lanes] = part[BLOCK:].astype(BF)


def last_kernel(
    k_ref, v_ref, wkt_ref, wvt_ref, q_ref, da_ref, bias_ref,
    dkh_ref, dvh_ref, dkn_ref, dvn_ref, dkf_ref, dvf_ref,
    att_ref, dq_ref, part_ref, dko_ref, dvo_ref,
    dkr, dvr, *scratch,
):
    upper_done = is_odd("lat")
    offset = jnp.where(upper_done, HALO, 0)

    def load(lanes):
        def one(ref):
            starts = [pl.multiple_of(i * BLOCK + offset, HALO) for i in range(4)]
            return jnp.concatenate([ref[pl.ds(at, HALF), lanes] for at in starts], axis=0)

        return one(k_ref), one(v_ref)

    def store(lanes, att, dq, dk, dv):
        att_ref[:, lanes] = att
        dq_ref[:, lanes] = dq
        for grad, half, near, far, rims, own in (
            (dk, dkh_ref, dkn_ref, dkf_ref, dkr, dko_ref),
            (dv, dvh_ref, dvn_ref, dvf_ref, dvr, dvo_ref),
        ):
            sides = sort_pair("lon", near[:, lanes], far[:, lanes])
            for i in range(4):
                edge = sides[i // 2][(i % 2) * BLOCK : (i % 2 + 1) * BLOCK]
                a = half[i * HALF : (i + 1) * HALF, lanes]
                b = grad[i * HALF : (i + 1) * HALF]
                up = jnp.where(upper_done, a, b)
                down = jnp.where(upper_done, b, a)
                low = edge[:HALO] + up[:HALO]
                mine = edge[HALO:HALF] + up[HALO:] + down[: HALF - HALO]
                high = edge[HALF:] + down[HALF - HALO :]
                low, mine, high = ((x * (1.0 / SCALE)).astype(BF) for x in (low, mine, high))
                rims[i * HALO : (i + 1) * HALO, lanes] = low
                rims[BLOCK + i * HALO : BLOCK + (i + 1) * HALO, lanes] = high
                own[i * 2 * HALO : (i + 1) * 2 * HALO, lanes] = mine

    attend(jnp.where(upper_done, 2, 1), load, store, q_ref, da_ref, bias_ref, scratch)
    for j in range(0, part_ref.shape[-1], WIDE):
        lanes = slice(j, j + WIDE)
        part_ref[:, lanes] = mm(dkr[...], wkt_ref[:, lanes], NN) + mm(dvr[...], wvt_ref[:, lanes], NN)


def merge_kernel(part_ref, got_a, got_b, send_a, send_b):
    left, right = (x.astype(F32) for x in sort_pair("lon", got_a[...], got_b[...]))
    sides = []
    for i, rows in enumerate((slice(0, HALO), slice(HALF, BLOCK))):
        part = part_ref[i * BLOCK : (i + 1) * BLOCK]
        parts = [part[:HALO] + left[rows], part[HALO:HALF], part[HALF:] + right[rows]]
        sides.append(jnp.concatenate(parts, axis=0).astype(BF))
    send_a[...], send_b[...] = sort_pair("lat", *sides)


def emit(res_ref, tiles, w_ref, dims, out_hbm, out_scr, sem):
    first, near, far, last = (ref[...] for ref in tiles)
    rows = jnp.concatenate(
        [*sort_pair("lon", near, far)[:1], *sort_pair("lat", first, last), sort_pair("lon", near, far)[1]],
        axis=0,
    )
    copies = []
    for i, j in enumerate(range(0, out_scr.shape[-1], 256)):
        lanes = slice(j, j + 256)
        w = w_ref[:, lanes] if dims is NN else w_ref[lanes, :]
        product = mm(rows, w, dims)
        tiles = [product[t * POINTS : (t + 1) * POINTS] for t in range(TILES)]
        out_scr[:, lanes] = (res_ref[:, lanes].astype(F32) + from_tiles(tiles)).astype(BF)
        copy = pltpu.make_async_copy(out_scr.at[:, lanes], out_hbm.at[:, lanes], sem.at[i])
        copy.start()
        copies.append(copy)
    return copies


def layer_out_kernel(x_ref, first, near, far, last, wo_ref, out_hbm, out_scr, sem):
    for copy in emit(x_ref, (first, near, far, last), wo_ref, NN, out_hbm, out_scr, sem):
        copy.wait()


def grid_grad_kernel(
    c_ref, first, near, far, last, wq_ref, dk_ref, dv_ref, wkt_ref, wvt_ref, got_a, got_b,
    grad_hbm, own_ref, out_scr, sem,
):
    copies = emit(c_ref, (first, near, far, last), wq_ref, NT, grad_hbm, out_scr, sem)
    left, right = (x.astype(F32)[HALO:HALF] for x in sort_pair("lon", got_a[...], got_b[...]))
    none = jnp.zeros((BLOCK, WIDE), F32)
    for j in range(0, own_ref.shape[-1], WIDE):
        lanes = slice(j, j + WIDE)
        rims = jnp.concatenate([left[:, lanes], none, right[:, lanes]], axis=0)
        own_ref[:, lanes] = (
            mm(dk_ref[...], wkt_ref[:, lanes], NN) + mm(dv_ref[...], wvt_ref[:, lanes], NN) + rims
        )
    for copy in copies:
        copy.wait()


def finish_kernel(own_ref, got_a, got_b, out_hbm, out_scr, sem):
    sides = [x.astype(F32) for x in sort_pair("lat", got_a[...], got_b[...])]
    parts = [side[i * HALO : (i + 1) * HALO] for i in range(4) for side in sides]
    total = (own_ref[...] + jnp.concatenate(parts, axis=0)).astype(BF)
    dst = lax.broadcasted_iota(jnp.int32, (2 * BLOCK, 2 * BLOCK), 0)
    src = lax.broadcasted_iota(jnp.int32, (2 * BLOCK, 2 * BLOCK), 1)
    pick = jnp.where(src == to_blocks(8)(dst), 1.0, 0.0).astype(BF)
    copies = []
    for i, j in enumerate(range(0, out_scr.shape[-1], 256)):
        lanes = slice(j, j + 256)
        out_scr[:, lanes] = mm(pick, total[:, lanes], NN).astype(BF)
        copy = pltpu.make_async_copy(out_scr.at[:, lanes], out_hbm.at[:, lanes], sem.at[i])
        copy.start()
        copies.append(copy)
    for copy in copies:
        copy.wait()


def pairs_of(axis):
    count = lax.axis_size(axis)
    even = [(i, i + 1) for i in range(0, count, 2)]
    odd = [(i, (i + 1) % count) for i in range(1, count, 2)]
    return [pairs + [(b, a) for a, b in pairs] for pairs in (even, odd)]


def local(grid_feat, mesh_feat, edges, edge_mask, w_query, w_key, w_value, w_out, cotangent):
    width = grid_feat.shape[-1]
    points = TILES * POINTS
    x = grid_feat.reshape(points, width)
    c = cotangent.reshape(points, width)
    own = mesh_feat.reshape(2 * BLOCK, width)
    product = 2 * width * width
    lat_a, lat_b = pairs_of("lat")
    lon_a, lon_b = pairs_of("lon")
    piece = ((BLOCK, width), BF)
    tiled = ((TILES, POINTS, width), BF)
    square = ((width, width), BF)

    send_a, send_b = call(
        lead_kernel, (own,), [piece, piece], 10**5,
        (pltpu.SemaphoreType.DMA((2,)),), hbm=(0,),
    )
    got_a = lax.ppermute(send_a, "lat", lat_a)
    got_b = lax.ppermute(send_b, "lat", lat_b)
    q, da, bias, wk, wv = call(
        project_kernel,
        (edges, edge_mask, x, w_query, c, w_out, w_key, w_value),
        [tiled, tiled, ((TILES, NODES, POINTS), F32), square, square],
        2 * points * product,
        (pltpu.VMEM(edges.shape, jnp.int32),) * 2
        + (pltpu.VMEM((points, width), BF), pltpu.VMEM((width, width), BF)) * 2
        + (pltpu.SemaphoreType.DMA((8,)),),
        hbm=tuple(range(8)),
    )
    common = (wk, wv, q, da, bias)
    rows = ((POINTS, width), BF)
    half, half_grad = ((NODES, width), BF), ((NODES, width), F32)
    mid, mid_grad = ((MIDDLE, width), BF), ((2 * BLOCK, width), F32)
    half_rows, rest, edge_a, edge_b = call(
        assemble_kernel, (got_a, got_b, send_a, send_b), [half] + [piece] * 3, 10**8
    )
    edge_a = lax.ppermute(edge_a, "lon", lon_a)
    edge_b = lax.ppermute(edge_b, "lon", lon_b)
    kh, vh, att_first, dq_first, dkh, dvh, wkt, wvt = call(
        first_kernel, (half_rows, *common),
        [half] * 2 + [rows] * 2 + [half_grad] * 2 + [square] * 2,
        4 * 10**9, PAIR_SCRATCH,
    )
    k, v, att_near, dq_near, dkn, dvn, rim_dk, rim_dv = call(
        near_kernel, (edge_a, rest, kh, vh, *common),
        [mid] * 2 + [rows] * 2 + [mid_grad] * 2 + [piece] * 2,
        4 * 10**9, (pltpu.VMEM((BLOCK, width), BF),) * 2 + PAIR_SCRATCH,
    )
    att_far, dq_far, dkf, dvf, edge_a, edge_b = call(
        far_kernel, (edge_b, k, v, *common, rim_dk, rim_dv, wkt, wvt),
        [rows] * 2 + [mid_grad] * 2 + [piece] * 2,
        4 * 10**9, (pltpu.VMEM((BLOCK, width), BF),) * 4 + PAIR_SCRATCH,
    )
    edge_a = lax.ppermute(edge_a, "lon", lon_a)
    edge_b = lax.ppermute(edge_b, "lon", lon_b)
    att_last, dq_last, part, dk_own, dv_own = call(
        last_kernel, (k, v, wkt, wvt, q, da, bias, dkh, dvh, dkn, dvn, dkf, dvf),
        [rows] * 2 + [mid_grad] + [((2 * BLOCK, width), BF)] * 2,
        4 * 10**9, (pltpu.VMEM((2 * BLOCK, width), BF),) * 2 + PAIR_SCRATCH,
    )
    send_a, send_b = call(merge_kernel, (part, edge_a, edge_b), [piece, piece], 10**8)
    got_a = lax.ppermute(send_a, "lat", lat_a)
    out_scratch = (pltpu.VMEM((points, width), BF), pltpu.SemaphoreType.DMA((4,)))
    got_b = lax.ppermute(send_b, "lat", lat_b)
    (layer_out,) = call(
        layer_out_kernel, (x, att_first, att_near, att_far, att_last, w_out),
        [((points, width), BF)],
        points * product, out_scratch, hbm_out=(0,),
    )
    grid_grad, kept = call(
        grid_grad_kernel,
        (c, dq_first, dq_near, dq_far, dq_last, w_query, dk_own, dv_own, wkt, wvt, edge_a, edge_b),
        [((points, width), BF), ((2 * BLOCK, width), F32)],
        points * product, out_scratch, hbm_out=(0,),
    )
    (mesh_grad,) = call(
        finish_kernel, (kept, got_a, got_b), [((2 * BLOCK, width), BF)], 10**6,
        (pltpu.VMEM((2 * BLOCK, width), BF), pltpu.SemaphoreType.DMA((4,))), hbm_out=(0,),
    )
    return (
        layer_out.reshape(grid_feat.shape),
        grid_grad.reshape(grid_feat.shape),
        mesh_grad.reshape(mesh_feat.shape),
    )


def solution(mesh):
    tiled = P("lat", "lon", None)
    placed = (tiled, tiled, P(None, "lat", "lon"), P(None, "lat", "lon")) + (P(),) * 4 + (tiled,)
    return jax.shard_map(
        local, mesh=mesh, in_specs=placed, out_specs=(tiled, tiled, tiled), check_vma=False
    )
```

```python
import jax
import jax.numpy as jnp
from jax import lax
from jax.experimental import pallas as pl
from jax.experimental.pallas import tpu as pltpu
from jax.sharding import PartitionSpec as P


HEADS = 16
HEAD = 64
SLOTS = 12
REACH = 4
NEG_FILL = -1e30
SCALE = 0.125
GROUP = 4
WIDE = GROUP * HEAD

TILES = 4
POINTS = 128
BLOCK = 64
NODES = 3 * BLOCK
MIDDLE = 4 * BLOCK
HALO = 16
HALF = 48

BF = jnp.bfloat16
F32 = jnp.float32
NT = (((1,), (1,)), ((), ()))
NN = (((1,), (0,)), ((), ()))
TN = (((0,), (0,)), ((), ()))
IN_VMEM = pl.BlockSpec(memory_space=pltpu.VMEM)
IN_HBM = pl.BlockSpec(memory_space=pltpu.MemorySpace.HBM)
IN_PLACE = pl.BlockSpec(memory_space=pl.ANY)


def mm(a, b, dims):
    return lax.dot_general(a, b, dims, preferred_element_type=F32)


def call(kernel, inputs, outs, flops, scratch=(), hbm=(), loose=(), hbm_out=(), limit=16 << 20):
    moved = sum(a.size * a.dtype.itemsize for a in inputs)

    def placed(i):
        return IN_HBM if i in hbm else IN_PLACE if i in loose else IN_VMEM

    return pl.pallas_call(
        kernel,
        in_specs=[placed(i) for i in range(len(inputs))],
        out_specs=[IN_HBM if i in hbm_out else IN_VMEM for i in range(len(outs))],
        out_shape=[
            jax.ShapeDtypeStruct(s, d) if i in hbm_out else pltpu.VMEM(s, d)
            for i, (s, d) in enumerate(outs)
        ],
        scratch_shapes=list(scratch),
        compiler_params=pltpu.CompilerParams(vmem_limit_bytes=limit),
        cost_estimate=pl.CostEstimate(flops=flops, bytes_accessed=moved, transcendentals=0),
    )(
        *(
            pltpu.with_memory_space_constraint(a, pltpu.MemorySpace.HBM) if i in hbm else a
            for i, a in enumerate(inputs)
        )
    )


def to_tiles(rows):
    cut = rows.reshape(16, TILES, 8, rows.shape[-1])
    parts = (cut[:, 0], cut[:8, 1:3], cut[8:, 1:3], cut[:, 3])
    return [part.reshape(POINTS, rows.shape[-1]) for part in parts]


def from_tiles(tiles):
    n = tiles[0].shape[-1]
    upper, lower = (t.reshape(8, 2, 8, n) for t in tiles[1:3])
    left, right = (t.reshape(16, 1, 8, n) for t in (tiles[0], tiles[3]))
    middle = jnp.concatenate([upper, lower], axis=0)
    return jnp.concatenate([left, middle, right], axis=1).reshape(TILES * POINTS, n)


def select(count, dst_of_src):
    dst = lax.broadcasted_iota(jnp.int32, (count, count), 0)
    src = lax.broadcasted_iota(jnp.int32, (count, count), 1)
    return jnp.where(dst == dst_of_src(src), 1.0, 0.0).astype(BF)


def to_blocks(rows):
    return lambda i: ((i % 16) // 4) * (4 * rows) + (i // 16) * 4 + i % 4


def is_odd(axis):
    return lax.axis_index(axis) % 2 == 1


def lead_kernel(mesh_ref, a_ref, b_ref, sem):
    odd = lax.axis_index("lat") % 2
    first = pltpu.make_async_copy(mesh_ref.at[pl.ds((1 - odd) * BLOCK, BLOCK)], a_ref, sem.at[0])
    second = pltpu.make_async_copy(mesh_ref.at[pl.ds(odd * BLOCK, BLOCK)], b_ref, sem.at[1])
    first.start()
    second.start()
    first.wait()
    second.wait()


def project_kernel(
    edges_hbm, mask_hbm, x_hbm, wq_hbm, c_hbm, wo_hbm, wk_hbm, wv_hbm,
    q_ref, da_ref, bias_ref, wk_ref, wv_ref,
    edges_scr, mask_scr, x_scr, wq_scr, c_scr, wo_scr, sem,
):
    pairs = (
        (edges_hbm, edges_scr), (mask_hbm, mask_scr), (x_hbm, x_scr), (wq_hbm, wq_scr),
        (c_hbm, c_scr), (wo_hbm, wo_scr), (wk_hbm, wk_ref), (wv_hbm, wv_ref),
    )
    copies = [pltpu.make_async_copy(a, b, sem.at[i]) for i, (a, b) in enumerate(pairs)]
    for copy in copies:
        copy.start()
    copies[0].wait()
    copies[1].wait()
    make_bias(edges_scr, mask_scr, bias_ref)
    for first, out_ref, project in (
        (2, q_ref, lambda lanes: mm(x_scr[...], wq_scr[:, lanes], NN)),
        (4, da_ref, lambda lanes: mm(c_scr[...], wo_scr[lanes, :], NT)),
    ):
        copies[first].wait()
        copies[first + 1].wait()
        for j in range(0, q_ref.shape[-1], 256):
            lanes = slice(j, j + 256)
            for t, rows in enumerate(to_tiles(project(lanes))):
                out_ref[t, :, lanes] = rows.astype(BF) * SCALE
    copies[6].wait()
    copies[7].wait()


def make_bias(edges_ref, mask_ref, bias_ref):
    lat_start = lax.axis_index("lat") * 8
    lon_start = lax.axis_index("lon") * 16
    edges = edges_ref[...]
    row = (edges >> 10) - lat_start + REACH
    col = (edges - lon_start + REACH) & 1023
    point_row = lax.broadcasted_iota(jnp.int32, edges.shape, 1)
    point_col = lax.broadcasted_iota(jnp.int32, edges.shape, 2)
    block, inner = col >> 2, row * 4 + (col & 3)
    slot = jnp.where(
        point_col < 8,
        block * BLOCK + inner,
        jnp.where(
            point_col >= 24,
            jnp.where(block == 5, 0, block - 2) * BLOCK + inner,
            (block - 1) * HALF + inner - jnp.where(point_row < 8, 0, HALO),
        ),
    )
    slot = jnp.where(mask_ref[...] > 0, slot, -1).astype(F32).astype(BF)
    slot = slot.reshape(SLOTS * 16, 32)

    def point(lane):
        tile, i = lane >> 7, lane & 127
        outer = (tile == 0) | (tile == 3)
        row = jnp.where(outer, i >> 3, (i >> 4) + jnp.where(tile == 2, 8, 0))
        col = jnp.where(outer, (i & 7) + tile * 8, (i & 15) + 8)
        return row, col

    src = lax.broadcasted_iota(jnp.int32, (32, TILES * POINTS), 0)
    dst = lax.broadcasted_iota(jnp.int32, (32, TILES * POINTS), 1)
    pick = jnp.where(src == point(dst)[1], 1.0, 0.0).astype(BF)
    wide = mm(slot, pick, NN).reshape(SLOTS, 16, TILES * POINTS)
    lane = lax.broadcasted_iota(jnp.int32, (16, TILES * POINTS), 1)
    own_row = lax.broadcasted_iota(jnp.int32, lane.shape, 0) == point(lane)[0]
    slots = jnp.sum(jnp.where(own_row[None], wide, 0.0), axis=1)
    node = lax.broadcasted_iota(jnp.int32, (NODES, POINTS), 0).astype(F32)
    for t in range(TILES):
        at = slice(t * POINTS, (t + 1) * POINTS)
        hit = node == slots[0:1, at]
        for e in range(1, SLOTS):
            hit = hit | (node == slots[e : e + 1, at])
        bias_ref[t] = jnp.where(hit, 0.0, NEG_FILL)


def sort_pair(axis, a, b):
    odd = lax.axis_index(axis) % 2 == 1
    return jnp.where(odd, a, b), jnp.where(odd, b, a)


def assemble_kernel(got_a, got_b, own_a, own_b, half_ref, rest_ref, send_a, send_b):
    first = is_odd("lat")
    top = jnp.where(first, got_a[...], own_b[...])
    bottom = jnp.where(first, own_b[...], got_a[...])
    rows = jnp.concatenate([top, own_a[...], bottom], axis=0)
    pick_most, pick_few = select(NODES, to_blocks(12)), select(BLOCK, to_blocks(4))
    for j in range(0, rest_ref.shape[-1], WIDE):
        lanes = slice(j, j + WIDE)
        half = mm(pick_most, rows[:, lanes], NN).astype(BF)
        rest = mm(pick_few, got_b[:, lanes], NN).astype(BF)
        half_ref[:, lanes] = half
        rest_ref[:, lanes] = rest

        def column(i):
            most = half[i * HALF : (i + 1) * HALF]
            few = rest[i * HALO : (i + 1) * HALO]
            return jnp.where(
                first, jnp.concatenate([most, few], axis=0), jnp.concatenate([few, most], axis=0)
            )

        send_a[:, lanes], send_b[:, lanes] = sort_pair("lon", column(0), column(3))


def half_masks():
    head = lax.broadcasted_iota(jnp.int32, (1, 2 * HEAD), 1) // HEAD
    return [jnp.where(head == h, 1.0, 0.0).astype(BF) for h in range(2)]


def spread_pair(block):
    return jnp.concatenate([block * m for m in half_masks()], axis=0)


def spread_group(block):
    zero = jnp.zeros((block.shape[0], 2 * HEAD), BF)
    low, high = block[:, : 2 * HEAD], block[:, 2 * HEAD :]
    masks = half_masks()
    rows = [jnp.concatenate([low * m, zero], axis=1) for m in masks]
    rows += [jnp.concatenate([zero, high * m], axis=1) for m in masks]
    return jnp.concatenate(rows, axis=0)


def pair_lanes(i):
    return slice(i * 2 * HEAD, (i + 1) * 2 * HEAD), slice(i * 2 * POINTS, (i + 1) * 2 * POINTS)


def score(keys, values, q4, d4, bufs):
    s_ref, d_ref, qs_ref, gs_ref = bufs[:4]
    for i in range(GROUP // 2):
        lanes, at = pair_lanes(i)
        qs_ref[at, :] = spread_pair(q4[:, lanes])
        gs_ref[at, :] = spread_pair(d4[:, lanes])
        s_ref[:, at] = mm(keys[:, lanes], qs_ref[at, :], NT)
        d_ref[:, at] = mm(values[:, lanes], gs_ref[at, :], NT)


def soften(bias, bufs):
    s_ref, d_ref, _, _, pw, sw, pt, st = bufs
    for h in range(GROUP):
        at = slice(h * POINTS, (h + 1) * POINTS)
        tall = slice(h * NODES, (h + 1) * NODES)
        top = jnp.max(s_ref[:, at] + bias, axis=0, keepdims=True)
        e = jnp.exp(s_ref[:, at] + bias - top)
        s_ref[:, at] = e
        inverse = 1.0 / jnp.sum(e, axis=0, keepdims=True)
        centred = jnp.sum(e * d_ref[:, at], axis=0, keepdims=True) * inverse
        p = s_ref[:, at] * inverse
        half = p.astype(BF)
        ds = (p * (d_ref[:, at] - centred)).astype(BF)
        pw[:, at] = half
        sw[:, at] = ds
        pt[tall, :] = half
        st[tall, :] = ds


def point_side(keys, values, pt, st):
    att = mm(pt[...], spread_group(values), TN).astype(BF)
    return att, mm(st[...], spread_group(keys), TN).astype(BF)


def gather_grads(keys, values, bufs, late):
    _, _, qs_ref, gs_ref, pw, sw, pt, st = bufs
    att, dq = (None, None) if late else point_side(keys, values, pt, st)
    dk, dv = [], []
    for i in range(GROUP // 2):
        _, at = pair_lanes(i)
        dk.append(mm(sw[:, at], qs_ref[at, :], NN))
        dv.append(mm(pw[:, at], gs_ref[at, :], NN))
    return att, dq, jnp.concatenate(dk, axis=1), jnp.concatenate(dv, axis=1)


ITEM_SCRATCH = (
    (pltpu.VMEM((NODES, GROUP * POINTS), F32),) * 2
    + (pltpu.VMEM((GROUP * POINTS, 2 * HEAD), BF),) * 2
    + (pltpu.VMEM((NODES, GROUP * POINTS), BF),) * 2
    + (pltpu.VMEM((GROUP * NODES, POINTS), BF),) * 2
)
PAIR_SCRATCH = ITEM_SCRATCH * 2


def attend(tile, load, store, q_ref, da_ref, bias_ref, scratch, late=None):
    n = len(ITEM_SCRATCH)
    halves = (scratch[:n], scratch[n:])

    def bufs(k):
        half = halves[k % 2]
        return half if late is None else (*half[:-2], late[0].at[k], late[1].at[k])

    items = [slice(j, j + WIDE) for j in range(0, HEADS * HEAD, WIDE)]

    def do_score(k):
        lanes = items[k]
        score(*load(lanes), q_ref[tile, :, lanes], da_ref[tile, :, lanes], bufs(k))

    def do_grads(k):
        store(items[k], *gather_grads(*load(items[k]), bufs(k), late is not None))

    do_score(0)
    for k in range(len(items)):
        if k > 0:
            do_grads(k - 1)
        soften(bias_ref[tile], bufs(k))
        if k + 1 < len(items):
            do_score(k + 1)
    do_grads(len(items) - 1)


def store_all(*refs):
    def store(lanes, *values):
        for ref, value in zip(refs, values):
            ref[:, lanes] = value

    return store


def first_kernel(
    half_ref, wk_ref, wv_ref, q_ref, da_ref, bias_ref,
    k_ref, v_ref, att_ref, dq_ref, dk_ref, dv_ref, wkt_ref, wvt_ref, *scratch,
):
    for j in range(0, half_ref.shape[-1], WIDE):
        lanes = slice(j, j + WIDE)
        k_ref[:, lanes] = mm(half_ref[...], wk_ref[:, lanes], NN).astype(BF)
        v_ref[:, lanes] = mm(half_ref[...], wv_ref[:, lanes], NN).astype(BF)
        for i in range(0, half_ref.shape[-1], WIDE):
            rows = slice(i, i + WIDE)
            wkt_ref[lanes, rows] = wk_ref[rows, lanes].T
            wvt_ref[lanes, rows] = wv_ref[rows, lanes].T

    def load(lanes):
        return k_ref[:, lanes], v_ref[:, lanes]

    tile = jnp.where(is_odd("lat"), 1, 2)
    store = store_all(att_ref, dq_ref, dk_ref, dv_ref)
    attend(tile, load, store, q_ref, da_ref, bias_ref, scratch)


def edge_load(left, k_ref, v_ref, kr, vr):
    start = pl.multiple_of(jnp.where(left, 0, 2 * BLOCK), 2 * BLOCK)

    def load(lanes):
        def one(rim, mid):
            return jnp.concatenate([rim[:, lanes], mid[pl.ds(start, 2 * BLOCK), lanes]], axis=0)

        return one(kr, k_ref), one(vr, v_ref)

    return load


def edge_tile(left, k_ref, v_ref, kr, vr, outs, q_ref, da_ref, bias_ref, scratch, late=None):
    att_ref, dq_ref, dk_ref, dv_ref, dkr, dvr = outs
    load = edge_load(left, k_ref, v_ref, kr, vr)

    def store(lanes, att, dq, dk, dv):
        if late is None:
            att_ref[:, lanes] = att
            dq_ref[:, lanes] = dq
        for grad, rim, out in ((dk, dkr, dk_ref), (dv, dvr, dv_ref)):
            rim[:, lanes] = (grad[:BLOCK] * (1.0 / SCALE)).astype(BF)
            out[:, lanes] = grad[BLOCK:]

    attend(jnp.where(left, 0, 3), load, store, q_ref, da_ref, bias_ref, scratch, late)


def near_kernel(
    got_a, rest_ref, kh_ref, vh_ref, wk_ref, wv_ref, q_ref, da_ref, bias_ref,
    k_ref, v_ref, att_ref, dq_ref, dk_ref, dv_ref, dkr, dvr,
    kr, vr, *scratch,
):
    rows = jnp.concatenate([got_a[...], rest_ref[...]], axis=0)
    first = is_odd("lat")
    for rim, mid, half, w in ((kr, k_ref, kh_ref, wk_ref), (vr, v_ref, vh_ref, wv_ref)):
        for j in range(0, rows.shape[-1], WIDE):
            lanes = slice(j, j + WIDE)
            made = mm(rows, w[:, lanes], NN).astype(BF)
            rim[:, lanes] = made[:BLOCK]
            for i in range(4):
                most = half[i * HALF : (i + 1) * HALF, lanes]
                few = made[BLOCK + i * HALO : BLOCK + (i + 1) * HALO]
                mid[i * BLOCK : (i + 1) * BLOCK, lanes] = jnp.where(
                    first,
                    jnp.concatenate([most, few], axis=0),
                    jnp.concatenate([few, most], axis=0),
                )
    outs = (att_ref, dq_ref, dk_ref, dv_ref, dkr, dvr)
    edge_tile(is_odd("lon"), k_ref, v_ref, kr, vr, outs, q_ref, da_ref, bias_ref, scratch)


def far_kernel(
    got_b, k_ref, v_ref, wk_ref, wv_ref, q_ref, da_ref, bias_ref, near_dkr, near_dvr,
    wkt_ref, wvt_ref,
    pt_ref, st_ref, kr, vr, dk_ref, dv_ref, send_a, send_b,
    dkr, dvr, *scratch,
):
    for j in range(0, kr.shape[-1], WIDE):
        lanes = slice(j, j + WIDE)
        kr[:, lanes] = mm(got_b[...], wk_ref[:, lanes], NN).astype(BF)
        vr[:, lanes] = mm(got_b[...], wv_ref[:, lanes], NN).astype(BF)
    outs = (None, None, dk_ref, dv_ref, dkr, dvr)
    left = lax.axis_index("lon") % 2 == 0
    late = (pt_ref, st_ref)
    edge_tile(left, k_ref, v_ref, kr, vr, outs, q_ref, da_ref, bias_ref, scratch, late)
    dk = jnp.concatenate([near_dkr[...], dkr[...]], axis=0)
    dv = jnp.concatenate([near_dvr[...], dvr[...]], axis=0)
    for j in range(0, kr.shape[-1], WIDE):
        lanes = slice(j, j + WIDE)
        part = mm(dk, wkt_ref[:, lanes], NN) + mm(dv, wvt_ref[:, lanes], NN)
        send_a[:, lanes] = part[:BLOCK].astype(BF)
        send_b[:, lanes] = part[BLOCK:].astype(BF)


def last_kernel(
    k_ref, v_ref, wkt_ref, wvt_ref, q_ref, da_ref, bias_ref,
    dkh_ref, dvh_ref, dkn_ref, dvn_ref, dkf_ref, dvf_ref, pt_ref, st_ref, kr, vr,
    att_ref, dq_ref, att_far, dq_far, part_ref, dko_ref, dvo_ref,
    dkr, dvr, *scratch,
):
    far = edge_load(lax.axis_index("lon") % 2 == 0, k_ref, v_ref, kr, vr)
    for g in range(HEADS // GROUP):
        lanes = slice(g * WIDE, (g + 1) * WIDE)
        att_far[:, lanes], dq_far[:, lanes] = point_side(*far(lanes), pt_ref.at[g], st_ref.at[g])
    upper_done = is_odd("lat")
    offset = jnp.where(upper_done, HALO, 0)

    def load(lanes):
        def one(ref):
            starts = [pl.multiple_of(i * BLOCK + offset, HALO) for i in range(4)]
            return jnp.concatenate([ref[pl.ds(at, HALF), lanes] for at in starts], axis=0)

        return one(k_ref), one(v_ref)

    def store(lanes, att, dq, dk, dv):
        att_ref[:, lanes] = att
        dq_ref[:, lanes] = dq
        for grad, half, near, far, rims, own in (
            (dk, dkh_ref, dkn_ref, dkf_ref, dkr, dko_ref),
            (dv, dvh_ref, dvn_ref, dvf_ref, dvr, dvo_ref),
        ):
            sides = sort_pair("lon", near[:, lanes], far[:, lanes])
            for i in range(4):
                edge = sides[i // 2][(i % 2) * BLOCK : (i % 2 + 1) * BLOCK]
                a = half[i * HALF : (i + 1) * HALF, lanes]
                b = grad[i * HALF : (i + 1) * HALF]
                up = jnp.where(upper_done, a, b)
                down = jnp.where(upper_done, b, a)
                low = edge[:HALO] + up[:HALO]
                mine = edge[HALO:HALF] + up[HALO:] + down[: HALF - HALO]
                high = edge[HALF:] + down[HALF - HALO :]
                low, mine, high = ((x * (1.0 / SCALE)).astype(BF) for x in (low, mine, high))
                rims[i * HALO : (i + 1) * HALO, lanes] = low
                rims[BLOCK + i * HALO : BLOCK + (i + 1) * HALO, lanes] = high
                own[i * 2 * HALO : (i + 1) * 2 * HALO, lanes] = mine

    attend(jnp.where(upper_done, 2, 1), load, store, q_ref, da_ref, bias_ref, scratch)
    for j in range(0, part_ref.shape[-1], WIDE):
        lanes = slice(j, j + WIDE)
        part_ref[:, lanes] = mm(dkr[...], wkt_ref[:, lanes], NN) + mm(dvr[...], wvt_ref[:, lanes], NN)


def merge_kernel(part_ref, got_a, got_b, send_a, send_b):
    left, right = (x.astype(F32) for x in sort_pair("lon", got_a[...], got_b[...]))
    sides = []
    for i, rows in enumerate((slice(0, HALO), slice(HALF, BLOCK))):
        part = part_ref[i * BLOCK : (i + 1) * BLOCK]
        parts = [part[:HALO] + left[rows], part[HALO:HALF], part[HALF:] + right[rows]]
        sides.append(jnp.concatenate(parts, axis=0).astype(BF))
    send_a[...], send_b[...] = sort_pair("lat", *sides)


def emit(res_ref, tiles, w_ref, dims, out_hbm, out_scr, sem):
    first, near, far, last = (ref[...] for ref in tiles)
    rows = jnp.concatenate(
        [*sort_pair("lon", near, far)[:1], *sort_pair("lat", first, last), sort_pair("lon", near, far)[1]],
        axis=0,
    )
    copies = []
    for i, j in enumerate(range(0, out_scr.shape[-1], 256)):
        lanes = slice(j, j + 256)
        w = w_ref[:, lanes] if dims is NN else w_ref[lanes, :]
        product = mm(rows, w, dims)
        tiles = [product[t * POINTS : (t + 1) * POINTS] for t in range(TILES)]
        out_scr[:, lanes] = (res_ref[:, lanes].astype(F32) + from_tiles(tiles)).astype(BF)
        copy = pltpu.make_async_copy(out_scr.at[:, lanes], out_hbm.at[:, lanes], sem.at[i])
        copy.start()
        copies.append(copy)
    return copies


def layer_out_kernel(x_ref, first, near, far, last, wo_ref, out_hbm, out_scr, sem):
    for copy in emit(x_ref, (first, near, far, last), wo_ref, NN, out_hbm, out_scr, sem):
        copy.wait()


def grid_grad_kernel(
    c_ref, first, near, far, last, wq_ref, dk_ref, dv_ref, wkt_ref, wvt_ref, got_a, got_b,
    grad_hbm, own_ref, out_scr, sem,
):
    copies = emit(c_ref, (first, near, far, last), wq_ref, NT, grad_hbm, out_scr, sem)
    left, right = (x.astype(F32)[HALO:HALF] for x in sort_pair("lon", got_a[...], got_b[...]))
    none = jnp.zeros((BLOCK, WIDE), F32)
    for j in range(0, own_ref.shape[-1], WIDE):
        lanes = slice(j, j + WIDE)
        rims = jnp.concatenate([left[:, lanes], none, right[:, lanes]], axis=0)
        own_ref[:, lanes] = (
            mm(dk_ref[...], wkt_ref[:, lanes], NN) + mm(dv_ref[...], wvt_ref[:, lanes], NN) + rims
        )
    for copy in copies:
        copy.wait()


def finish_kernel(own_ref, got_a, got_b, out_hbm, out_scr, sem):
    sides = [x.astype(F32) for x in sort_pair("lat", got_a[...], got_b[...])]
    parts = [side[i * HALO : (i + 1) * HALO] for i in range(4) for side in sides]
    total = (own_ref[...] + jnp.concatenate(parts, axis=0)).astype(BF)
    dst = lax.broadcasted_iota(jnp.int32, (2 * BLOCK, 2 * BLOCK), 0)
    src = lax.broadcasted_iota(jnp.int32, (2 * BLOCK, 2 * BLOCK), 1)
    pick = jnp.where(src == to_blocks(8)(dst), 1.0, 0.0).astype(BF)
    copies = []
    for i, j in enumerate(range(0, out_scr.shape[-1], 256)):
        lanes = slice(j, j + 256)
        out_scr[:, lanes] = mm(pick, total[:, lanes], NN).astype(BF)
        copy = pltpu.make_async_copy(out_scr.at[:, lanes], out_hbm.at[:, lanes], sem.at[i])
        copy.start()
        copies.append(copy)
    for copy in copies:
        copy.wait()


def pairs_of(axis):
    count = lax.axis_size(axis)
    even = [(i, i + 1) for i in range(0, count, 2)]
    odd = [(i, (i + 1) % count) for i in range(1, count, 2)]
    return [pairs + [(b, a) for a, b in pairs] for pairs in (even, odd)]


def local(grid_feat, mesh_feat, edges, edge_mask, w_query, w_key, w_value, w_out, cotangent):
    width = grid_feat.shape[-1]
    points = TILES * POINTS
    x = grid_feat.reshape(points, width)
    c = cotangent.reshape(points, width)
    own = mesh_feat.reshape(2 * BLOCK, width)
    product = 2 * width * width
    lat_a, lat_b = pairs_of("lat")
    lon_a, lon_b = pairs_of("lon")
    piece = ((BLOCK, width), BF)
    tiled = ((TILES, POINTS, width), BF)
    square = ((width, width), BF)

    send_a, send_b = call(
        lead_kernel, (own,), [piece, piece], 10**5,
        (pltpu.SemaphoreType.DMA((2,)),), hbm=(0,),
    )
    got_a = lax.ppermute(send_a, "lat", lat_a)
    got_b = lax.ppermute(send_b, "lat", lat_b)
    q, da, bias, wk, wv = call(
        project_kernel,
        (edges, edge_mask, x, w_query, c, w_out, w_key, w_value),
        [tiled, tiled, ((TILES, NODES, POINTS), F32), square, square],
        2 * points * product,
        (pltpu.VMEM(edges.shape, jnp.int32),) * 2
        + (pltpu.VMEM((points, width), BF), pltpu.VMEM((width, width), BF)) * 2
        + (pltpu.SemaphoreType.DMA((8,)),),
        hbm=tuple(range(8)),
    )
    common = (wk, wv, q, da, bias)
    rows = ((POINTS, width), BF)
    half, half_grad = ((NODES, width), BF), ((NODES, width), F32)
    mid, mid_grad = ((MIDDLE, width), BF), ((2 * BLOCK, width), F32)
    half_rows, rest, edge_a, edge_b = call(
        assemble_kernel, (got_a, got_b, send_a, send_b), [half] + [piece] * 3, 10**8
    )
    edge_a = lax.ppermute(edge_a, "lon", lon_a)
    edge_b = lax.ppermute(edge_b, "lon", lon_b)
    kh, vh, att_first, dq_first, dkh, dvh, wkt, wvt = call(
        first_kernel, (half_rows, *common),
        [half] * 2 + [rows] * 2 + [half_grad] * 2 + [square] * 2,
        4 * 10**9, PAIR_SCRATCH,
    )
    k, v, att_near, dq_near, dkn, dvn, rim_dk, rim_dv = call(
        near_kernel, (edge_a, rest, kh, vh, *common),
        [mid] * 2 + [rows] * 2 + [mid_grad] * 2 + [piece] * 2,
        4 * 10**9, (pltpu.VMEM((BLOCK, width), BF),) * 2 + PAIR_SCRATCH,
    )
    kept = ((HEADS // GROUP, GROUP * NODES, POINTS), BF)
    pt, st, kr, vr, dkf, dvf, edge_a, edge_b = call(
        far_kernel, (edge_b, k, v, *common, rim_dk, rim_dv, wkt, wvt),
        [kept] * 2 + [piece] * 2 + [mid_grad] * 2 + [piece] * 2,
        4 * 10**9, (pltpu.VMEM((BLOCK, width), BF),) * 2 + PAIR_SCRATCH,
    )
    edge_a = lax.ppermute(edge_a, "lon", lon_a)
    edge_b = lax.ppermute(edge_b, "lon", lon_b)
    att_last, dq_last, att_far, dq_far, part, dk_own, dv_own = call(
        last_kernel, (k, v, wkt, wvt, q, da, bias, dkh, dvh, dkn, dvn, dkf, dvf, pt, st, kr, vr),
        [rows] * 4 + [mid_grad] + [((2 * BLOCK, width), BF)] * 2,
        4 * 10**9, (pltpu.VMEM((2 * BLOCK, width), BF),) * 2 + PAIR_SCRATCH,
    )
    send_a, send_b = call(merge_kernel, (part, edge_a, edge_b), [piece, piece], 10**8)
    got_a = lax.ppermute(send_a, "lat", lat_a)
    out_scratch = (pltpu.VMEM((points, width), BF), pltpu.SemaphoreType.DMA((4,)))
    got_b = lax.ppermute(send_b, "lat", lat_b)
    (layer_out,) = call(
        layer_out_kernel, (x, att_first, att_near, att_far, att_last, w_out),
        [((points, width), BF)],
        points * product, out_scratch, hbm_out=(0,),
    )
    grid_grad, kept = call(
        grid_grad_kernel,
        (c, dq_first, dq_near, dq_far, dq_last, w_query, dk_own, dv_own, wkt, wvt, edge_a, edge_b),
        [((points, width), BF), ((2 * BLOCK, width), F32)],
        points * product, out_scratch, hbm_out=(0,),
    )
    (mesh_grad,) = call(
        finish_kernel, (kept, got_a, got_b), [((2 * BLOCK, width), BF)], 10**6,
        (pltpu.VMEM((2 * BLOCK, width), BF), pltpu.SemaphoreType.DMA((4,))), hbm_out=(0,),
    )
    return (
        layer_out.reshape(grid_feat.shape),
        grid_grad.reshape(grid_feat.shape),
        mesh_grad.reshape(mesh_feat.shape),
    )


def solution(mesh):
    tiled = P("lat", "lon", None)
    placed = (tiled, tiled, P(None, "lat", "lon"), P(None, "lat", "lon")) + (P(),) * 4 + (tiled,)
    return jax.shard_map(
        local, mesh=mesh, in_specs=placed, out_specs=(tiled, tiled, tiled), check_vma=False
    )
```
